32 devices in a mesh: groups: 2 (over y), seq: 8 (over z, x), vocab: 2 (over core).
Axes of the slice: x: 2, y: 2, z: 4, core: 2. Of those that a mesh axis runs over, the one named last changes fastest.
Arguments:
- ssm_input: bfloat16 [128, 2560], P(('groups', 'seq'), 'vocab'), parts along dimension 0, may hold values from -6 to 6
- gate_input: bfloat16 [128, 2560], P(('groups', 'seq'), 'vocab'), parts along dimension 0, may hold values from -6 to 6
- b_proj: bfloat16 [128, 128], P(('groups', 'seq')), parts along dimension 0, may hold values from -1.796875 to 1.796875
- readout_matrix: bfloat16 [128, 128], P(('groups', 'seq')), parts along dimension 0, may hold values from -1.796875 to 1.796875
- step_raw: float32 [128, 40], P(('groups', 'seq'), 'vocab'), parts along dimension 0, may hold values from -3 to 7
- step_bias: float32 [40], P('vocab'), may hold values from -1 to 1
- decay_log: float32 [40], P('vocab'), may hold values from -9 to -2
- head_skip_gain: float32 [40], P('vocab'), may hold values from 0.5 to 1.5
- norm_gain: float32 [2560], P('vocab'), may hold values from 0.1 to 1.9
- out_weight: bfloat16 [2560, 2560], P('vocab', 'seq'), may hold values from -0.125 to 0.125
- residual: bfloat16 [128, 2560], P('groups', 'seq'), parts along dimension 0, may hold values from -6 to 6
- final_gain: float32 [2560], replicated, may hold values from 0.1 to 1.9
- head_weight: bfloat16 [2560, 3136], P(None, ('seq', 'vocab')), may hold values from -12.253826 to 12.253826
- mask_table: int32 [96, 3136], P(None, ('seq', 'vocab')), may hold values 0 or 1
- state_ids: int32 [128], P(('groups', 'seq')), parts along dimension 0, may hold values from 0 to 95
- targets: int32 [128], P(('groups', 'seq')), parts along dimension 0, may hold values from 0 to 3135
Outputs:
- token_nll_loss: float32 [128], P(('groups', 'seq', 'vocab')), parts along dimension 0
The draws below stay inside these ranges and needn't reach their ends.
There are 2 independent parts, one for each index of `groups`. The reference program is written for one: setup_inputs(seed, part) draws one part's arguments, and reference() takes and returns one part's arrays. A program takes and returns all parts, laid end to end along the dimension named above; an argument that names none is the same for every part. Nothing has to cross between parts.
All inputs are finite; a program needn't handle non-finite values. No bound on the sum of `mask_table` on one device may be relied on, other than what follows from the above.
Results may differ from the reference program's by a relative error of at most 0.0022.
Values may be sent and summed in bfloat16 or wider, within the bound.
No kernel may reach another device: no remote copies, remote signals or barrier semaphores. Data moves between devices by JAX's collectives and lax.ppermute only.
A program may use at most 192 MiB of HBM per device.

```python
import jax
import jax.numpy as jnp
from jax import lax

D = 2560
HEADDIM = 64
DSTATE = 128
HEADS = 40
STATES = 96
TOK_DEV = 8
INNER = 2560
TEXT_LENGTH = 64
VOCAB = 3136
N_SEQ = 8


def draw_step_raw(key, part):
    first, second, third = jax.random.split(key, 3)
    starting_displacement = jnp.clip(jax.random.normal(first, (TEXT_LENGTH, HEADS), jnp.float32) * 0.5, -2.0, 2.0)
    offset = jax.random.uniform(second, (TEXT_LENGTH // TOK_DEV, 1, HEADS), jnp.float32, -0.7, 0.7)
    starting_displacement = (starting_displacement.reshape(TEXT_LENGTH // TOK_DEV, TOK_DEV, HEADS) + offset).reshape(TEXT_LENGTH, HEADS)
    label_locations = jax.random.randint(third, (4,), 0, TEXT_LENGTH)
    contiguous_span = jnp.zeros((TEXT_LENGTH,), jnp.float32).at[label_locations].set(4.0)
    return starting_displacement + contiguous_span[:, None]


def draw_decay_log(key, part):
    first, second, third = jax.random.split(key, 3)
    slow = jnp.log(jax.random.uniform(first, (HEADS,), jnp.float32, 0.3, 1.5) / TEXT_LENGTH)
    fast = jnp.log(jax.random.uniform(second, (HEADS,), jnp.float32, 0.05, 0.12))
    pick = jax.random.bernoulli(third, 0.5, (HEADS,))
    return jnp.where(pick, fast, slow)


def draw_head_weight(key, part):
    first = jax.random.fold_in(key, 0)
    starting_displacement = jnp.clip(jax.random.normal(first, (D, VOCAB), jnp.float32), -4.0, 4.0) * D ** (-0.5)
    return starting_displacement.astype(jnp.bfloat16)


def plant(entries, rng, smallest, largest):
    longest = entries.shape.index(max(entries.shape))
    spots = []
    for shift in (0, 1):
        where = [jax.random.randint(jax.random.fold_in(rng, axis), (), 0, length) for axis, length in enumerate(entries.shape)]
        where[longest] = (where[longest] + shift) % entries.shape[longest]
        spots.append(tuple(where))
    return entries.at[spots[0]].set(smallest).at[spots[1]].set(largest)


def block_scale(key, dims, pieces, least, high):
    level, own = 1.0, jax.random.fold_in(key, 6)
    for axis_at, shards_of in pieces:
        steps = jnp.exp(jax.random.uniform(jax.random.fold_in(own, axis_at), (shards_of,), jnp.float32, least / len(pieces), high / len(pieces)))
        level = level * jnp.repeat(steps, dims[axis_at] // shards_of).reshape([-1 if axis == axis_at else 1 for axis in range(len(dims))])
    return level


def gaussian(key, dims, spread, reach, cuts=(), held_as=jnp.bfloat16):
    drawn = spread * jax.random.normal(key, dims, jnp.float32)
    if cuts:
        drawn = drawn * block_scale(key, dims, cuts, -0.22, 0.18)
    return jnp.clip(drawn, -reach, reach).astype(held_as)


def setup_inputs(seed: int = 0, part: int = 0) -> dict:
    keys = jax.random.split(jax.random.key(seed), 17)
    part_keys = jax.random.split(jax.random.fold_in(keys[16], part), 17)
    ssm_input = gaussian(part_keys[0], (TEXT_LENGTH, INNER), 1.0, 6.0, ((0, 8), (1, 2)))
    gate_input = gaussian(part_keys[1], (TEXT_LENGTH, INNER), 1.0, 6.0, ((0, 8), (1, 2)))
    b_proj = gaussian(part_keys[2], (TEXT_LENGTH, DSTATE), 0.3, 1.796875, ((0, 8),))
    readout_matrix = gaussian(part_keys[3], (TEXT_LENGTH, DSTATE), 0.3, 1.796875, ((0, 8),))
    step_raw = draw_step_raw(jax.random.fold_in(jax.random.fold_in(keys[16], part), 71), part)
    step_bias = jnp.clip(jax.random.uniform(keys[5], (HEADS,), jnp.float32, -1.0, 1.0) * block_scale(keys[5], (HEADS,), ((0, 2),), -0.4, 0.0), -1.0, 1.0)
    decay_log = draw_decay_log(jax.random.fold_in(keys[16], 71), part)
    head_skip_gain = jnp.clip(0.5 + 1.0 * jax.random.uniform(keys[7], (HEADS,), jnp.float32) ** block_scale(keys[7], (HEADS,), ((0, 2),), -0.2, 0.2), 0.5, 1.5)
    norm_gain = jnp.clip(1.0 + 0.18 * jax.random.normal(keys[8], (INNER,), jnp.float32), 0.1, 1.9)
    out_weight = gaussian(keys[9], (INNER, D), INNER ** -0.5, 0.125, ((0, 2), (1, 8)))
    residual = gaussian(part_keys[10], (TEXT_LENGTH, D), 1.0, 6.0, ((1, 8),))
    final_gain = jnp.clip(1.0 + 0.18 * jax.random.normal(keys[11], (D,), jnp.float32), 0.1, 1.9)
    head_weight = draw_head_weight(jax.random.fold_in(keys[16], 71), part)
    mask_table = plant((jax.random.randint(keys[13], (STATES, VOCAB), 0, 2) < 1).astype(jnp.int32), jax.random.fold_in(keys[13], 1), 0, 1)
    state_ids = plant(jax.random.randint(part_keys[14], (TEXT_LENGTH,), 0, STATES), jax.random.fold_in(part_keys[14], 1), 0, STATES - 1).astype(jnp.int32)
    targets = plant(jax.random.randint(part_keys[15], (TEXT_LENGTH,), 0, VOCAB), jax.random.fold_in(part_keys[15], 1), 0, VOCAB - 1).astype(jnp.int32)
    return {"ssm_input": ssm_input, "gate_input": gate_input, "b_proj": b_proj, "readout_matrix": readout_matrix, "step_raw": step_raw, "step_bias": step_bias, "decay_log": decay_log, "head_skip_gain": head_skip_gain, "norm_gain": norm_gain, "out_weight": out_weight, "residual": residual, "final_gain": final_gain, "head_weight": head_weight, "mask_table": mask_table, "state_ids": state_ids, "targets": targets}


def reference(ssm_input, gate_input, b_proj, readout_matrix, step_raw, step_bias, decay_log, head_skip_gain, norm_gain, out_weight, residual, final_gain, head_weight, mask_table, state_ids, targets):
    step = jax.nn.softplus(step_raw + step_bias)
    decay = jnp.exp(step * -jnp.exp(decay_log))
    values = ssm_input.astype(jnp.float32).reshape(TEXT_LENGTH, HEADS, HEADDIM)
    in_rows = b_proj.astype(jnp.float32)
    out_rows = readout_matrix.astype(jnp.float32)

    def advance(state, inputs):
        factor, size, value, in_row, emitted_line_entries = inputs
        state = factor[:, None, None] * state + (size[:, None] * value)[:, :, None] * in_row[None, None, :]
        result = jnp.einsum('hpn,n->hp', state, emitted_line_entries, precision=lax.Precision.HIGHEST)
        return (state, result)
    start = jnp.zeros((HEADS, HEADDIM, DSTATE), jnp.float32)
    _, outputs = lax.scan(advance, start, (decay, step, values, in_rows, out_rows))
    mixed = outputs + head_skip_gain[None, :, None] * values
    gated = (mixed.reshape(TEXT_LENGTH, INNER) * jax.nn.silu(gate_input.astype(jnp.float32))).astype(jnp.bfloat16)
    gated_f = gated.astype(jnp.float32)
    scale = lax.rsqrt(lax.optimization_barrier(jnp.mean(gated_f * gated_f, axis=-1)) + 1e-05)
    normed = (gated_f * scale[:, None] * norm_gain[None, :]).astype(jnp.bfloat16)
    hidden = (residual.astype(jnp.float32) + jnp.dot(normed, out_weight, preferred_element_type=jnp.float32)).astype(jnp.bfloat16)
    hidden_f = hidden.astype(jnp.float32)
    scale_two = lax.rsqrt(lax.optimization_barrier(jnp.mean(hidden_f * hidden_f, axis=-1)) + 1e-05)
    final = (hidden_f * scale_two[:, None] * final_gain[None, :]).astype(jnp.bfloat16)
    vocab_ids = jnp.arange(VOCAB, dtype=jnp.int32)

    def score(inputs):
        block, states, wanted = inputs
        vocab_logits = jnp.dot(block, head_weight, preferred_element_type=jnp.float32)
        allowed = (mask_table[states] == 1) | (vocab_ids[None, :] == wanted[:, None])
        top = lax.optimization_barrier(jnp.max(jnp.where(allowed, vocab_logits, -1e+30), axis=-1))
        total = lax.optimization_barrier(jnp.sum(jnp.where(allowed, jnp.exp(vocab_logits - top[:, None]), 0.0), axis=-1))
        picked = lax.optimization_barrier(jnp.sum(jnp.where(vocab_ids[None, :] == wanted[:, None], vocab_logits, 0.0), axis=-1))
        return jnp.log(total) + top - picked
    losses = lax.map(score, (final.reshape(N_SEQ, TOK_DEV, D), state_ids.reshape(N_SEQ, TOK_DEV), targets.reshape(N_SEQ, TOK_DEV)))
    return losses.reshape(TEXT_LENGTH)
```

```python
import jax
import jax.numpy as jnp
from jax import lax
from jax.experimental import pallas as pl
from jax.experimental.pallas import tpu as pltpu
from jax.sharding import PartitionSpec as P

F32 = jnp.float32
BF16 = jnp.bfloat16
HIGHEST = lax.Precision.HIGHEST
EPS = 1e-05
LANES = 128
NEG = -1e30
IDS = 64
VMEM = pltpu.VMEM


def dims(shape):
    return (((len(shape) - 1,), (0,)), ((), ()))


def pack_kernel(ssm_ref, gate_ref, b_ref, c_ref, raw_ref, ids_ref, targets_ref, out_ref):
    count, rows, _ = out_ref.shape
    channels = ssm_ref.shape[1]
    state = b_ref.shape[1]
    heads = raw_ref.shape[1]
    raw = raw_ref[...]
    high = raw.astype(BF16)
    rest = raw - high.astype(F32)
    middle = rest.astype(BF16)
    low = (rest - middle.astype(F32)).astype(BF16)
    ids = ids_ref[...].astype(F32)
    targets = targets_ref[...]
    upper = lax.shift_right_logical(targets, 8)
    under = (targets - upper * 256).astype(F32)
    parts = [high.astype(F32), middle.astype(F32), low.astype(F32)]
    parts.append(jnp.zeros((rows, IDS - 3 * heads), F32))
    for part in (ids, upper.astype(F32), under):
        parts.append(jnp.broadcast_to(part, (rows, rows)))
    parts.append(jnp.zeros((rows, LANES - IDS - 3 * rows), F32))
    misc = jnp.concatenate(parts, axis=1).astype(BF16)
    edge = 2 * channels
    for k in range(count):
        out_ref[k, :, 0:channels] = ssm_ref[...]
        out_ref[k, :, channels:edge] = gate_ref[...]
        out_ref[k, :, edge : edge + state] = b_ref[...]
        out_ref[k, :, edge + state : edge + 2 * state] = c_ref[...]
        out_ref[k, :, edge + 2 * state :] = misc


def pack(count, ssm, gate, b, c, raw, ids, targets):
    rows, channels = ssm.shape
    width = 2 * channels + 2 * b.shape[1] + LANES
    return pl.pallas_call(
        pack_kernel,
        out_shape=jax.ShapeDtypeStruct((count, rows, width), BF16),
        name="pack",
    )(ssm, gate, b, c, raw, ids.reshape(1, rows), targets.reshape(1, rows))


def mixer_kernel(
    seq_rows, x_ref, bias_ref, decay_ref, skip_ref, gain_ref, weight_ref, residual_ref,
    mine_ref, theirs_ref, kept_ref, unit_ref,
):
    core = lax.axis_index("vocab")
    rows = x_ref.shape[0]
    heads = bias_ref.shape[1]
    channels = gain_ref.shape[1]
    state = (x_ref.shape[1] - LANES - 2 * channels) // 2
    edge = 2 * channels
    half = rows // 2
    size = channels // heads
    misc = x_ref[:, edge + 2 * state :].astype(F32)
    raw = misc[:, 0:heads] + misc[:, heads : 2 * heads] + misc[:, 2 * heads : 3 * heads]
    step = jax.nn.softplus(raw + bias_ref[...])
    rate = step * -jnp.exp(decay_ref[...])
    r64 = lax.broadcasted_iota(jnp.int32, (rows, rows), 0)
    c64 = lax.broadcasted_iota(jnp.int32, (rows, rows), 1)
    tri = (c64 <= r64).astype(F32)
    log_cum = jnp.dot(tri, rate, precision=HIGHEST, preferred_element_type=F32)
    fill = jnp.zeros((rows, LANES - heads), F32)
    wide_cum = jnp.concatenate([log_cum, fill], axis=1)
    wide_step = jnp.concatenate([step, fill], axis=1)
    cum_rows = jnp.concatenate([wide_cum, wide_cum], axis=0).T
    step_rows = jnp.concatenate([wide_step, wide_step], axis=0).T
    b = x_ref[:, edge : edge + state]
    c = x_ref[:, edge + state : edge + 2 * state]
    twice = jnp.concatenate([b, b], axis=0)
    corr = lax.dot_general(c, twice, (((1,), (1,)), ((), ())), preferred_element_type=F32)
    lane = lax.broadcasted_iota(jnp.int32, (rows, LANES), 1)
    row = lax.broadcasted_iota(jnp.int32, (rows, LANES), 0)
    first = lane < size
    causal = jnp.where(first, lane, lane - size) <= row
    first_row = lax.broadcasted_iota(jnp.int32, (1, LANES), 1) < size

    own = seq_rows // 2
    side = r64 // half
    place = r64 - side * half
    which = jnp.where(side == 0, core, 1 - core)
    source = (place // own) * seq_rows + which * own + place % own
    order = (c64 == source).astype(BF16)

    squares = jnp.zeros((rows, LANES), F32)
    for j in range(heads // 2):
        left, right = 2 * j, 2 * j + 1
        span = slice(j * LANES, (j + 1) * LANES)
        at = jnp.where(first, log_cum[:, left : left + 1], log_cum[:, right : right + 1])
        back = jnp.where(first_row, cum_rows[left : left + 1], cum_rows[right : right + 1])
        sizes = jnp.where(first_row, step_rows[left : left + 1], step_rows[right : right + 1])
        weights = jnp.exp(jnp.where(causal, at - back, NEG)) * (corr * sizes)
        high = weights.astype(BF16)
        low = (weights - high.astype(F32)).astype(BF16)
        v = x_ref[:, span]
        none = jnp.zeros_like(v)
        stacked = jnp.concatenate([jnp.where(first, v, none), jnp.where(first, none, v)], axis=0)
        y = jnp.dot(high, stacked, preferred_element_type=F32)
        y = y + jnp.dot(low, stacked, preferred_element_type=F32)
        skip = jnp.where(first_row, skip_ref[0, left], skip_ref[0, right])
        mixed = y + skip * v.astype(F32)
        gate = x_ref[:, channels + j * LANES : channels + (j + 1) * LANES].astype(F32)
        gated = (mixed * (gate / (1.0 + jnp.exp(-gate)))).astype(BF16)
        moved = jnp.dot(order, gated, preferred_element_type=F32)
        squares = squares + moved * moved
        unit_ref[:, span] = (moved * gain_ref[:, span]).astype(BF16)
    partial = jnp.dot(unit_ref[...], weight_ref[...], preferred_element_type=F32)
    kept_ref[...] = jnp.dot(order[0:half], residual_ref[...], preferred_element_type=F32)

    at_row = row % seq_rows
    info = jnp.zeros((rows, LANES), F32)
    for k in range(3):
        column = jnp.sum(
            jnp.where(lane == IDS + k * seq_rows + at_row, misc, 0.0), axis=1, keepdims=True
        )
        info = jnp.where(lane == k + 1, column, info)
    info = jnp.dot(order, info.astype(BF16), preferred_element_type=F32)
    total = jnp.sum(squares, axis=1, keepdims=True)
    info = jnp.where(lane == 0, total, info)
    width = partial.shape[1]
    start = mine_ref.shape[1] - LANES
    mine_ref[:, 0:width] = partial[0:half]
    mine_ref[:, start:] = info[0:half]
    theirs_ref[:, 0:width] = partial[half:]
    theirs_ref[:, start:] = info[half:]


def mixer(x, seq_rows, bias, decay, skip, gain, weight, residual):
    rows = x.shape[0]
    heads = bias.shape[0]
    channels = gain.shape[0]
    width = weight.shape[1]
    total = (width + LANES - 1) // LANES * LANES + LANES
    half = rows // 2
    sums = jax.ShapeDtypeStruct((half, total), F32)
    whole = pl.BlockSpec(memory_space=VMEM)

    def kernel(*refs):
        mixer_kernel(seq_rows, *refs)

    return pl.pallas_call(
        kernel,
        out_shape=(sums, sums, jax.ShapeDtypeStruct((half, width), F32)),
        in_specs=[whole, whole, whole, pl.BlockSpec(memory_space=pltpu.SMEM), whole, whole, whole],
        scratch_shapes=[VMEM((rows, channels), BF16)],
        name="mixer",
    )(
        x, bias.reshape(1, heads), decay.reshape(1, heads), skip.reshape(1, heads),
        gain.reshape(1, channels), weight, residual,
    )


def hidden_kernel(features, mine_ref, theirs_ref, kept_ref, out_ref):
    count, _, width = out_ref.shape
    start = mine_ref.shape[1] - LANES
    squares = mine_ref[:, start : start + 1] + theirs_ref[:, start : start + 1]
    scale = lax.rsqrt(squares / features + EPS)
    sums = mine_ref[:, 0:width] + theirs_ref[:, 0:width]
    hidden = (kept_ref[...] + sums * scale).astype(BF16)
    for k in range(count):
        out_ref[k] = hidden


def hidden_rows(count, features, mine, theirs, kept):
    def kernel(*refs):
        hidden_kernel(features, *refs)

    return pl.pallas_call(
        kernel,
        out_shape=jax.ShapeDtypeStruct((count,) + kept.shape, BF16),
        name="hidden",
    )(mine, theirs, kept)


def head_kernel(
    h_ref, gain_ref, own_ref, other_ref, own_mask_ref, other_mask_ref, info_ref, out_ref
):
    core = lax.axis_index("vocab")
    block = lax.axis_index("seq") * 2
    count, rows, width = h_ref.shape
    features = count * width
    squares = jnp.zeros((rows, width), F32)
    for k in range(count):
        part = h_ref[k].astype(F32)
        squares = squares + part * part
    scale = lax.rsqrt(jnp.sum(squares, axis=1, keepdims=True) / features + EPS)
    entries = own_ref.shape[1]
    logits = [jnp.zeros((rows, entries), F32), jnp.zeros((rows, entries), F32)]
    for k in range(count):
        final = (h_ref[k].astype(F32) * scale * gain_ref[k : k + 1, :]).astype(BF16)
        span = slice(k * width, (k + 1) * width)
        for i, ref in enumerate((own_ref, other_ref)):
            logits[i] = logits[i] + jnp.dot(final, ref[span, :], preferred_element_type=F32)
    states = own_mask_ref.shape[0]
    start = info_ref.shape[1] - LANES
    ids = info_ref[:, start + 1 : start + 2].astype(jnp.int32)
    upper = info_ref[:, start + 2 : start + 3].astype(jnp.int32)
    target = upper * 256 + info_ref[:, start + 3 : start + 4].astype(jnp.int32)
    pick_row = (lax.broadcasted_iota(jnp.int32, (rows, states), 1) == ids).astype(BF16)
    column = lax.broadcasted_iota(jnp.int32, (rows, entries), 1)
    allowed, wanted = [], []
    for ref, which in ((own_mask_ref, core), (other_mask_ref, 1 - core)):
        table = (ref[...] == 1).astype(F32).astype(BF16)
        chosen = jnp.dot(pick_row, table, preferred_element_type=F32)
        is_target = column + (block + which) * entries == target
        wanted.append(is_target)
        allowed.append((chosen > 0.5) | is_target)
    tops = [
        jnp.max(jnp.where(a, x, NEG), axis=1, keepdims=True) for a, x in zip(allowed, logits)
    ]
    top = jnp.maximum(tops[0], tops[1])
    total = jnp.zeros((rows, 1), F32)
    picked = jnp.zeros((rows, 1), F32)
    for a, w, x in zip(allowed, wanted, logits):
        total = total + jnp.sum(jnp.where(a, jnp.exp(x - top), 0.0), axis=1, keepdims=True)
        picked = picked + jnp.sum(jnp.where(w, x, 0.0), axis=1, keepdims=True)
    lane = lax.broadcasted_iota(jnp.int32, (rows, LANES), 1)
    stats = jnp.where(lane == 0, top, jnp.where(lane == 1, total, picked))
    own = out_ref.shape[1]
    for k in range(count):
        out_ref[k] = stats[k * own : (k + 1) * own]


def head(h, gain, own, other, own_mask, other_mask, info):
    count, rows, width = h.shape
    whole = pl.BlockSpec(memory_space=VMEM)
    return pl.pallas_call(
        head_kernel,
        out_shape=jax.ShapeDtypeStruct((count, rows // count, LANES), F32),
        in_specs=[whole] * 7,
        name="head",
    )(h, gain.reshape(count, width), own, other, own_mask, other_mask, info)


def combine_kernel(stats_ref, out_ref):
    count = stats_ref.shape[0]
    top = stats_ref[0, :, 0:1]
    for k in range(1, count):
        top = jnp.maximum(top, stats_ref[k, :, 0:1])
    total = jnp.zeros_like(top)
    picked = jnp.zeros_like(top)
    for k in range(count):
        total = total + stats_ref[k, :, 1:2] * jnp.exp(stats_ref[k, :, 0:1] - top)
        picked = picked + stats_ref[k, :, 2:3]
    out_ref[...] = jnp.log(total) + top - picked


def combine(stats):
    own = stats.shape[1]
    out = pl.pallas_call(
        combine_kernel, out_shape=jax.ShapeDtypeStruct((own, 1), F32), name="combine"
    )(stats)
    return out.reshape(own)


def wide_pack(count, ssm, gate, b, c, raw, ids, targets):
    rows = ssm.shape[0]
    heads = raw.shape[1]
    high = lax.reduce_precision(raw, 8, 7)
    middle = lax.reduce_precision(raw - high, 8, 7)
    low = raw - high - middle
    parts = [high, middle, low, jnp.zeros((rows, IDS - 3 * heads), F32)]
    parts += [a.astype(F32)[:, None] for a in (ids, targets // 256, targets % 256)]
    parts.append(jnp.zeros((rows, LANES - IDS - 3), F32))
    misc = jnp.concatenate(parts, axis=1).astype(BF16)
    row = jnp.concatenate([ssm, gate, b, c, misc], axis=1)
    return jnp.broadcast_to(row[None], (count,) + row.shape)


def wide_mixer(x, seq_rows, bias, decay, skip, gain, weight, residual):
    rows = x.shape[0]
    heads, channels = bias.shape[0], gain.shape[0]
    state = (x.shape[1] - LANES - 2 * channels) // 2
    edge = 2 * channels
    core = lax.axis_index("vocab")
    misc = x[:, edge + 2 * state :].astype(F32)
    raw = misc[:, 0:heads] + misc[:, heads : 2 * heads] + misc[:, 2 * heads : 3 * heads]
    step = jax.nn.softplus(raw + bias[None, :])
    log_cum = jnp.cumsum(step * -jnp.exp(decay)[None, :], axis=0)
    corr = jnp.dot(
        x[:, edge + state : edge + 2 * state],
        x[:, edge : edge + state].T,
        preferred_element_type=F32,
    )
    values = x[:, 0:channels].astype(F32).reshape(rows, heads, -1).transpose(1, 0, 2)
    causal = jnp.arange(rows)[:, None] >= jnp.arange(rows)[None, :]

    def one(inputs):
        cum, size, v = inputs
        weights = jnp.exp(jnp.where(causal, cum[:, None] - cum[None, :], NEG))
        return jnp.dot(weights * corr * size[None, :], v, precision=HIGHEST)

    y = lax.map(one, (log_cum.T, step.T, values))
    mixed = (y + skip[:, None, None] * values).transpose(1, 0, 2).reshape(rows, channels)
    gated = (mixed * jax.nn.silu(x[:, channels:edge].astype(F32))).astype(BF16)
    wide = gated.astype(F32)
    squares = jnp.sum(wide * wide, axis=1, keepdims=True)
    unit = (wide * gain[None, :]).astype(BF16)
    partial = jnp.dot(unit, weight, preferred_element_type=F32)
    width = weight.shape[1]
    start = (width + LANES - 1) // LANES * LANES
    info = jnp.concatenate([squares, misc[:, IDS : IDS + 3]], axis=1)
    sums = jnp.concatenate(
        [
            partial,
            jnp.zeros((rows, start - width), F32),
            info,
            jnp.zeros((rows, LANES - info.shape[1]), F32),
        ],
        axis=1,
    )

    def side(a, which):
        split = a.reshape(rows // seq_rows, 2, seq_rows // 2, -1)
        return lax.dynamic_index_in_dim(split, which, 1, False).reshape(rows // 2, -1)

    return side(sums, core), side(sums, 1 - core), side(residual.astype(F32), core)


def shards(
    ssm_input,
    gate_input,
    b_proj,
    readout_matrix,
    step_raw,
    step_bias,
    decay_log,
    head_skip_gain,
    norm_gain,
    out_weight,
    residual,
    final_gain,
    head_weight,
    mask_table,
    state_ids,
    targets,
):
    count = lax.axis_size("seq")
    rows, channels = ssm_input.shape
    features = 2 * channels
    small = count * rows <= LANES // 2
    swap = [(0, 1), (1, 0)]
    other_weight = lax.ppermute(head_weight, "vocab", swap)
    other_mask = lax.ppermute(mask_table, "vocab", swap)
    packed = (pack if small else wide_pack)(
        count, ssm_input, gate_input, b_proj, readout_matrix, step_raw, state_ids, targets
    )
    gathered = lax.all_to_all(packed, "seq", 0, 0, tiled=True)
    x = gathered.reshape(count * rows, packed.shape[2])
    mine, theirs, kept = (mixer if small else wide_mixer)(
        x, rows, step_bias, decay_log, head_skip_gain, norm_gain, out_weight, residual
    )
    arrived = lax.ppermute(theirs, "vocab", swap)
    if small:
        spread = hidden_rows(count, features, mine, arrived, kept)
    else:
        width = kept.shape[1]
        start = mine.shape[1] - LANES
        sums = mine + arrived
        scale = lax.rsqrt(sums[:, start : start + 1] / features + EPS)
        hidden = (kept + sums[:, 0:width] * scale).astype(BF16)
        spread = jnp.broadcast_to(hidden[None], (count,) + hidden.shape)
    full = lax.all_to_all(spread, "seq", 0, 0, tiled=True)
    if small:
        stats = head(full, final_gain, head_weight, other_weight, mask_table, other_mask, mine)
    else:
        stats = wide_head(
            full, final_gain, head_weight, other_weight, mask_table, other_mask, mine
        )
    placed = lax.all_to_all(stats, "seq", 0, 0, tiled=True)
    return combine(placed) if small else wide_combine(placed)


def wide_head(full, gain, own, other, own_mask, other_mask, info):
    count, rows, width = full.shape
    core = lax.axis_index("vocab")
    block = lax.axis_index("seq") * 2
    wide = full.transpose(1, 0, 2).reshape(rows, count * width).astype(F32)
    scale = lax.rsqrt(jnp.mean(wide * wide, axis=1, keepdims=True) + EPS)
    final = (wide * scale * gain[None, :]).astype(BF16)
    start = info.shape[1] - LANES
    ids, upper, under = (info[:, start + k].astype(jnp.int32) for k in (1, 2, 3))
    target = upper * 256 + under
    entries = own.shape[1]
    logits, allowed, wanted = [], [], []
    for weight, table, which in ((own, own_mask, core), (other, other_mask, 1 - core)):
        logits.append(jnp.dot(final, weight, preferred_element_type=F32))
        column = (block + which) * entries + jnp.arange(entries, dtype=jnp.int32)
        wanted.append(column[None, :] == target[:, None])
        one_hot = (ids[:, None] == jnp.arange(table.shape[0])[None, :]).astype(BF16)
        chosen = jnp.dot(one_hot, (table == 1).astype(BF16), preferred_element_type=F32)
        allowed.append((chosen > 0.5) | wanted[-1])
    x, a, w = (jnp.concatenate(p, axis=1) for p in (logits, allowed, wanted))
    top = jnp.max(jnp.where(a, x, NEG), axis=1)
    total = jnp.sum(jnp.where(a, jnp.exp(x - top[:, None]), 0.0), axis=1)
    picked = jnp.sum(jnp.where(w, x, 0.0), axis=1)
    return jnp.stack([top, total, picked], axis=1).reshape(count, rows // count, 3)


def wide_combine(stats):
    top = jnp.max(stats[:, :, 0], axis=0)
    total = jnp.sum(stats[:, :, 1] * jnp.exp(stats[:, :, 0] - top[None, :]), axis=0)
    return jnp.log(total) + top - jnp.sum(stats[:, :, 2], axis=0)


def solution(mesh):
    placed = (
        P(("groups", "seq"), "vocab"),
        P(("groups", "seq"), "vocab"),
        P(("groups", "seq"), None),
        P(("groups", "seq"), None),
        P(("groups", "seq"), "vocab"),
        P("vocab"),
        P("vocab"),
        P("vocab"),
        P("vocab"),
        P("vocab", "seq"),
        P("groups", "seq"),
        P(),
        P(None, ("seq", "vocab")),
        P(None, ("seq", "vocab")),
        P(("groups", "seq")),
        P(("groups", "seq")),
    )
    return jax.shard_map(
        shards, mesh=mesh, in_specs=placed, out_specs=P(("groups", "seq", "vocab")), check_vma=False
    )
```

```python
import jax
import jax.numpy as jnp
from jax import lax
from jax.experimental import pallas as pl
from jax.experimental.pallas import tpu as pltpu
from jax.sharding import PartitionSpec as P

F32 = jnp.float32
BF16 = jnp.bfloat16
HIGHEST = lax.Precision.HIGHEST
EPS = 1e-05
LANES = 128
NEG = -1e30
IDS = 64
VMEM = pltpu.VMEM


def grant(mebibytes):
    return pltpu.CompilerParams(vmem_limit_bytes=mebibytes << 20)


def dims(shape):
    return (((len(shape) - 1,), (0,)), ((), ()))


def pack_kernel(ssm_ref, gate_ref, b_ref, c_ref, raw_ref, ids_ref, targets_ref, out_ref):
    count, rows, _ = out_ref.shape
    channels = ssm_ref.shape[1]
    state = b_ref.shape[1]
    heads = raw_ref.shape[1]
    raw = raw_ref[...]
    high = raw.astype(BF16)
    rest = raw - high.astype(F32)
    middle = rest.astype(BF16)
    low = (rest - middle.astype(F32)).astype(BF16)
    ids = ids_ref[...].astype(F32)
    targets = targets_ref[...]
    upper = lax.shift_right_logical(targets, 8)
    under = (targets - upper * 256).astype(F32)
    parts = [high.astype(F32), middle.astype(F32), low.astype(F32)]
    parts.append(jnp.zeros((rows, IDS - 3 * heads), F32))
    for part in (ids, upper.astype(F32), under):
        parts.append(jnp.broadcast_to(part, (rows, rows)))
    parts.append(jnp.zeros((rows, LANES - IDS - 3 * rows), F32))
    misc = jnp.concatenate(parts, axis=1).astype(BF16)
    edge = 2 * channels
    for k in range(count):
        out_ref[k, :, 0:channels] = ssm_ref[...]
        out_ref[k, :, channels:edge] = gate_ref[...]
        out_ref[k, :, edge : edge + state] = b_ref[...]
        out_ref[k, :, edge + state : edge + 2 * state] = c_ref[...]
        out_ref[k, :, edge + 2 * state :] = misc


def pack(count, ssm, gate, b, c, raw, ids, targets):
    rows, channels = ssm.shape
    width = 2 * channels + 2 * b.shape[1] + LANES
    return pl.pallas_call(
        pack_kernel,
        out_shape=jax.ShapeDtypeStruct((count, rows, width), BF16),
        name="pack",
    )(ssm, gate, b, c, raw, ids.reshape(1, rows), targets.reshape(1, rows))


def mixer_kernel(
    seq_rows, x_ref, bias_ref, decay_ref, skip_ref, gain_ref, weight_ref, residual_ref,
    mine_ref, theirs_ref, kept_ref, unit_ref,
):
    core = lax.axis_index("vocab")
    rows = x_ref.shape[0]
    heads = bias_ref.shape[1]
    channels = gain_ref.shape[1]
    state = (x_ref.shape[1] - LANES - 2 * channels) // 2
    edge = 2 * channels
    half = rows // 2
    size = channels // heads
    misc = x_ref[:, edge + 2 * state :].astype(F32)
    raw = misc[:, 0:heads] + misc[:, heads : 2 * heads] + misc[:, 2 * heads : 3 * heads]
    step = jax.nn.softplus(raw + bias_ref[...])
    rate = step * -jnp.exp(decay_ref[...])
    r64 = lax.broadcasted_iota(jnp.int32, (rows, rows), 0)
    c64 = lax.broadcasted_iota(jnp.int32, (rows, rows), 1)
    tri = (c64 <= r64).astype(F32)
    log_cum = jnp.dot(tri, rate, precision=HIGHEST, preferred_element_type=F32)
    fill = jnp.zeros((rows, LANES - heads), F32)
    wide_cum = jnp.concatenate([log_cum, fill], axis=1)
    wide_step = jnp.concatenate([step, fill], axis=1)
    cum_rows = jnp.concatenate([wide_cum, wide_cum], axis=0).T
    step_rows = jnp.concatenate([wide_step, wide_step], axis=0).T
    b = x_ref[:, edge : edge + state]
    c = x_ref[:, edge + state : edge + 2 * state]
    twice = jnp.concatenate([b, b], axis=0)
    corr = lax.dot_general(c, twice, (((1,), (1,)), ((), ())), preferred_element_type=F32)
    lane = lax.broadcasted_iota(jnp.int32, (rows, LANES), 1)
    row = lax.broadcasted_iota(jnp.int32, (rows, LANES), 0)
    first = lane < size
    causal = jnp.where(first, lane, lane - size) <= row
    first_row = lax.broadcasted_iota(jnp.int32, (1, LANES), 1) < size

    own = seq_rows // 2
    side = r64 // half
    place = r64 - side * half
    which = jnp.where(side == 0, core, 1 - core)
    source = (place // own) * seq_rows + which * own + place % own
    order = (c64 == source).astype(BF16)

    squares = jnp.zeros((rows, LANES), F32)
    for j in range(heads // 2):
        left, right = 2 * j, 2 * j + 1
        span = slice(j * LANES, (j + 1) * LANES)
        at = jnp.where(first, log_cum[:, left : left + 1], log_cum[:, right : right + 1])
        back = jnp.where(first_row, cum_rows[left : left + 1], cum_rows[right : right + 1])
        sizes = jnp.where(first_row, step_rows[left : left + 1], step_rows[right : right + 1])
        weights = jnp.exp(jnp.where(causal, at - back, NEG)) * (corr * sizes)
        high = weights.astype(BF16)
        low = (weights - high.astype(F32)).astype(BF16)
        v = x_ref[:, span]
        none = jnp.zeros_like(v)
        stacked = jnp.concatenate([jnp.where(first, v, none), jnp.where(first, none, v)], axis=0)
        y = jnp.dot(high, stacked, preferred_element_type=F32)
        y = y + jnp.dot(low, stacked, preferred_element_type=F32)
        skip = jnp.where(first_row, skip_ref[0, left], skip_ref[0, right])
        mixed = y + skip * v.astype(F32)
        gate = x_ref[:, channels + j * LANES : channels + (j + 1) * LANES].astype(F32)
        gated = (mixed * (gate / (1.0 + jnp.exp(-gate)))).astype(BF16)
        moved = jnp.dot(order, gated, preferred_element_type=F32)
        squares = squares + moved * moved
        unit_ref[:, span] = (moved * gain_ref[:, span]).astype(BF16)
    partial = jnp.dot(unit_ref[...], weight_ref[...], preferred_element_type=F32)
    kept_ref[...] = jnp.dot(order[0:half], residual_ref[...], preferred_element_type=F32)

    at_row = row % seq_rows
    info = jnp.zeros((rows, LANES), F32)
    for k in range(3):
        column = jnp.sum(
            jnp.where(lane == IDS + k * seq_rows + at_row, misc, 0.0), axis=1, keepdims=True
        )
        info = jnp.where(lane == k + 1, column, info)
    info = jnp.dot(order, info.astype(BF16), preferred_element_type=F32)
    total = jnp.sum(squares, axis=1, keepdims=True)
    info = jnp.where(lane == 0, total, info)
    width = partial.shape[1]
    start = mine_ref.shape[1] - LANES
    mine_ref[:, 0:width] = partial[0:half]
    mine_ref[:, start:] = info[0:half]
    theirs_ref[:, 0:width] = partial[half:]
    theirs_ref[:, start:] = info[half:]


def mixer(x, seq_rows, bias, decay, skip, gain, weight, residual):
    rows = x.shape[0]
    heads = bias.shape[0]
    channels = gain.shape[0]
    width = weight.shape[1]
    total = (width + LANES - 1) // LANES * LANES + LANES
    half = rows // 2
    sums = jax.ShapeDtypeStruct((half, total), F32)
    whole = pl.BlockSpec(memory_space=VMEM)

    def kernel(*refs):
        mixer_kernel(seq_rows, *refs)

    return pl.pallas_call(
        kernel,
        out_shape=(sums, sums, jax.ShapeDtypeStruct((half, width), F32)),
        in_specs=[whole, whole, whole, pl.BlockSpec(memory_space=pltpu.SMEM), whole, whole, whole],
        scratch_shapes=[VMEM((rows, channels), BF16)],
        compiler_params=grant(8),
        name="mixer",
    )(
        x, bias.reshape(1, heads), decay.reshape(1, heads), skip.reshape(1, heads),
        gain.reshape(1, channels), weight, residual,
    )


def hidden_kernel(features, mine_ref, theirs_ref, kept_ref, out_ref):
    count, _, width = out_ref.shape
    start = mine_ref.shape[1] - LANES
    squares = mine_ref[:, start : start + 1] + theirs_ref[:, start : start + 1]
    scale = lax.rsqrt(squares / features + EPS)
    sums = mine_ref[:, 0:width] + theirs_ref[:, 0:width]
    hidden = (kept_ref[...] + sums * scale).astype(BF16)
    for k in range(count):
        out_ref[k] = hidden


def hidden_rows(count, features, mine, theirs, kept):
    def kernel(*refs):
        hidden_kernel(features, *refs)

    return pl.pallas_call(
        kernel,
        out_shape=jax.ShapeDtypeStruct((count,) + kept.shape, BF16),
        compiler_params=grant(4),
        name="hidden",
    )(mine, theirs, kept)


def head_kernel(
    h_ref, gain_ref, own_ref, other_ref, own_mask_ref, other_mask_ref, info_ref, out_ref
):
    core = lax.axis_index("vocab")
    block = lax.axis_index("seq") * 2
    count, rows, width = h_ref.shape
    features = count * width
    squares = jnp.zeros((rows, width), F32)
    for k in range(count):
        part = h_ref[k].astype(F32)
        squares = squares + part * part
    scale = lax.rsqrt(jnp.sum(squares, axis=1, keepdims=True) / features + EPS)
    entries = own_ref.shape[1]
    logits = [jnp.zeros((rows, entries), F32), jnp.zeros((rows, entries), F32)]
    for k in range(count):
        final = (h_ref[k].astype(F32) * scale * gain_ref[k : k + 1, :]).astype(BF16)
        span = slice(k * width, (k + 1) * width)
        for i, ref in enumerate((own_ref, other_ref)):
            logits[i] = logits[i] + jnp.dot(final, ref[span, :], preferred_element_type=F32)
    states = own_mask_ref.shape[0]
    start = info_ref.shape[1] - LANES
    ids = info_ref[:, start + 1 : start + 2].astype(jnp.int32)
    upper = info_ref[:, start + 2 : start + 3].astype(jnp.int32)
    target = upper * 256 + info_ref[:, start + 3 : start + 4].astype(jnp.int32)
    pick_row = (lax.broadcasted_iota(jnp.int32, (rows, states), 1) == ids).astype(BF16)
    column = lax.broadcasted_iota(jnp.int32, (rows, entries), 1)
    allowed, wanted = [], []
    for ref, which in ((own_mask_ref, core), (other_mask_ref, 1 - core)):
        table = (ref[...] == 1).astype(F32).astype(BF16)
        chosen = jnp.dot(pick_row, table, preferred_element_type=F32)
        is_target = column + (block + which) * entries == target
        wanted.append(is_target)
        allowed.append((chosen > 0.5) | is_target)
    tops = [
        jnp.max(jnp.where(a, x, NEG), axis=1, keepdims=True) for a, x in zip(allowed, logits)
    ]
    top = jnp.maximum(tops[0], tops[1])
    total = jnp.zeros((rows, 1), F32)
    picked = jnp.zeros((rows, 1), F32)
    for a, w, x in zip(allowed, wanted, logits):
        total = total + jnp.sum(jnp.where(a, jnp.exp(x - top), 0.0), axis=1, keepdims=True)
        picked = picked + jnp.sum(jnp.where(w, x, 0.0), axis=1, keepdims=True)
    lane = lax.broadcasted_iota(jnp.int32, (rows, LANES), 1)
    stats = jnp.where(lane == 0, top, jnp.where(lane == 1, total, picked))
    own = out_ref.shape[1]
    for k in range(count):
        out_ref[k] = stats[k * own : (k + 1) * own]


def head(h, gain, own, other, own_mask, other_mask, info):
    count, rows, width = h.shape
    whole = pl.BlockSpec(memory_space=VMEM)
    return pl.pallas_call(
        head_kernel,
        out_shape=jax.ShapeDtypeStruct((count, rows // count, LANES), F32),
        in_specs=[whole] * 7,
        compiler_params=grant(12),
        name="head",
    )(h, gain.reshape(count, width), own, other, own_mask, other_mask, info)


def combine_kernel(stats_ref, out_ref):
    count = stats_ref.shape[0]
    top = stats_ref[0, :, 0:1]
    for k in range(1, count):
        top = jnp.maximum(top, stats_ref[k, :, 0:1])
    total = jnp.zeros_like(top)
    picked = jnp.zeros_like(top)
    for k in range(count):
        total = total + stats_ref[k, :, 1:2] * jnp.exp(stats_ref[k, :, 0:1] - top)
        picked = picked + stats_ref[k, :, 2:3]
    losses = jnp.broadcast_to(jnp.log(total) + top - picked, (top.shape[0], LANES))
    row = lax.broadcasted_iota(jnp.int32, losses.shape, 0)
    lane = lax.broadcasted_iota(jnp.int32, losses.shape, 1)
    flat = jnp.sum(jnp.where(row == lane, losses, 0.0), axis=0, keepdims=True)
    out_ref[...] = flat[:, 0 : out_ref.shape[1]]


def combine(stats):
    own = stats.shape[1]
    out = pl.pallas_call(
        combine_kernel,
        out_shape=jax.ShapeDtypeStruct((1, own), F32),
        compiler_params=grant(2),
        name="combine",
    )(stats)
    return out.reshape(own)


def wide_pack(count, ssm, gate, b, c, raw, ids, targets):
    rows = ssm.shape[0]
    heads = raw.shape[1]
    high = lax.reduce_precision(raw, 8, 7)
    middle = lax.reduce_precision(raw - high, 8, 7)
    low = raw - high - middle
    parts = [high, middle, low, jnp.zeros((rows, IDS - 3 * heads), F32)]
    parts += [a.astype(F32)[:, None] for a in (ids, targets // 256, targets % 256)]
    parts.append(jnp.zeros((rows, LANES - IDS - 3), F32))
    misc = jnp.concatenate(parts, axis=1).astype(BF16)
    row = jnp.concatenate([ssm, gate, b, c, misc], axis=1)
    return jnp.broadcast_to(row[None], (count,) + row.shape)


def wide_mixer(x, seq_rows, bias, decay, skip, gain, weight, residual):
    rows = x.shape[0]
    heads, channels = bias.shape[0], gain.shape[0]
    state = (x.shape[1] - LANES - 2 * channels) // 2
    edge = 2 * channels
    core = lax.axis_index("vocab")
    misc = x[:, edge + 2 * state :].astype(F32)
    raw = misc[:, 0:heads] + misc[:, heads : 2 * heads] + misc[:, 2 * heads : 3 * heads]
    step = jax.nn.softplus(raw + bias[None, :])
    log_cum = jnp.cumsum(step * -jnp.exp(decay)[None, :], axis=0)
    corr = jnp.dot(
        x[:, edge + state : edge + 2 * state],
        x[:, edge : edge + state].T,
        preferred_element_type=F32,
    )
    values = x[:, 0:channels].astype(F32).reshape(rows, heads, -1).transpose(1, 0, 2)
    causal = jnp.arange(rows)[:, None] >= jnp.arange(rows)[None, :]

    def one(inputs):
        cum, size, v = inputs
        weights = jnp.exp(jnp.where(causal, cum[:, None] - cum[None, :], NEG))
        return jnp.dot(weights * corr * size[None, :], v, precision=HIGHEST)

    y = lax.map(one, (log_cum.T, step.T, values))
    mixed = (y + skip[:, None, None] * values).transpose(1, 0, 2).reshape(rows, channels)
    gated = (mixed * jax.nn.silu(x[:, channels:edge].astype(F32))).astype(BF16)
    wide = gated.astype(F32)
    squares = jnp.sum(wide * wide, axis=1, keepdims=True)
    unit = (wide * gain[None, :]).astype(BF16)
    partial = jnp.dot(unit, weight, preferred_element_type=F32)
    width = weight.shape[1]
    start = (width + LANES - 1) // LANES * LANES
    info = jnp.concatenate([squares, misc[:, IDS : IDS + 3]], axis=1)
    sums = jnp.concatenate(
        [
            partial,
            jnp.zeros((rows, start - width), F32),
            info,
            jnp.zeros((rows, LANES - info.shape[1]), F32),
        ],
        axis=1,
    )

    def side(a, which):
        split = a.reshape(rows // seq_rows, 2, seq_rows // 2, -1)
        return lax.dynamic_index_in_dim(split, which, 1, False).reshape(rows // 2, -1)

    return side(sums, core), side(sums, 1 - core), side(residual.astype(F32), core)


def shards(
    ssm_input,
    gate_input,
    b_proj,
    readout_matrix,
    step_raw,
    step_bias,
    decay_log,
    head_skip_gain,
    norm_gain,
    out_weight,
    residual,
    final_gain,
    head_weight,
    mask_table,
    state_ids,
    targets,
):
    count = lax.axis_size("seq")
    rows, channels = ssm_input.shape
    features = 2 * channels
    small = count * rows <= LANES // 2
    swap = [(0, 1), (1, 0)]
    other_weight = lax.ppermute(head_weight, "vocab", swap)
    other_mask = lax.ppermute(mask_table, "vocab", swap)
    packed = (pack if small else wide_pack)(
        count, ssm_input, gate_input, b_proj, readout_matrix, step_raw, state_ids, targets
    )
    gathered = lax.all_to_all(packed, "seq", 0, 0, tiled=True)
    x = gathered.reshape(count * rows, packed.shape[2])
    mine, theirs, kept = (mixer if small else wide_mixer)(
        x, rows, step_bias, decay_log, head_skip_gain, norm_gain, out_weight, residual
    )
    arrived = lax.ppermute(theirs, "vocab", swap)
    if small:
        spread = hidden_rows(count, features, mine, arrived, kept)
    else:
        width = kept.shape[1]
        start = mine.shape[1] - LANES
        sums = mine + arrived
        scale = lax.rsqrt(sums[:, start : start + 1] / features + EPS)
        hidden = (kept + sums[:, 0:width] * scale).astype(BF16)
        spread = jnp.broadcast_to(hidden[None], (count,) + hidden.shape)
    full = lax.all_to_all(spread, "seq", 0, 0, tiled=True)
    if small:
        stats = head(full, final_gain, head_weight, other_weight, mask_table, other_mask, mine)
    else:
        stats = wide_head(
            full, final_gain, head_weight, other_weight, mask_table, other_mask, mine
        )
    placed = lax.all_to_all(stats, "seq", 0, 0, tiled=True)
    return combine(placed) if small else wide_combine(placed)


def wide_head(full, gain, own, other, own_mask, other_mask, info):
    count, rows, width = full.shape
    core = lax.axis_index("vocab")
    block = lax.axis_index("seq") * 2
    wide = full.transpose(1, 0, 2).reshape(rows, count * width).astype(F32)
    scale = lax.rsqrt(jnp.mean(wide * wide, axis=1, keepdims=True) + EPS)
    final = (wide * scale * gain[None, :]).astype(BF16)
    start = info.shape[1] - LANES
    ids, upper, under = (info[:, start + k].astype(jnp.int32) for k in (1, 2, 3))
    target = upper * 256 + under
    entries = own.shape[1]
    logits, allowed, wanted = [], [], []
    for weight, table, which in ((own, own_mask, core), (other, other_mask, 1 - core)):
        logits.append(jnp.dot(final, weight, preferred_element_type=F32))
        column = (block + which) * entries + jnp.arange(entries, dtype=jnp.int32)
        wanted.append(column[None, :] == target[:, None])
        one_hot = (ids[:, None] == jnp.arange(table.shape[0])[None, :]).astype(BF16)
        chosen = jnp.dot(one_hot, (table == 1).astype(BF16), preferred_element_type=F32)
        allowed.append((chosen > 0.5) | wanted[-1])
    x, a, w = (jnp.concatenate(p, axis=1) for p in (logits, allowed, wanted))
    top = jnp.max(jnp.where(a, x, NEG), axis=1)
    total = jnp.sum(jnp.where(a, jnp.exp(x - top[:, None]), 0.0), axis=1)
    picked = jnp.sum(jnp.where(w, x, 0.0), axis=1)
    return jnp.stack([top, total, picked], axis=1).reshape(count, rows // count, 3)


def wide_combine(stats):
    top = jnp.max(stats[:, :, 0], axis=0)
    total = jnp.sum(stats[:, :, 1] * jnp.exp(stats[:, :, 0] - top[None, :]), axis=0)
    return jnp.log(total) + top - jnp.sum(stats[:, :, 2], axis=0)


def solution(mesh):
    placed = (
        P(("groups", "seq"), "vocab"),
        P(("groups", "seq"), "vocab"),
        P(("groups", "seq"), None),
        P(("groups", "seq"), None),
        P(("groups", "seq"), "vocab"),
        P("vocab"),
        P("vocab"),
        P("vocab"),
        P("vocab"),
        P("vocab", "seq"),
        P("groups", "seq"),
        P(),
        P(None, ("seq", "vocab")),
        P(None, ("seq", "vocab")),
        P(("groups", "seq")),
        P(("groups", "seq")),
    )
    return jax.shard_map(
        shards, mesh=mesh, in_specs=placed, out_specs=P(("groups", "seq", "vocab")), check_vma=False
    )
```

```python
import jax
import jax.numpy as jnp
from jax import lax
from jax.experimental import pallas as pl
from jax.experimental.pallas import tpu as pltpu
from jax.sharding import PartitionSpec as P

F32 = jnp.float32
BF16 = jnp.bfloat16
HIGHEST = lax.Precision.HIGHEST
EPS = 1e-05
LANES = 128
NEG = -1e30
IDS = 64
VMEM = pltpu.VMEM


def grant(mebibytes):
    return pltpu.CompilerParams(vmem_limit_bytes=mebibytes << 20)


def turn(seq):
    return (seq // 2) % 2


def circles(count):
    return [[2 * s + (w + turn(s)) % 2 for s in range(count)] for w in range(2)]


def pack_kernel(ssm_ref, gate_ref, b_ref, c_ref, raw_ref, ids_ref, targets_ref, out_ref):
    count, rows, _ = out_ref.shape
    channels = ssm_ref.shape[1]
    state = b_ref.shape[1]
    heads = raw_ref.shape[1]
    raw = raw_ref[...]
    high = raw.astype(BF16)
    rest = raw - high.astype(F32)
    middle = rest.astype(BF16)
    low = (rest - middle.astype(F32)).astype(BF16)
    ids = ids_ref[...].astype(F32)
    targets = targets_ref[...]
    upper = lax.shift_right_logical(targets, 8)
    under = (targets - upper * 256).astype(F32)
    parts = [high.astype(F32), middle.astype(F32), low.astype(F32)]
    parts.append(jnp.zeros((rows, IDS - 3 * heads), F32))
    for part in (ids, upper.astype(F32), under):
        parts.append(jnp.broadcast_to(part, (rows, rows)))
    parts.append(jnp.zeros((rows, LANES - IDS - 3 * rows), F32))
    misc = jnp.concatenate(parts, axis=1).astype(BF16)
    edge = 2 * channels
    for k in range(count):
        out_ref[k, :, 0:channels] = ssm_ref[...]
        out_ref[k, :, channels:edge] = gate_ref[...]
        out_ref[k, :, edge : edge + state] = b_ref[...]
        out_ref[k, :, edge + state : edge + 2 * state] = c_ref[...]
        out_ref[k, :, edge + 2 * state :] = misc


def pack(count, ssm, gate, b, c, raw, ids, targets):
    rows, channels = ssm.shape
    width = 2 * channels + 2 * b.shape[1] + LANES
    return pl.pallas_call(
        pack_kernel,
        out_shape=jax.ShapeDtypeStruct((count, rows, width), BF16),
        name="pack",
    )(ssm, gate, b, c, raw, ids.reshape(1, rows), targets.reshape(1, rows))


def mixer_kernel(
    seq_rows, x_ref, bias_ref, decay_ref, skip_ref, gain_ref, weight_ref, residual_ref,
    mine_ref, theirs_ref, kept_ref, unit_ref,
):
    mine = lax.axis_index("vocab") + turn(lax.axis_index("seq"))
    rows = x_ref.shape[0]
    heads = bias_ref.shape[1]
    channels = gain_ref.shape[1]
    state = (x_ref.shape[1] - LANES - 2 * channels) // 2
    edge = 2 * channels
    half = rows // 2
    size = channels // heads
    misc = x_ref[:, edge + 2 * state :].astype(F32)
    raw = misc[:, 0:heads] + misc[:, heads : 2 * heads] + misc[:, 2 * heads : 3 * heads]
    step = jax.nn.softplus(raw + bias_ref[...])
    rate = step * -jnp.exp(decay_ref[...])
    r64 = lax.broadcasted_iota(jnp.int32, (rows, rows), 0)
    c64 = lax.broadcasted_iota(jnp.int32, (rows, rows), 1)
    tri = (c64 <= r64).astype(F32)
    log_cum = jnp.dot(tri, rate, precision=HIGHEST, preferred_element_type=F32)
    fill = jnp.zeros((rows, LANES - heads), F32)
    wide_cum = jnp.concatenate([log_cum, fill], axis=1)
    wide_step = jnp.concatenate([step, fill], axis=1)
    cum_rows = jnp.concatenate([wide_cum, wide_cum], axis=0).T
    step_rows = jnp.concatenate([wide_step, wide_step], axis=0).T
    b = x_ref[:, edge : edge + state]
    c = x_ref[:, edge + state : edge + 2 * state]
    twice = jnp.concatenate([b, b], axis=0)
    corr = lax.dot_general(c, twice, (((1,), (1,)), ((), ())), preferred_element_type=F32)
    lane = lax.broadcasted_iota(jnp.int32, (rows, LANES), 1)
    row = lax.broadcasted_iota(jnp.int32, (rows, LANES), 0)
    first = lane < size
    causal = jnp.where(first, lane, lane - size) <= row
    first_row = lax.broadcasted_iota(jnp.int32, (1, LANES), 1) < size

    own = seq_rows // 2
    side = r64 // half
    place = r64 - side * half
    which = (mine + side + turn(place // own)) % 2
    source = (place // own) * seq_rows + which * own + place % own
    order = (c64 == source).astype(BF16)

    squares = jnp.zeros((rows, LANES), F32)
    for j in range(heads // 2):
        left, right = 2 * j, 2 * j + 1
        span = slice(j * LANES, (j + 1) * LANES)
        at = jnp.where(first, log_cum[:, left : left + 1], log_cum[:, right : right + 1])
        back = jnp.where(first_row, cum_rows[left : left + 1], cum_rows[right : right + 1])
        sizes = jnp.where(first_row, step_rows[left : left + 1], step_rows[right : right + 1])
        weights = jnp.exp(jnp.where(causal, at - back, NEG)) * (corr * sizes)
        high = weights.astype(BF16)
        low = (weights - high.astype(F32)).astype(BF16)
        v = x_ref[:, span]
        none = jnp.zeros_like(v)
        stacked = jnp.concatenate([jnp.where(first, v, none), jnp.where(first, none, v)], axis=0)
        y = jnp.dot(high, stacked, preferred_element_type=F32)
        y = y + jnp.dot(low, stacked, preferred_element_type=F32)
        skip = jnp.where(first_row, skip_ref[0, left], skip_ref[0, right])
        mixed = y + skip * v.astype(F32)
        gate = x_ref[:, channels + j * LANES : channels + (j + 1) * LANES].astype(F32)
        gated = (mixed * (gate / (1.0 + jnp.exp(-gate)))).astype(BF16)
        moved = jnp.dot(order, gated, preferred_element_type=F32)
        squares = squares + moved * moved
        unit_ref[:, span] = (moved * gain_ref[:, span]).astype(BF16)
    partial = jnp.dot(unit_ref[...], weight_ref[...], preferred_element_type=F32)
    kept_ref[...] = jnp.dot(order[0:half], residual_ref[...], preferred_element_type=F32)

    at_row = row % seq_rows
    info = jnp.zeros((rows, LANES), F32)
    for k in range(3):
        column = jnp.sum(
            jnp.where(lane == IDS + k * seq_rows + at_row, misc, 0.0), axis=1, keepdims=True
        )
        info = jnp.where(lane == k + 1, column, info)
    info = jnp.dot(order, info.astype(BF16), preferred_element_type=F32)
    total = jnp.sum(squares, axis=1, keepdims=True)
    info = jnp.where(lane == 0, total, info)
    width = partial.shape[1]
    start = mine_ref.shape[1] - LANES
    mine_ref[:, 0:width] = partial[0:half]
    mine_ref[:, start:] = info[0:half]
    theirs_ref[:, 0:width] = partial[half:]
    theirs_ref[:, start:] = info[half:]


def mixer(x, seq_rows, bias, decay, skip, gain, weight, residual):
    rows = x.shape[0]
    heads = bias.shape[0]
    channels = gain.shape[0]
    width = weight.shape[1]
    total = (width + LANES - 1) // LANES * LANES + LANES
    half = rows // 2
    sums = jax.ShapeDtypeStruct((half, total), F32)
    whole = pl.BlockSpec(memory_space=VMEM)

    def kernel(*refs):
        mixer_kernel(seq_rows, *refs)

    return pl.pallas_call(
        kernel,
        out_shape=(sums, sums, jax.ShapeDtypeStruct((half, width), F32)),
        in_specs=[whole, whole, whole, pl.BlockSpec(memory_space=pltpu.SMEM), whole, whole, whole],
        scratch_shapes=[VMEM((rows, channels), BF16)],
        compiler_params=grant(8),
        name="mixer",
    )(
        x, bias.reshape(1, heads), decay.reshape(1, heads), skip.reshape(1, heads),
        gain.reshape(1, channels), weight, residual,
    )


def hidden_kernel(features, mine_ref, theirs_ref, kept_ref, out_ref):
    count, half, _ = out_ref.shape
    width = kept_ref.shape[1]
    start = mine_ref.shape[1] - LANES
    squares = mine_ref[:, start : start + 1] + theirs_ref[:, start : start + 1]
    scale = lax.rsqrt(squares / features + EPS)
    sums = mine_ref[:, 0:width] + theirs_ref[:, 0:width]
    hidden = (kept_ref[...] + sums * scale).astype(BF16).astype(F32)
    paired = jnp.concatenate([hidden[0:half], hidden[half:]], axis=1).astype(BF16)
    for k in range(count):
        out_ref[k] = paired


def hidden_rows(count, features, mine, theirs, kept):
    def kernel(*refs):
        hidden_kernel(features, *refs)

    return pl.pallas_call(
        kernel,
        out_shape=jax.ShapeDtypeStruct((count, kept.shape[0] // 2, 2 * kept.shape[1]), BF16),
        compiler_params=grant(4),
        name="hidden",
    )(mine, theirs, kept)


def head_kernel(
    h_ref, gain_ref, own_ref, other_ref, own_mask_ref, other_mask_ref, info_ref, out_ref
):
    core = lax.axis_index("vocab")
    block = lax.axis_index("seq") * 2
    count, half, width = h_ref.shape
    rows, width = 2 * half, width // 2
    features = count * width
    squares = jnp.zeros((rows, width), F32)
    parts = []
    for k in range(count):
        pair = h_ref[k].astype(F32)
        part = jnp.concatenate([pair[:, 0:width], pair[:, width:]], axis=0)
        parts.append(part)
        squares = squares + part * part
    scale = lax.rsqrt(jnp.sum(squares, axis=1, keepdims=True) / features + EPS)
    entries = own_ref.shape[1]
    logits = [jnp.zeros((rows, entries), F32), jnp.zeros((rows, entries), F32)]
    for k in range(count):
        final = (parts[k] * scale * gain_ref[k : k + 1, :]).astype(BF16)
        span = slice(k * width, (k + 1) * width)
        for i, ref in enumerate((own_ref, other_ref)):
            logits[i] = logits[i] + jnp.dot(final, ref[span, :], preferred_element_type=F32)
    states = own_mask_ref.shape[0]
    start = info_ref.shape[1] - LANES
    ids = info_ref[:, start + 1 : start + 2].astype(jnp.int32)
    upper = info_ref[:, start + 2 : start + 3].astype(jnp.int32)
    target = upper * 256 + info_ref[:, start + 3 : start + 4].astype(jnp.int32)
    pick_row = (lax.broadcasted_iota(jnp.int32, (rows, states), 1) == ids).astype(BF16)
    column = lax.broadcasted_iota(jnp.int32, (rows, entries), 1)
    allowed, wanted = [], []
    for ref, which in ((own_mask_ref, core), (other_mask_ref, 1 - core)):
        table = (ref[...] == 1).astype(F32).astype(BF16)
        chosen = jnp.dot(pick_row, table, preferred_element_type=F32)
        is_target = column + (block + which) * entries == target
        wanted.append(is_target)
        allowed.append((chosen > 0.5) | is_target)
    tops = [
        jnp.max(jnp.where(a, x, NEG), axis=1, keepdims=True) for a, x in zip(allowed, logits)
    ]
    top = jnp.maximum(tops[0], tops[1])
    total = jnp.zeros((rows, 1), F32)
    picked = jnp.zeros((rows, 1), F32)
    for a, w, x in zip(allowed, wanted, logits):
        total = total + jnp.sum(jnp.where(a, jnp.exp(x - top), 0.0), axis=1, keepdims=True)
        picked = picked + jnp.sum(jnp.where(w, x, 0.0), axis=1, keepdims=True)
    lane = lax.broadcasted_iota(jnp.int32, (rows, LANES), 1)
    stats = jnp.where(lane == 0, top, jnp.where(lane == 1, total, picked))
    own = out_ref.shape[1]
    for k in range(count):
        out_ref[k] = stats[k * own : (k + 1) * own]


def head(h, gain, own, other, own_mask, other_mask, info):
    count, half, width = h.shape
    whole = pl.BlockSpec(memory_space=VMEM)
    return pl.pallas_call(
        head_kernel,
        out_shape=jax.ShapeDtypeStruct((count, 2 * half // count, LANES), F32),
        in_specs=[whole] * 7,
        compiler_params=grant(12),
        name="head",
    )(h, gain.reshape(count, width // 2), own, other, own_mask, other_mask, info)


def combine_kernel(stats_ref, out_ref):
    count = stats_ref.shape[0]
    top = stats_ref[0, :, 0:1]
    for k in range(1, count):
        top = jnp.maximum(top, stats_ref[k, :, 0:1])
    total = jnp.zeros_like(top)
    picked = jnp.zeros_like(top)
    for k in range(count):
        total = total + stats_ref[k, :, 1:2] * jnp.exp(stats_ref[k, :, 0:1] - top)
        picked = picked + stats_ref[k, :, 2:3]
    losses = jnp.broadcast_to(jnp.log(total) + top - picked, (top.shape[0], LANES))
    row = lax.broadcasted_iota(jnp.int32, losses.shape, 0)
    lane = lax.broadcasted_iota(jnp.int32, losses.shape, 1)
    flat = jnp.sum(jnp.where(row == lane, losses, 0.0), axis=0, keepdims=True)
    out_ref[...] = flat[:, 0 : out_ref.shape[1]]


def combine(stats):
    own = stats.shape[1]
    out = pl.pallas_call(
        combine_kernel,
        out_shape=jax.ShapeDtypeStruct((1, own), F32),
        compiler_params=grant(2),
        name="combine",
    )(stats)
    return out.reshape(own)


def wide_pack(count, ssm, gate, b, c, raw, ids, targets):
    rows = ssm.shape[0]
    heads = raw.shape[1]
    high = lax.reduce_precision(raw, 8, 7)
    middle = lax.reduce_precision(raw - high, 8, 7)
    low = raw - high - middle
    parts = [high, middle, low, jnp.zeros((rows, IDS - 3 * heads), F32)]
    parts += [a.astype(F32)[:, None] for a in (ids, targets // 256, targets % 256)]
    parts.append(jnp.zeros((rows, LANES - IDS - 3), F32))
    misc = jnp.concatenate(parts, axis=1).astype(BF16)
    row = jnp.concatenate([ssm, gate, b, c, misc], axis=1)
    return jnp.broadcast_to(row[None], (count,) + row.shape)


def wide_mixer(x, seq_rows, bias, decay, skip, gain, weight, residual):
    rows = x.shape[0]
    heads, channels = bias.shape[0], gain.shape[0]
    state = (x.shape[1] - LANES - 2 * channels) // 2
    edge = 2 * channels
    core = lax.axis_index("vocab")
    misc = x[:, edge + 2 * state :].astype(F32)
    raw = misc[:, 0:heads] + misc[:, heads : 2 * heads] + misc[:, 2 * heads : 3 * heads]
    step = jax.nn.softplus(raw + bias[None, :])
    log_cum = jnp.cumsum(step * -jnp.exp(decay)[None, :], axis=0)
    corr = jnp.dot(
        x[:, edge + state : edge + 2 * state],
        x[:, edge : edge + state].T,
        preferred_element_type=F32,
    )
    values = x[:, 0:channels].astype(F32).reshape(rows, heads, -1).transpose(1, 0, 2)
    causal = jnp.arange(rows)[:, None] >= jnp.arange(rows)[None, :]

    def one(inputs):
        cum, size, v = inputs
        weights = jnp.exp(jnp.where(causal, cum[:, None] - cum[None, :], NEG))
        return jnp.dot(weights * corr * size[None, :], v, precision=HIGHEST)

    y = lax.map(one, (log_cum.T, step.T, values))
    mixed = (y + skip[:, None, None] * values).transpose(1, 0, 2).reshape(rows, channels)
    gated = (mixed * jax.nn.silu(x[:, channels:edge].astype(F32))).astype(BF16)
    wide = gated.astype(F32)
    squares = jnp.sum(wide * wide, axis=1, keepdims=True)
    unit = (wide * gain[None, :]).astype(BF16)
    partial = jnp.dot(unit, weight, preferred_element_type=F32)
    width = weight.shape[1]
    start = (width + LANES - 1) // LANES * LANES
    info = jnp.concatenate([squares, misc[:, IDS : IDS + 3]], axis=1)
    sums = jnp.concatenate(
        [
            partial,
            jnp.zeros((rows, start - width), F32),
            info,
            jnp.zeros((rows, LANES - info.shape[1]), F32),
        ],
        axis=1,
    )

    def side(a, which):
        split = a.reshape(rows // seq_rows, 2, seq_rows // 2, -1)
        return lax.dynamic_index_in_dim(split, which, 1, False).reshape(rows // 2, -1)

    return side(sums, core), side(sums, 1 - core), side(residual.astype(F32), core)


def shards(
    ssm_input,
    gate_input,
    b_proj,
    readout_matrix,
    step_raw,
    step_bias,
    decay_log,
    head_skip_gain,
    norm_gain,
    out_weight,
    residual,
    final_gain,
    head_weight,
    mask_table,
    state_ids,
    targets,
):
    count = lax.axis_size("seq")
    rows, channels = ssm_input.shape
    features = 2 * channels
    small = count * rows <= LANES // 2
    swap = [(0, 1), (1, 0)]
    both = ("seq", "vocab")

    def exchange(a):
        if small:
            groups = circles(count)
            return lax.all_to_all(a, both, 0, 0, tiled=True, axis_index_groups=groups)
        return lax.all_to_all(a, "seq", 0, 0, tiled=True)

    other_weight = lax.ppermute(head_weight, "vocab", swap)
    other_mask = lax.ppermute(mask_table, "vocab", swap)
    packed = (pack if small else wide_pack)(
        count, ssm_input, gate_input, b_proj, readout_matrix, step_raw, state_ids, targets
    )
    gathered = lax.all_to_all(packed, "seq", 0, 0, tiled=True)
    x = gathered.reshape(count * rows, packed.shape[2])
    mine, theirs, kept = (mixer if small else wide_mixer)(
        x, rows, step_bias, decay_log, head_skip_gain, norm_gain, out_weight, residual
    )
    arrived = lax.ppermute(theirs, "vocab", swap)
    if small:
        spread = hidden_rows(count, features, mine, arrived, kept)
    else:
        width = kept.shape[1]
        start = mine.shape[1] - LANES
        sums = mine + arrived
        scale = lax.rsqrt(sums[:, start : start + 1] / features + EPS)
        hidden = (kept + sums[:, 0:width] * scale).astype(BF16)
        spread = jnp.broadcast_to(hidden[None], (count,) + hidden.shape)
    full = exchange(spread)
    if small:
        stats = head(full, final_gain, head_weight, other_weight, mask_table, other_mask, mine)
    else:
        stats = wide_head(
            full, final_gain, head_weight, other_weight, mask_table, other_mask, mine
        )
    placed = exchange(stats)
    return combine(placed) if small else wide_combine(placed)


def wide_head(full, gain, own, other, own_mask, other_mask, info):
    count, rows, width = full.shape
    core = lax.axis_index("vocab")
    block = lax.axis_index("seq") * 2
    wide = full.transpose(1, 0, 2).reshape(rows, count * width).astype(F32)
    scale = lax.rsqrt(jnp.mean(wide * wide, axis=1, keepdims=True) + EPS)
    final = (wide * scale * gain[None, :]).astype(BF16)
    start = info.shape[1] - LANES
    ids, upper, under = (info[:, start + k].astype(jnp.int32) for k in (1, 2, 3))
    target = upper * 256 + under
    entries = own.shape[1]
    logits, allowed, wanted = [], [], []
    for weight, table, which in ((own, own_mask, core), (other, other_mask, 1 - core)):
        logits.append(jnp.dot(final, weight, preferred_element_type=F32))
        column = (block + which) * entries + jnp.arange(entries, dtype=jnp.int32)
        wanted.append(column[None, :] == target[:, None])
        one_hot = (ids[:, None] == jnp.arange(table.shape[0])[None, :]).astype(BF16)
        chosen = jnp.dot(one_hot, (table == 1).astype(BF16), preferred_element_type=F32)
        allowed.append((chosen > 0.5) | wanted[-1])
    x, a, w = (jnp.concatenate(p, axis=1) for p in (logits, allowed, wanted))
    top = jnp.max(jnp.where(a, x, NEG), axis=1)
    total = jnp.sum(jnp.where(a, jnp.exp(x - top[:, None]), 0.0), axis=1)
    picked = jnp.sum(jnp.where(w, x, 0.0), axis=1)
    return jnp.stack([top, total, picked], axis=1).reshape(count, rows // count, 3)


def wide_combine(stats):
    top = jnp.max(stats[:, :, 0], axis=0)
    total = jnp.sum(stats[:, :, 1] * jnp.exp(stats[:, :, 0] - top[None, :]), axis=0)
    return jnp.log(total) + top - jnp.sum(stats[:, :, 2], axis=0)


def solution(mesh):
    placed = (
        P(("groups", "seq"), "vocab"),
        P(("groups", "seq"), "vocab"),
        P(("groups", "seq"), None),
        P(("groups", "seq"), None),
        P(("groups", "seq"), "vocab"),
        P("vocab"),
        P("vocab"),
        P("vocab"),
        P("vocab"),
        P("vocab", "seq"),
        P("groups", "seq"),
        P(),
        P(None, ("seq", "vocab")),
        P(None, ("seq", "vocab")),
        P(("groups", "seq")),
        P(("groups", "seq")),
    )
    return jax.shard_map(
        shards, mesh=mesh, in_specs=placed, out_specs=P(("groups", "seq", "vocab")), check_vma=False
    )
```

```python
import jax
import jax.numpy as jnp
from jax import lax
from jax.experimental import pallas as pl
from jax.experimental.pallas import tpu as pltpu
from jax.sharding import PartitionSpec as P

F32 = jnp.float32
BF16 = jnp.bfloat16
HIGHEST = lax.Precision.HIGHEST
EPS = 1e-05
LANES = 128
NEG = -1e30
INFO = 60
PARAMS = 64
VMEM = pltpu.VMEM


def times_transposed(a, b):
    return lax.dot_general(a, b, (((1,), (1,)), ((), ())), preferred_element_type=F32)


def grant(mebibytes):
    return pltpu.CompilerParams(vmem_limit_bytes=mebibytes << 20)


def turn(seq):
    return (seq // 2) % 2


def circles(count):
    return [[2 * s + (w + turn(s)) % 2 for s in range(count)] for w in range(2)]


def thirds(a):
    high = a.astype(BF16).astype(F32)
    middle = (a - high).astype(BF16).astype(F32)
    return high, middle, a - high - middle


def pack_kernel(
    ssm_ref, gate_ref, b_ref, c_ref, raw_ref, bias_ref, decay_ref, skip_ref, ids_ref, targets_ref,
    out_ref,
):
    count, rows, _ = out_ref.shape
    channels = ssm_ref.shape[1]
    state = b_ref.shape[1]
    heads = raw_ref.shape[1]
    edge = 2 * channels
    parts = list(thirds(jax.nn.softplus(raw_ref[...] + bias_ref[...])))
    row = lax.broadcasted_iota(jnp.int32, (rows, rows), 0)
    diagonal = row == lax.broadcasted_iota(jnp.int32, (rows, rows), 1)

    def upright(a):
        wide = jnp.broadcast_to(a.astype(F32), (rows, rows))
        return jnp.sum(jnp.where(diagonal, wide, 0.0), axis=1, keepdims=True)

    targets = upright(targets_ref[...])
    upper = jnp.floor(targets / 256.0)
    parts += [upright(ids_ref[...]), upper, targets - upper * 256.0]
    parts.append(jnp.zeros((rows, PARAMS - INFO - 3), F32))
    params = list(thirds(-jnp.exp(decay_ref[...]))) + list(thirds(skip_ref[...]))
    place = lax.broadcasted_iota(jnp.int32, (rows, heads), 0)
    table = jnp.zeros((rows, heads), F32)
    for k, part in enumerate(params):
        table = jnp.where(place == k, part, table)
    parts += [table, jnp.zeros((rows, LANES - PARAMS - heads), F32)]
    misc = jnp.concatenate(parts, axis=1).astype(BF16)
    for k in range(count):
        out_ref[k, :, 0:channels] = ssm_ref[...]
        out_ref[k, :, channels:edge] = gate_ref[...]
        out_ref[k, :, edge : edge + state] = b_ref[...]
        out_ref[k, :, edge + state : edge + 2 * state] = c_ref[...]
        out_ref[k, :, edge + 2 * state :] = misc


def pack(count, ssm, gate, b, c, raw, bias, decay, skip, ids, targets):
    rows, channels = ssm.shape
    heads = bias.shape[0]
    width = 2 * channels + 2 * b.shape[1] + LANES
    return pl.pallas_call(
        pack_kernel,
        out_shape=jax.ShapeDtypeStruct((count, rows, width), BF16),
        name="pack",
    )(
        ssm, gate, b, c, raw, bias.reshape(1, heads), decay.reshape(1, heads),
        skip.reshape(1, heads), ids.reshape(1, rows), targets.reshape(1, rows),
    )


def mixer_kernel(
    seq_rows, heads, x_ref, gain_ref, weight_ref, residual_ref,
    mine_ref, theirs_ref, kept_ref, unit_ref,
):
    mine = lax.axis_index("vocab") + turn(lax.axis_index("seq"))
    rows = x_ref.shape[0]
    channels = gain_ref.shape[1]
    state = (x_ref.shape[1] - LANES - 2 * channels) // 2
    edge = 2 * channels
    half = rows // 2
    size = channels // heads
    packed = x_ref[:, edge + 2 * state :]
    misc = packed.astype(F32)
    step = misc[:, 0:heads] + misc[:, heads : 2 * heads] + misc[:, 2 * heads : 3 * heads]
    params = pltpu.roll(misc[0:8], LANES - PARAMS, 1)
    decay = params[0:1] + params[1:2] + params[2:3]
    gains = params[3:4] + params[4:5] + params[5:6]
    rate = step * decay[:, 0:heads]
    r64 = lax.broadcasted_iota(jnp.int32, (rows, rows), 0)
    c64 = lax.broadcasted_iota(jnp.int32, (rows, rows), 1)
    tri = (c64 <= r64).astype(F32)
    log_cum = jnp.dot(tri, rate, precision=HIGHEST, preferred_element_type=F32)
    fill = jnp.zeros((rows, LANES - heads), F32)
    wide_cum = jnp.concatenate([log_cum, fill], axis=1)
    wide_step = jnp.concatenate([step, fill], axis=1)
    cum_rows = jnp.concatenate([wide_cum, wide_cum], axis=0).T
    step_rows = jnp.concatenate([wide_step, wide_step], axis=0).T
    b = x_ref[:, edge : edge + state]
    c = x_ref[:, edge + state : edge + 2 * state]
    twice = jnp.concatenate([b, b], axis=0)
    corr = times_transposed(c, twice)
    lane = lax.broadcasted_iota(jnp.int32, (rows, LANES), 1)
    row = lax.broadcasted_iota(jnp.int32, (rows, LANES), 0)
    first = lane < size
    causal = jnp.where(first, lane, lane - size) <= row
    first_row = lax.broadcasted_iota(jnp.int32, (1, LANES), 1) < size

    own = seq_rows // 2
    side = r64 // half
    place = r64 - side * half
    which = (mine + side + turn(place // own)) % 2
    source = (place // own) * seq_rows + which * own + place % own
    order = (c64 == source).astype(BF16)

    squares = jnp.zeros((rows, LANES), F32)
    for j in range(heads // 2):
        left, right = 2 * j, 2 * j + 1
        span = slice(j * LANES, (j + 1) * LANES)
        at = jnp.where(first, log_cum[:, left : left + 1], log_cum[:, right : right + 1])
        back = jnp.where(first_row, cum_rows[left : left + 1], cum_rows[right : right + 1])
        sizes = jnp.where(first_row, step_rows[left : left + 1], step_rows[right : right + 1])
        weights = jnp.exp(jnp.where(causal, at - back, NEG)) * (corr * sizes)
        high = weights.astype(BF16)
        low = (weights - high.astype(F32)).astype(BF16)
        v = x_ref[:, span]
        none = jnp.zeros_like(v)
        stacked = jnp.concatenate([jnp.where(first, v, none), jnp.where(first, none, v)], axis=0)
        y = jnp.dot(high, stacked, preferred_element_type=F32)
        y = y + jnp.dot(low, stacked, preferred_element_type=F32)
        skip = jnp.where(
            first_row, gains[:, left : left + 1], gains[:, right : right + 1]
        )
        mixed = y + skip * v.astype(F32)
        gate = x_ref[:, channels + j * LANES : channels + (j + 1) * LANES].astype(F32)
        gated = (mixed * (gate / (1.0 + jnp.exp(-gate)))).astype(BF16)
        moved = jnp.dot(order, gated, preferred_element_type=F32)
        squares = squares + moved * moved
        unit_ref[:, span] = (moved * gain_ref[:, span]).astype(BF16)
    partial = times_transposed(unit_ref[...], weight_ref[...])
    kept_ref[...] = jnp.dot(order[0:half], residual_ref[...], preferred_element_type=F32)

    info = pltpu.roll(
        jnp.dot(order, packed, preferred_element_type=F32), LANES + 1 - INFO, 1
    )
    total = jnp.sum(squares, axis=1, keepdims=True)
    info = jnp.where(lane == 0, total, info)
    width = partial.shape[1]
    start = mine_ref.shape[1] - LANES
    mine_ref[:, 0:width] = partial[0:half]
    mine_ref[:, start:] = info[0:half]
    theirs_ref[:, 0:width] = partial[half:]
    theirs_ref[:, start:] = info[half:]


def mixer(x, seq_rows, heads, gain, weight, residual):
    rows = x.shape[0]
    channels = gain.shape[1]
    width = weight.shape[1]
    total = (width + LANES - 1) // LANES * LANES + LANES
    half = rows // 2
    sums = jax.ShapeDtypeStruct((half, total), F32)
    whole = pl.BlockSpec(memory_space=VMEM)

    def kernel(*refs):
        mixer_kernel(seq_rows, heads, *refs)

    return pl.pallas_call(
        kernel,
        out_shape=(sums, sums, jax.ShapeDtypeStruct((half, width), F32)),
        in_specs=[whole] * 4,
        scratch_shapes=[VMEM((rows, channels), BF16)],
        compiler_params=grant(8),
        name="mixer",
    )(x, gain, weight.T, residual)


def hidden_kernel(features, mine_ref, theirs_ref, kept_ref, out_ref):
    count, half, _ = out_ref.shape
    width = kept_ref.shape[1]
    start = mine_ref.shape[1] - LANES
    squares = mine_ref[:, start : start + 1] + theirs_ref[:, start : start + 1]
    scale = lax.rsqrt(squares / features + EPS)
    sums = mine_ref[:, 0:width] + theirs_ref[:, 0:width]
    hidden = (kept_ref[...] + sums * scale).astype(BF16).astype(F32)
    paired = jnp.concatenate([hidden[0:half], hidden[half:]], axis=1).astype(BF16)
    for k in range(count):
        out_ref[k] = paired


def hidden_rows(count, features, mine, theirs, kept):
    def kernel(*refs):
        hidden_kernel(features, *refs)

    return pl.pallas_call(
        kernel,
        out_shape=jax.ShapeDtypeStruct((count, kept.shape[0] // 2, 2 * kept.shape[1]), BF16),
        compiler_params=grant(4),
        name="hidden",
    )(mine, theirs, kept)


def head_kernel(
    h_ref, gain_ref, own_ref, o0_ref, o1_ref, o2_ref, o3_ref, own_mask_ref, other_mask_ref,
    info_ref, out_ref,
):
    core = lax.axis_index("vocab")
    block = lax.axis_index("seq") * 2
    count, half, width = h_ref.shape
    rows, width = 2 * half, width // 2
    features = count * width
    squares = jnp.zeros((rows, width), F32)
    parts = []
    for k in range(count):
        pair = h_ref[k].astype(F32)
        part = jnp.concatenate([pair[:, 0:width], pair[:, width:]], axis=0)
        parts.append(part)
        squares = squares + part * part
    scale = lax.rsqrt(jnp.sum(squares, axis=1, keepdims=True) / features + EPS)
    entries = own_ref.shape[0]
    parts = [parts[k] * scale * gain_ref[k : k + 1, :] for k in range(count)]
    final = jnp.concatenate(parts, axis=1).astype(BF16)
    logits = [times_transposed(final, own_ref[...])]
    depth = features // 4
    pieces = [
        times_transposed(final[:, k * depth : (k + 1) * depth], ref[...])
        for k, ref in enumerate((o0_ref, o1_ref, o2_ref, o3_ref))
    ]
    logits.append((pieces[0] + pieces[1]) + (pieces[2] + pieces[3]))
    states = own_mask_ref.shape[0]
    start = info_ref.shape[1] - LANES
    ids = info_ref[:, start + 1 : start + 2].astype(jnp.int32)
    upper = info_ref[:, start + 2 : start + 3].astype(jnp.int32)
    target = upper * 256 + info_ref[:, start + 3 : start + 4].astype(jnp.int32)
    pick_row = (lax.broadcasted_iota(jnp.int32, (rows, states), 1) == ids).astype(BF16)
    column = lax.broadcasted_iota(jnp.int32, (rows, entries), 1)
    allowed, wanted = [], []
    for ref, which in ((own_mask_ref, core), (other_mask_ref, 1 - core)):
        table = (ref[...] == 1).astype(F32).astype(BF16)
        chosen = jnp.dot(pick_row, table, preferred_element_type=F32)
        is_target = column + (block + which) * entries == target
        wanted.append(is_target)
        allowed.append((chosen > 0.5) | is_target)
    tops = [
        jnp.max(jnp.where(a, x, NEG), axis=1, keepdims=True) for a, x in zip(allowed, logits)
    ]
    top = jnp.maximum(tops[0], tops[1])
    total = jnp.zeros((rows, 1), F32)
    picked = jnp.zeros((rows, 1), F32)
    for a, w, x in zip(allowed, wanted, logits):
        total = total + jnp.sum(jnp.where(a, jnp.exp(x - top), 0.0), axis=1, keepdims=True)
        picked = picked + jnp.sum(jnp.where(w, x, 0.0), axis=1, keepdims=True)
    lane = lax.broadcasted_iota(jnp.int32, (rows, LANES), 1)
    stats = jnp.where(lane == 0, top, jnp.where(lane == 1, total, picked))
    own = out_ref.shape[1]
    for k in range(count):
        out_ref[k] = stats[k * own : (k + 1) * own]


def head(h, gain, own, other, own_mask, other_mask, info):
    count, half, width = h.shape
    whole = pl.BlockSpec(memory_space=VMEM)
    return pl.pallas_call(
        head_kernel,
        out_shape=jax.ShapeDtypeStruct((count, 2 * half // count, LANES), F32),
        in_specs=[whole] * 10,
        compiler_params=grant(12),
        name="head",
    )(h, gain, own.T, *(o.T for o in other), own_mask, other_mask, info)


def combine_kernel(stats_ref, out_ref):
    count = stats_ref.shape[0]
    top = stats_ref[0, :, 0:1]
    for k in range(1, count):
        top = jnp.maximum(top, stats_ref[k, :, 0:1])
    total = jnp.zeros_like(top)
    picked = jnp.zeros_like(top)
    for k in range(count):
        total = total + stats_ref[k, :, 1:2] * jnp.exp(stats_ref[k, :, 0:1] - top)
        picked = picked + stats_ref[k, :, 2:3]
    losses = jnp.broadcast_to(jnp.log(total) + top - picked, (top.shape[0], LANES))
    row = lax.broadcasted_iota(jnp.int32, losses.shape, 0)
    lane = lax.broadcasted_iota(jnp.int32, losses.shape, 1)
    flat = jnp.sum(jnp.where(row == lane, losses, 0.0), axis=0, keepdims=True)
    out_ref[...] = flat[:, 0 : out_ref.shape[1]]


def combine(stats):
    own = stats.shape[1]
    out = pl.pallas_call(
        combine_kernel,
        out_shape=jax.ShapeDtypeStruct((1, own), F32),
        compiler_params=grant(2),
        name="combine",
    )(stats)
    return out.reshape(own)


def wide_pack(count, ssm, gate, b, c, raw, bias, decay, skip, ids, targets):
    rows = ssm.shape[0]
    heads = raw.shape[1]

    def split(a):
        high = lax.reduce_precision(a, 8, 7)
        middle = lax.reduce_precision(a - high, 8, 7)
        return [high, middle, a - high - middle]

    parts = split(jax.nn.softplus(raw + bias[None, :]))
    parts += [a.astype(F32)[:, None] for a in (ids, targets // 256, targets % 256)]
    parts.append(jnp.zeros((rows, PARAMS - INFO - 3), F32))
    params = jnp.stack(split(-jnp.exp(decay)) + split(skip))
    parts.append(jnp.pad(params, ((0, rows - 6), (0, LANES - PARAMS - heads))))
    misc = jnp.concatenate(parts, axis=1).astype(BF16)
    row = jnp.concatenate([ssm, gate, b, c, misc], axis=1)
    return jnp.broadcast_to(row[None], (count,) + row.shape)


def wide_mixer(x, seq_rows, heads, gain, weight, residual):
    rows = x.shape[0]
    channels = gain.shape[1]
    state = (x.shape[1] - LANES - 2 * channels) // 2
    edge = 2 * channels
    core = lax.axis_index("vocab")
    misc = x[:, edge + 2 * state :].astype(F32)
    step = misc[:, 0:heads] + misc[:, heads : 2 * heads] + misc[:, 2 * heads : 3 * heads]
    params = misc[0:8, PARAMS : PARAMS + heads]
    decay = params[0] + params[1] + params[2]
    skip = params[3] + params[4] + params[5]
    log_cum = jnp.cumsum(step * decay[None, :], axis=0)
    corr = jnp.dot(
        x[:, edge + state : edge + 2 * state],
        x[:, edge : edge + state].T,
        preferred_element_type=F32,
    )
    values = x[:, 0:channels].astype(F32).reshape(rows, heads, -1).transpose(1, 0, 2)
    causal = jnp.arange(rows)[:, None] >= jnp.arange(rows)[None, :]

    def one(inputs):
        cum, size, v = inputs
        weights = jnp.exp(jnp.where(causal, cum[:, None] - cum[None, :], NEG))
        return jnp.dot(weights * corr * size[None, :], v, precision=HIGHEST)

    y = lax.map(one, (log_cum.T, step.T, values))
    mixed = (y + skip[:, None, None] * values).transpose(1, 0, 2).reshape(rows, channels)
    gated = (mixed * jax.nn.silu(x[:, channels:edge].astype(F32))).astype(BF16)
    wide = gated.astype(F32)
    squares = jnp.sum(wide * wide, axis=1, keepdims=True)
    unit = (wide * gain).astype(BF16)
    partial = jnp.dot(unit, weight, preferred_element_type=F32)
    width = weight.shape[1]
    start = (width + LANES - 1) // LANES * LANES
    info = jnp.concatenate([squares, misc[:, INFO : INFO + 3]], axis=1)
    sums = jnp.concatenate(
        [
            partial,
            jnp.zeros((rows, start - width), F32),
            info,
            jnp.zeros((rows, LANES - info.shape[1]), F32),
        ],
        axis=1,
    )

    def side(a, which):
        split = a.reshape(rows // seq_rows, 2, seq_rows // 2, -1)
        return lax.dynamic_index_in_dim(split, which, 1, False).reshape(rows // 2, -1)

    return side(sums, core), side(sums, 1 - core), side(residual.astype(F32), core)


def shards(
    ssm_input,
    gate_input,
    b_proj,
    readout_matrix,
    step_raw,
    step_bias,
    decay_log,
    head_skip_gain,
    norm_gain,
    out_weight,
    residual,
    final_gain,
    head_weight,
    mask_table,
    state_ids,
    targets,
):
    count = lax.axis_size("seq")
    rows, channels = ssm_input.shape
    features = 2 * channels
    small = count * rows <= LANES // 2
    swap = [(0, 1), (1, 0)]
    both = ("seq", "vocab")

    def exchange(a):
        if small:
            groups = circles(count)
            return lax.all_to_all(a, both, 0, 0, tiled=True, axis_index_groups=groups)
        return lax.all_to_all(a, "seq", 0, 0, tiled=True)

    packed = (pack if small else wide_pack)(
        count, ssm_input, gate_input, b_proj, readout_matrix, step_raw, step_bias, decay_log,
        head_skip_gain, state_ids, targets,
    )
    if small:
        depth = features // 4
        other_weight = tuple(
            lax.ppermute(head_weight[k * depth : (k + 1) * depth], "vocab", swap) for k in range(4)
        )
    else:
        other_weight = lax.ppermute(head_weight, "vocab", swap)
    other_mask = lax.ppermute(mask_table, "vocab", swap)
    gathered = lax.all_to_all(packed, "seq", 0, 0, tiled=True)
    final_gain = final_gain.reshape(count, features // count)
    norm_gain = norm_gain.reshape(1, channels)
    if small:
        gathered, other_weight, other_mask, final_gain = lax.optimization_barrier(
            (gathered, other_weight, other_mask, final_gain)
        )
    x = gathered.reshape(count * rows, packed.shape[2])
    mine, theirs, kept = (mixer if small else wide_mixer)(
        x, rows, step_bias.shape[0], norm_gain, out_weight, residual
    )
    arrived = lax.ppermute(theirs, "vocab", swap)
    if small:
        spread = hidden_rows(count, features, mine, arrived, kept)
    else:
        width = kept.shape[1]
        start = mine.shape[1] - LANES
        sums = mine + arrived
        scale = lax.rsqrt(sums[:, start : start + 1] / features + EPS)
        hidden = (kept + sums[:, 0:width] * scale).astype(BF16)
        spread = jnp.broadcast_to(hidden[None], (count,) + hidden.shape)
    full = exchange(spread)
    if small:
        stats = head(full, final_gain, head_weight, other_weight, mask_table, other_mask, mine)
    else:
        stats = wide_head(
            full, final_gain, head_weight, other_weight, mask_table, other_mask, mine
        )
    placed = exchange(stats)
    return combine(placed) if small else wide_combine(placed)


def wide_head(full, gain, own, other, own_mask, other_mask, info):
    count, rows, width = full.shape
    core = lax.axis_index("vocab")
    block = lax.axis_index("seq") * 2
    wide = full.transpose(1, 0, 2).reshape(rows, count * width).astype(F32)
    scale = lax.rsqrt(jnp.mean(wide * wide, axis=1, keepdims=True) + EPS)
    final = (wide * scale * gain.reshape(1, -1)).astype(BF16)
    start = info.shape[1] - LANES
    ids, upper, under = (info[:, start + k].astype(jnp.int32) for k in (1, 2, 3))
    target = upper * 256 + under
    entries = own.shape[1]
    logits, allowed, wanted = [], [], []
    for weight, table, which in ((own, own_mask, core), (other, other_mask, 1 - core)):
        logits.append(jnp.dot(final, weight, preferred_element_type=F32))
        column = (block + which) * entries + jnp.arange(entries, dtype=jnp.int32)
        wanted.append(column[None, :] == target[:, None])
        one_hot = (ids[:, None] == jnp.arange(table.shape[0])[None, :]).astype(BF16)
        chosen = jnp.dot(one_hot, (table == 1).astype(BF16), preferred_element_type=F32)
        allowed.append((chosen > 0.5) | wanted[-1])
    x, a, w = (jnp.concatenate(p, axis=1) for p in (logits, allowed, wanted))
    top = jnp.max(jnp.where(a, x, NEG), axis=1)
    total = jnp.sum(jnp.where(a, jnp.exp(x - top[:, None]), 0.0), axis=1)
    picked = jnp.sum(jnp.where(w, x, 0.0), axis=1)
    return jnp.stack([top, total, picked], axis=1).reshape(count, rows // count, 3)


def wide_combine(stats):
    top = jnp.max(stats[:, :, 0], axis=0)
    total = jnp.sum(stats[:, :, 1] * jnp.exp(stats[:, :, 0] - top[None, :]), axis=0)
    return jnp.log(total) + top - jnp.sum(stats[:, :, 2], axis=0)


def solution(mesh):
    placed = (
        P(("groups", "seq"), "vocab"),
        P(("groups", "seq"), "vocab"),
        P(("groups", "seq"), None),
        P(("groups", "seq"), None),
        P(("groups", "seq"), "vocab"),
        P("vocab"),
        P("vocab"),
        P("vocab"),
        P("vocab"),
        P("vocab", "seq"),
        P("groups", "seq"),
        P(),
        P(None, ("seq", "vocab")),
        P(None, ("seq", "vocab")),
        P(("groups", "seq")),
        P(("groups", "seq")),
    )
    return jax.shard_map(
        shards, mesh=mesh, in_specs=placed, out_specs=P(("groups", "seq", "vocab")), check_vma=False
    )
```

```python
import jax
import jax.numpy as jnp
from jax import lax
from jax.experimental import pallas as pl
from jax.experimental.pallas import tpu as pltpu
from jax.sharding import PartitionSpec as P

F32 = jnp.float32
BF16 = jnp.bfloat16
HIGHEST = lax.Precision.HIGHEST
EPS = 1e-05
LANES = 128
NEG = -1e30
INFO = 60
PARAMS = 64
VMEM = pltpu.VMEM


def times_transposed(a, b):
    return lax.dot_general(a, b, (((1,), (1,)), ((), ())), preferred_element_type=F32)


def grant(mebibytes):
    return pltpu.CompilerParams(vmem_limit_bytes=mebibytes << 20)


def turn(seq):
    return (seq // 2) % 2


def circles(count):
    return [[2 * s + (w + turn(s)) % 2 for s in range(count)] for w in range(2)]


def thirds(a):
    high = a.astype(BF16).astype(F32)
    middle = (a - high).astype(BF16).astype(F32)
    return high, middle, a - high - middle


def pack_kernel(
    ssm_ref, gate_ref, b_ref, c_ref, raw_ref, bias_ref, decay_ref, skip_ref, ids_ref, targets_ref,
    out_ref,
):
    count, rows, _ = out_ref.shape
    channels = ssm_ref.shape[1]
    state = b_ref.shape[1]
    heads = raw_ref.shape[1]
    edge = 2 * channels
    parts = list(thirds(jax.nn.softplus(raw_ref[...] + bias_ref[...])))
    row = lax.broadcasted_iota(jnp.int32, (rows, rows), 0)
    diagonal = row == lax.broadcasted_iota(jnp.int32, (rows, rows), 1)

    def upright(a):
        wide = jnp.broadcast_to(a.astype(F32), (rows, rows))
        return jnp.sum(jnp.where(diagonal, wide, 0.0), axis=1, keepdims=True)

    targets = upright(targets_ref[...])
    upper = jnp.floor(targets / 256.0)
    parts += [upright(ids_ref[...]), upper, targets - upper * 256.0]
    parts.append(jnp.zeros((rows, PARAMS - INFO - 3), F32))
    params = list(thirds(-jnp.exp(decay_ref[...]))) + list(thirds(skip_ref[...]))
    place = lax.broadcasted_iota(jnp.int32, (rows, heads), 0)
    table = jnp.zeros((rows, heads), F32)
    for k, part in enumerate(params):
        table = jnp.where(place == k, part, table)
    parts += [table, jnp.zeros((rows, LANES - PARAMS - heads), F32)]
    misc = jnp.concatenate(parts, axis=1).astype(BF16)
    for k in range(count):
        out_ref[k, :, 0:channels] = ssm_ref[...]
        out_ref[k, :, channels:edge] = gate_ref[...]
        out_ref[k, :, edge : edge + state] = b_ref[...]
        out_ref[k, :, edge + state : edge + 2 * state] = c_ref[...]
        out_ref[k, :, edge + 2 * state :] = misc


def pack(count, ssm, gate, b, c, raw, bias, decay, skip, ids, targets):
    rows, channels = ssm.shape
    heads = bias.shape[0]
    width = 2 * channels + 2 * b.shape[1] + LANES
    return pl.pallas_call(
        pack_kernel,
        out_shape=jax.ShapeDtypeStruct((count, rows, width), BF16),
        name="pack",
    )(
        ssm, gate, b, c, raw, bias.reshape(1, heads), decay.reshape(1, heads),
        skip.reshape(1, heads), ids.reshape(1, rows), targets.reshape(1, rows),
    )


def mixer_kernel(
    seq_rows, heads, x_ref, gain_ref, weight_ref, residual_ref,
    mine_ref, theirs_ref, kept_ref,
):
    mine = lax.axis_index("vocab") + turn(lax.axis_index("seq"))
    rows = x_ref.shape[0]
    channels = gain_ref.shape[1]
    state = (x_ref.shape[1] - LANES - 2 * channels) // 2
    edge = 2 * channels
    half = rows // 2
    size = channels // heads
    r64 = lax.broadcasted_iota(jnp.int32, (rows, rows), 0)
    c64 = lax.broadcasted_iota(jnp.int32, (rows, rows), 1)
    own = seq_rows // 2
    side = (r64 >= half).astype(jnp.int32)
    place = r64 - side * half
    seq = lax.shift_right_logical(place, own.bit_length() - 1)
    which = (mine + side + lax.shift_right_logical(seq, 1)) & 1
    source = place + seq * own + which * own
    order = (c64 == source).astype(BF16)
    causal = c64 <= source
    moved = jnp.dot(order, x_ref[...], preferred_element_type=F32)

    misc = x_ref[:, edge + 2 * state :].astype(F32)
    step = misc[:, 0:heads] + misc[:, heads : 2 * heads] + misc[:, 2 * heads : 3 * heads]
    params = pltpu.roll(misc[0:8], LANES - PARAMS, 1)
    decay = params[0:1] + params[1:2] + params[2:3]
    gains = params[3:4] + params[4:5] + params[5:6]
    rates = jnp.concatenate(thirds(step * decay[:, 0:heads]), axis=1).astype(BF16)
    sums = jnp.concatenate([(c64 <= r64).astype(BF16), causal.astype(BF16)], axis=0)
    cums = jnp.dot(sums, rates, preferred_element_type=F32)
    cums = cums[:, 0:heads] + cums[:, heads : 2 * heads] + cums[:, 2 * heads :]
    middle = cums[half - 1 : half]
    ahead = jnp.exp(cums[rows:] - middle)
    back = jnp.exp(middle - cums[0:rows]) * step
    skips = jnp.broadcast_to(gains[:, 0:heads], (8, heads))
    factors = jnp.concatenate([ahead, back, skips], axis=0)
    factors = jnp.concatenate(thirds(factors), axis=1).astype(BF16)
    head_row = lax.broadcasted_iota(jnp.int32, (3 * heads, channels), 0)
    for _ in range(2):
        head_row = jnp.where(head_row >= heads, head_row - heads, head_row)
    from_head = lax.broadcasted_iota(jnp.int32, (3 * heads, channels), 1) - head_row * size
    spread = ((from_head >= 0) & (from_head < size)).astype(BF16)
    wide = jnp.dot(factors, spread, preferred_element_type=F32)

    c = moved[:, edge + state : edge + 2 * state].astype(BF16)
    corr = times_transposed(c, x_ref[:, edge : edge + state])
    corr = jnp.where(causal, corr, 0.0)
    high = corr.astype(BF16).astype(F32)
    corr = jnp.concatenate([high, corr - high, high], axis=1).astype(BF16)
    scaled = wide[rows : 2 * rows] * x_ref[:, 0:channels].astype(F32)
    high = scaled.astype(BF16)
    low = (scaled - high.astype(F32)).astype(BF16)
    y = jnp.dot(corr, jnp.concatenate([high, high, low], axis=0), preferred_element_type=F32)
    mixed = wide[0:rows] * y + wide[2 * rows : 2 * rows + 1] * moved[:, 0:channels]
    gate = moved[:, channels:edge]
    gated = (mixed * (gate / (1.0 + jnp.exp(-gate)))).astype(BF16).astype(F32)
    unit = (gated * gain_ref[...]).astype(BF16)
    partial = times_transposed(unit, weight_ref[...])
    total = jnp.sum(gated * gated, axis=1, keepdims=True)
    kept_ref[...] = jnp.dot(order[0:half], residual_ref[...], preferred_element_type=F32)

    lane = lax.broadcasted_iota(jnp.int32, (rows, LANES), 1)
    info = pltpu.roll(moved[:, edge + 2 * state :], LANES + 1 - INFO, 1)
    info = jnp.where(lane == 0, total, info)
    width = partial.shape[1]
    start = mine_ref.shape[1] - LANES
    mine_ref[:, 0:width] = partial[0:half]
    mine_ref[:, start:] = info[0:half]
    theirs_ref[:, 0:width] = partial[half:]
    theirs_ref[:, start:] = info[half:]


def mixer(x, seq_rows, heads, gain, weight, residual):
    rows = x.shape[0]
    channels = gain.shape[1]
    width = weight.shape[1]
    total = (width + LANES - 1) // LANES * LANES + LANES
    half = rows // 2
    sums = jax.ShapeDtypeStruct((half, total), F32)
    whole = pl.BlockSpec(memory_space=VMEM)

    def kernel(*refs):
        mixer_kernel(seq_rows, heads, *refs)

    return pl.pallas_call(
        kernel,
        out_shape=(sums, sums, jax.ShapeDtypeStruct((half, width), F32)),
        in_specs=[whole] * 4,
        compiler_params=grant(8),
        name="mixer",
    )(x, gain, weight.T, residual)


def hidden_kernel(features, mine_ref, theirs_ref, kept_ref, out_ref):
    count, half, _ = out_ref.shape
    width = kept_ref.shape[1]
    start = mine_ref.shape[1] - LANES
    squares = mine_ref[:, start : start + 1] + theirs_ref[:, start : start + 1]
    scale = lax.rsqrt(squares / features + EPS)
    sums = mine_ref[:, 0:width] + theirs_ref[:, 0:width]
    hidden = (kept_ref[...] + sums * scale).astype(BF16).astype(F32)
    paired = jnp.concatenate([hidden[0:half], hidden[half:]], axis=1).astype(BF16)
    for k in range(count):
        out_ref[k] = paired


def hidden_rows(count, features, mine, theirs, kept):
    def kernel(*refs):
        hidden_kernel(features, *refs)

    return pl.pallas_call(
        kernel,
        out_shape=jax.ShapeDtypeStruct((count, kept.shape[0] // 2, 2 * kept.shape[1]), BF16),
        compiler_params=grant(4),
        name="hidden",
    )(mine, theirs, kept)


def head_kernel(
    h_ref, gain_ref, own_ref, o0_ref, o1_ref, o2_ref, o3_ref, own_mask_ref, other_mask_ref,
    info_ref, out_ref,
):
    core = lax.axis_index("vocab")
    block = lax.axis_index("seq") * 2
    count, half, width = h_ref.shape
    rows, width = 2 * half, width // 2
    features = count * width
    squares = jnp.zeros((rows, width), F32)
    parts = []
    for k in range(count):
        pair = h_ref[k].astype(F32)
        part = jnp.concatenate([pair[:, 0:width], pair[:, width:]], axis=0)
        parts.append(part)
        squares = squares + part * part
    scale = lax.rsqrt(jnp.sum(squares, axis=1, keepdims=True) / features + EPS)
    entries = own_ref.shape[0]
    parts = [parts[k] * scale * gain_ref[k : k + 1, :] for k in range(count)]
    final = jnp.concatenate(parts, axis=1).astype(BF16)
    logits = [times_transposed(final, own_ref[...])]
    depth = features // 4
    pieces = [
        times_transposed(final[:, k * depth : (k + 1) * depth], ref[...])
        for k, ref in enumerate((o0_ref, o1_ref, o2_ref, o3_ref))
    ]
    logits.append((pieces[0] + pieces[1]) + (pieces[2] + pieces[3]))
    states = own_mask_ref.shape[0]
    start = info_ref.shape[1] - LANES
    ids = info_ref[:, start + 1 : start + 2].astype(jnp.int32)
    upper = info_ref[:, start + 2 : start + 3].astype(jnp.int32)
    target = upper * 256 + info_ref[:, start + 3 : start + 4].astype(jnp.int32)
    pick_row = (lax.broadcasted_iota(jnp.int32, (rows, states), 1) == ids).astype(BF16)
    column = lax.broadcasted_iota(jnp.int32, (rows, entries), 1)
    allowed, wanted = [], []
    for ref, which in ((own_mask_ref, core), (other_mask_ref, 1 - core)):
        table = (ref[...] == 1).astype(F32).astype(BF16)
        chosen = jnp.dot(pick_row, table, preferred_element_type=F32)
        is_target = column + (block + which) * entries == target
        wanted.append(is_target)
        allowed.append((chosen > 0.5) | is_target)
    tops = [
        jnp.max(jnp.where(a, x, NEG), axis=1, keepdims=True) for a, x in zip(allowed, logits)
    ]
    top = jnp.maximum(tops[0], tops[1])
    total = jnp.zeros((rows, 1), F32)
    picked = jnp.zeros((rows, 1), F32)
    for a, w, x in zip(allowed, wanted, logits):
        total = total + jnp.sum(jnp.where(a, jnp.exp(x - top), 0.0), axis=1, keepdims=True)
        picked = picked + jnp.sum(jnp.where(w, x, 0.0), axis=1, keepdims=True)
    lane = lax.broadcasted_iota(jnp.int32, (rows, LANES), 1)
    stats = jnp.where(lane == 0, top, jnp.where(lane == 1, total, picked))
    own = out_ref.shape[1]
    for k in range(count):
        out_ref[k] = stats[k * own : (k + 1) * own]


def head(h, gain, own, other, own_mask, other_mask, info):
    count, half, width = h.shape
    whole = pl.BlockSpec(memory_space=VMEM)
    return pl.pallas_call(
        head_kernel,
        out_shape=jax.ShapeDtypeStruct((count, 2 * half // count, LANES), F32),
        in_specs=[whole] * 10,
        compiler_params=grant(12),
        name="head",
    )(h, gain, own.T, *(o.T for o in other), own_mask, other_mask, info)


def combine_kernel(stats_ref, out_ref):
    count = stats_ref.shape[0]
    top = stats_ref[0, :, 0:1]
    for k in range(1, count):
        top = jnp.maximum(top, stats_ref[k, :, 0:1])
    total = jnp.zeros_like(top)
    picked = jnp.zeros_like(top)
    for k in range(count):
        total = total + stats_ref[k, :, 1:2] * jnp.exp(stats_ref[k, :, 0:1] - top)
        picked = picked + stats_ref[k, :, 2:3]
    losses = jnp.broadcast_to(jnp.log(total) + top - picked, (top.shape[0], LANES))
    row = lax.broadcasted_iota(jnp.int32, losses.shape, 0)
    lane = lax.broadcasted_iota(jnp.int32, losses.shape, 1)
    flat = jnp.sum(jnp.where(row == lane, losses, 0.0), axis=0, keepdims=True)
    out_ref[...] = flat[:, 0 : out_ref.shape[1]]


def combine(stats):
    own = stats.shape[1]
    out = pl.pallas_call(
        combine_kernel,
        out_shape=jax.ShapeDtypeStruct((1, own), F32),
        compiler_params=grant(2),
        name="combine",
    )(stats)
    return out.reshape(own)


def wide_pack(count, ssm, gate, b, c, raw, bias, decay, skip, ids, targets):
    rows = ssm.shape[0]
    heads = raw.shape[1]

    def split(a):
        high = lax.reduce_precision(a, 8, 7)
        middle = lax.reduce_precision(a - high, 8, 7)
        return [high, middle, a - high - middle]

    parts = split(jax.nn.softplus(raw + bias[None, :]))
    parts += [a.astype(F32)[:, None] for a in (ids, targets // 256, targets % 256)]
    parts.append(jnp.zeros((rows, PARAMS - INFO - 3), F32))
    params = jnp.stack(split(-jnp.exp(decay)) + split(skip))
    parts.append(jnp.pad(params, ((0, rows - 6), (0, LANES - PARAMS - heads))))
    misc = jnp.concatenate(parts, axis=1).astype(BF16)
    row = jnp.concatenate([ssm, gate, b, c, misc], axis=1)
    return jnp.broadcast_to(row[None], (count,) + row.shape)


def wide_mixer(x, seq_rows, heads, gain, weight, residual):
    rows = x.shape[0]
    channels = gain.shape[1]
    state = (x.shape[1] - LANES - 2 * channels) // 2
    edge = 2 * channels
    core = lax.axis_index("vocab")
    misc = x[:, edge + 2 * state :].astype(F32)
    step = misc[:, 0:heads] + misc[:, heads : 2 * heads] + misc[:, 2 * heads : 3 * heads]
    params = misc[0:8, PARAMS : PARAMS + heads]
    decay = params[0] + params[1] + params[2]
    skip = params[3] + params[4] + params[5]
    log_cum = jnp.cumsum(step * decay[None, :], axis=0)
    corr = jnp.dot(
        x[:, edge + state : edge + 2 * state],
        x[:, edge : edge + state].T,
        preferred_element_type=F32,
    )
    values = x[:, 0:channels].astype(F32).reshape(rows, heads, -1).transpose(1, 0, 2)
    causal = jnp.arange(rows)[:, None] >= jnp.arange(rows)[None, :]

    def one(inputs):
        cum, size, v = inputs
        weights = jnp.exp(jnp.where(causal, cum[:, None] - cum[None, :], NEG))
        return jnp.dot(weights * corr * size[None, :], v, precision=HIGHEST)

    y = lax.map(one, (log_cum.T, step.T, values))
    mixed = (y + skip[:, None, None] * values).transpose(1, 0, 2).reshape(rows, channels)
    gated = (mixed * jax.nn.silu(x[:, channels:edge].astype(F32))).astype(BF16)
    wide = gated.astype(F32)
    squares = jnp.sum(wide * wide, axis=1, keepdims=True)
    unit = (wide * gain).astype(BF16)
    partial = jnp.dot(unit, weight, preferred_element_type=F32)
    width = weight.shape[1]
    start = (width + LANES - 1) // LANES * LANES
    info = jnp.concatenate([squares, misc[:, INFO : INFO + 3]], axis=1)
    sums = jnp.concatenate(
        [
            partial,
            jnp.zeros((rows, start - width), F32),
            info,
            jnp.zeros((rows, LANES - info.shape[1]), F32),
        ],
        axis=1,
    )

    def side(a, which):
        split = a.reshape(rows // seq_rows, 2, seq_rows // 2, -1)
        return lax.dynamic_index_in_dim(split, which, 1, False).reshape(rows // 2, -1)

    return side(sums, core), side(sums, 1 - core), side(residual.astype(F32), core)


def shards(
    ssm_input,
    gate_input,
    b_proj,
    readout_matrix,
    step_raw,
    step_bias,
    decay_log,
    head_skip_gain,
    norm_gain,
    out_weight,
    residual,
    final_gain,
    head_weight,
    mask_table,
    state_ids,
    targets,
):
    count = lax.axis_size("seq")
    rows, channels = ssm_input.shape
    features = 2 * channels
    small = count * rows <= LANES // 2
    swap = [(0, 1), (1, 0)]
    both = ("seq", "vocab")

    def exchange(a):
        if small:
            groups = circles(count)
            return lax.all_to_all(a, both, 0, 0, tiled=True, axis_index_groups=groups)
        return lax.all_to_all(a, "seq", 0, 0, tiled=True)

    packed = (pack if small else wide_pack)(
        count, ssm_input, gate_input, b_proj, readout_matrix, step_raw, step_bias, decay_log,
        head_skip_gain, state_ids, targets,
    )
    if small:
        depth = features // 4
        other_weight = tuple(
            lax.ppermute(head_weight[k * depth : (k + 1) * depth], "vocab", swap) for k in range(4)
        )
    else:
        other_weight = lax.ppermute(head_weight, "vocab", swap)
    other_mask = lax.ppermute(mask_table, "vocab", swap)
    gathered = lax.all_to_all(packed, "seq", 0, 0, tiled=True)
    final_gain = final_gain.reshape(count, features // count)
    norm_gain = norm_gain.reshape(1, channels)
    if small:
        gathered, other_weight, other_mask, final_gain = lax.optimization_barrier(
            (gathered, other_weight, other_mask, final_gain)
        )
    x = gathered.reshape(count * rows, packed.shape[2])
    mine, theirs, kept = (mixer if small else wide_mixer)(
        x, rows, step_bias.shape[0], norm_gain, out_weight, residual
    )
    arrived = lax.ppermute(theirs, "vocab", swap)
    if small:
        spread = hidden_rows(count, features, mine, arrived, kept)
    else:
        width = kept.shape[1]
        start = mine.shape[1] - LANES
        sums = mine + arrived
        scale = lax.rsqrt(sums[:, start : start + 1] / features + EPS)
        hidden = (kept + sums[:, 0:width] * scale).astype(BF16)
        spread = jnp.broadcast_to(hidden[None], (count,) + hidden.shape)
    full = exchange(spread)
    if small:
        stats = head(full, final_gain, head_weight, other_weight, mask_table, other_mask, mine)
    else:
        stats = wide_head(
            full, final_gain, head_weight, other_weight, mask_table, other_mask, mine
        )
    placed = exchange(stats)
    return combine(placed) if small else wide_combine(placed)


def wide_head(full, gain, own, other, own_mask, other_mask, info):
    count, rows, width = full.shape
    core = lax.axis_index("vocab")
    block = lax.axis_index("seq") * 2
    wide = full.transpose(1, 0, 2).reshape(rows, count * width).astype(F32)
    scale = lax.rsqrt(jnp.mean(wide * wide, axis=1, keepdims=True) + EPS)
    final = (wide * scale * gain.reshape(1, -1)).astype(BF16)
    start = info.shape[1] - LANES
    ids, upper, under = (info[:, start + k].astype(jnp.int32) for k in (1, 2, 3))
    target = upper * 256 + under
    entries = own.shape[1]
    logits, allowed, wanted = [], [], []
    for weight, table, which in ((own, own_mask, core), (other, other_mask, 1 - core)):
        logits.append(jnp.dot(final, weight, preferred_element_type=F32))
        column = (block + which) * entries + jnp.arange(entries, dtype=jnp.int32)
        wanted.append(column[None, :] == target[:, None])
        one_hot = (ids[:, None] == jnp.arange(table.shape[0])[None, :]).astype(BF16)
        chosen = jnp.dot(one_hot, (table == 1).astype(BF16), preferred_element_type=F32)
        allowed.append((chosen > 0.5) | wanted[-1])
    x, a, w = (jnp.concatenate(p, axis=1) for p in (logits, allowed, wanted))
    top = jnp.max(jnp.where(a, x, NEG), axis=1)
    total = jnp.sum(jnp.where(a, jnp.exp(x - top[:, None]), 0.0), axis=1)
    picked = jnp.sum(jnp.where(w, x, 0.0), axis=1)
    return jnp.stack([top, total, picked], axis=1).reshape(count, rows // count, 3)


def wide_combine(stats):
    top = jnp.max(stats[:, :, 0], axis=0)
    total = jnp.sum(stats[:, :, 1] * jnp.exp(stats[:, :, 0] - top[None, :]), axis=0)
    return jnp.log(total) + top - jnp.sum(stats[:, :, 2], axis=0)


def solution(mesh):
    placed = (
        P(("groups", "seq"), "vocab"),
        P(("groups", "seq"), "vocab"),
        P(("groups", "seq"), None),
        P(("groups", "seq"), None),
        P(("groups", "seq"), "vocab"),
        P("vocab"),
        P("vocab"),
        P("vocab"),
        P("vocab"),
        P("vocab", "seq"),
        P("groups", "seq"),
        P(),
        P(None, ("seq", "vocab")),
        P(None, ("seq", "vocab")),
        P(("groups", "seq")),
        P(("groups", "seq")),
    )
    return jax.shard_map(
        shards, mesh=mesh, in_specs=placed, out_specs=P(("groups", "seq", "vocab")), check_vma=False
    )
```

```python
import jax
import jax.numpy as jnp
from jax import lax
from jax.experimental import pallas as pl
from jax.experimental.pallas import tpu as pltpu
from jax.sharding import PartitionSpec as P

F32 = jnp.float32
BF16 = jnp.bfloat16
HIGHEST = lax.Precision.HIGHEST
EPS = 1e-05
LANES = 128
NEG = -1e30
INFO = 60
GAP = 32
PARAMS = 64
VMEM = pltpu.VMEM


def times_transposed(a, b):
    return lax.dot_general(a, b, (((1,), (1,)), ((), ())), preferred_element_type=F32)


def grant(mebibytes):
    return pltpu.CompilerParams(vmem_limit_bytes=mebibytes << 20)


def turn(seq):
    return seq % 2


def circles(count):
    return [[2 * s + (w + turn(s)) % 2 for s in range(count)] for w in range(2)]


def thirds(a):
    high = a.astype(BF16).astype(F32)
    middle = (a - high).astype(BF16).astype(F32)
    return high, middle, a - high - middle


def pack_kernel(
    ssm_ref, gate_ref, b_ref, c_ref, raw_ref, bias_ref, decay_ref, skip_ref, ids_ref, targets_ref,
    out_ref,
):
    count, rows, _ = out_ref.shape
    channels = ssm_ref.shape[1]
    state = b_ref.shape[1]
    heads = raw_ref.shape[1]
    edge = 2 * channels
    parts = list(thirds(jax.nn.softplus(raw_ref[...] + bias_ref[...])))
    row = lax.broadcasted_iota(jnp.int32, (rows, rows), 0)
    diagonal = row == lax.broadcasted_iota(jnp.int32, (rows, rows), 1)

    def upright(a):
        wide = jnp.broadcast_to(a.astype(F32), (rows, rows))
        return jnp.sum(jnp.where(diagonal, wide, 0.0), axis=1, keepdims=True)

    targets = upright(targets_ref[...])
    upper = jnp.floor(targets / 256.0)
    parts += [upright(ids_ref[...]), upper, targets - upper * 256.0]
    parts.append(jnp.zeros((rows, PARAMS - INFO - 3), F32))
    params = list(thirds(-jnp.exp(decay_ref[...]))) + list(thirds(skip_ref[...]))
    place = lax.broadcasted_iota(jnp.int32, (rows, heads), 0)
    table = jnp.zeros((rows, heads), F32)
    for k, part in enumerate(params):
        table = jnp.where(place == k, part, table)
    parts += [table, jnp.zeros((rows, LANES - PARAMS - heads), F32)]
    misc = jnp.concatenate(parts, axis=1).astype(BF16)
    for k in range(count):
        out_ref[k, :, 0:channels] = ssm_ref[...]
        out_ref[k, :, channels:edge] = gate_ref[...]
        out_ref[k, :, edge : edge + state] = b_ref[...]
        out_ref[k, :, edge + state : edge + 2 * state] = c_ref[...]
        out_ref[k, :, edge + 2 * state :] = misc


def pack(count, ssm, gate, b, c, raw, bias, decay, skip, ids, targets):
    rows, channels = ssm.shape
    heads = bias.shape[0]
    width = 2 * channels + 2 * b.shape[1] + LANES
    return pl.pallas_call(
        pack_kernel,
        out_shape=jax.ShapeDtypeStruct((count, rows, width), BF16),
        name="pack",
    )(
        ssm, gate, b, c, raw, bias.reshape(1, heads), decay.reshape(1, heads),
        skip.reshape(1, heads), ids.reshape(1, rows), targets.reshape(1, rows),
    )


def mixer_kernel(
    seq_rows, heads, x_ref, gain_ref, weight_ref, residual_ref,
    mine_ref, theirs_ref, kept_ref,
):
    mine = lax.axis_index("vocab") + turn(lax.axis_index("seq"))
    rows = x_ref.shape[0]
    channels = gain_ref.shape[1]
    state = (x_ref.shape[1] - LANES - 2 * channels) // 2
    edge = 2 * channels
    half = rows // 2
    size = channels // heads
    r64 = lax.broadcasted_iota(jnp.int32, (rows, rows), 0)
    c64 = lax.broadcasted_iota(jnp.int32, (rows, rows), 1)
    own = seq_rows // 2
    side = (r64 >= half).astype(jnp.int32)
    place = r64 - side * half
    seq = lax.shift_right_logical(place, own.bit_length() - 1)
    which = (mine + side + seq) & 1
    source = place + seq * own + which * own
    order = (c64 == source).astype(BF16)
    causal = c64 <= source
    moved = jnp.dot(order, x_ref[...], preferred_element_type=F32)

    misc = x_ref[:, edge + 2 * state :].astype(F32)
    step = misc[:, 0:heads] + misc[:, heads : 2 * heads] + misc[:, 2 * heads : 3 * heads]
    params = pltpu.roll(misc[0:8], LANES - PARAMS, 1)
    decay = params[0:1] + params[1:2] + params[2:3]
    gains = params[3:4] + params[4:5] + params[5:6]
    rates = jnp.concatenate(thirds(step * decay[:, 0:heads]), axis=1).astype(BF16)
    sums = jnp.concatenate([(c64 <= r64).astype(BF16), causal.astype(BF16)], axis=0)
    cums = jnp.dot(sums, rates, preferred_element_type=F32)
    cums = cums[:, 0:heads] + cums[:, heads : 2 * heads] + cums[:, 2 * heads :]
    middle = cums[half - 1 : half]
    ahead = jnp.exp(cums[rows:] - middle)
    back = jnp.exp(middle - cums[0:rows]) * step
    skips = jnp.broadcast_to(gains[:, 0:heads], (8, heads))
    factors = jnp.concatenate([ahead, back, skips], axis=0)
    factors = jnp.concatenate(thirds(factors), axis=1).astype(BF16)
    head_row = lax.broadcasted_iota(jnp.int32, (3 * heads, channels), 0)
    for _ in range(2):
        head_row = jnp.where(head_row >= heads, head_row - heads, head_row)
    from_head = lax.broadcasted_iota(jnp.int32, (3 * heads, channels), 1) - head_row * size
    spread = ((from_head >= 0) & (from_head < size)).astype(BF16)
    wide = jnp.dot(factors, spread, preferred_element_type=F32)

    c = moved[:, edge + state : edge + 2 * state].astype(BF16)
    corr = times_transposed(c, x_ref[:, edge : edge + state])
    corr = jnp.where(causal, corr, 0.0)
    high = corr.astype(BF16).astype(F32)
    corr = jnp.concatenate([high, corr - high, high], axis=1).astype(BF16)
    scaled = wide[rows : 2 * rows] * x_ref[:, 0:channels].astype(F32)
    high = scaled.astype(BF16)
    low = (scaled - high.astype(F32)).astype(BF16)
    y = jnp.dot(corr, jnp.concatenate([high, high, low], axis=0), preferred_element_type=F32)
    mixed = wide[0:rows] * y + wide[2 * rows : 2 * rows + 1] * moved[:, 0:channels]
    gate = moved[:, channels:edge]
    gated = (mixed * (gate / (1.0 + jnp.exp(-gate)))).astype(BF16).astype(F32)
    unit = (gated * gain_ref[...]).astype(BF16)
    partial = times_transposed(unit, weight_ref[...])
    total = jnp.sum(gated * gated, axis=1, keepdims=True)
    kept_ref[...] = jnp.dot(order[0:half], residual_ref[...], preferred_element_type=F32)

    lane = lax.broadcasted_iota(jnp.int32, (rows, LANES), 1)
    info = pltpu.roll(moved[:, edge + 2 * state :], LANES + 1 - INFO, 1)
    info = jnp.where(lane == 0, total, info)
    width = partial.shape[1]
    start = mine_ref.shape[1] - LANES
    mine_ref[:, 0:width] = partial[0:half]
    mine_ref[:, start:] = info[0:half]
    theirs_ref[:, 0:width] = partial[half:]
    theirs_ref[:, start:] = info[half:]


def mixer(x, seq_rows, heads, gain, weight, residual):
    rows = x.shape[0]
    channels = gain.shape[1]
    width = weight.shape[1]
    total = (width + LANES - 1) // LANES * LANES + LANES
    half = rows // 2
    sums = jax.ShapeDtypeStruct((half, total), F32)
    whole = pl.BlockSpec(memory_space=VMEM)

    def kernel(*refs):
        mixer_kernel(seq_rows, heads, *refs)

    return pl.pallas_call(
        kernel,
        out_shape=(sums, sums, jax.ShapeDtypeStruct((half, width), F32)),
        in_specs=[whole] * 4,
        compiler_params=grant(8),
        name="mixer",
    )(x, gain, weight.T, residual)


def hidden_kernel(features, mine_ref, theirs_ref, kept_ref, out_ref):
    count, half, _ = out_ref.shape
    width = kept_ref.shape[1]
    start = mine_ref.shape[1] - LANES
    squares = mine_ref[:, start : start + 1] + theirs_ref[:, start : start + 1]
    scale = lax.rsqrt(squares / features + EPS)
    sums = mine_ref[:, 0:width] + theirs_ref[:, 0:width]
    hidden = (kept_ref[...] + sums * scale).astype(BF16).astype(F32)
    paired = jnp.concatenate([hidden[0:half], hidden[half:]], axis=1).astype(BF16)
    for k in range(count):
        out_ref[k] = paired


def hidden_rows(count, features, mine, theirs, kept):
    def kernel(*refs):
        hidden_kernel(features, *refs)

    return pl.pallas_call(
        kernel,
        out_shape=jax.ShapeDtypeStruct((count, kept.shape[0] // 2, 2 * kept.shape[1]), BF16),
        compiler_params=grant(4),
        name="hidden",
    )(mine, theirs, kept)


def head_kernel(
    h_ref, gain_ref, own_ref, upper_ref, lower_ref, own_mask_ref, other_mask_ref, info_ref, out_ref
):
    core = lax.axis_index("vocab")
    block = lax.axis_index("seq") * 2
    count, half, width = h_ref.shape
    rows, width = 2 * half, width // 2
    features = count * width
    squares = jnp.zeros((rows, width), F32)
    parts = []
    for k in range(count):
        pair = h_ref[k].astype(F32)
        part = jnp.concatenate([pair[:, 0:width], pair[:, width:]], axis=0)
        parts.append(part)
        squares = squares + part * part
    scale = lax.rsqrt(jnp.sum(squares, axis=1, keepdims=True) / features + EPS)
    entries = own_ref.shape[0]
    parts = [parts[k] * scale * gain_ref[k : k + 1, :] for k in range(count)]
    final = jnp.concatenate(parts, axis=1).astype(BF16)
    logits = [times_transposed(final, own_ref[...])]
    depth = features // 2
    logits.append(
        times_transposed(final[:, :depth], upper_ref[...])
        + times_transposed(final[:, depth:], lower_ref[...])
    )
    states = own_mask_ref.shape[0]
    start = info_ref.shape[1] - LANES
    ids = info_ref[:, start + 1 : start + 2].astype(jnp.int32)
    upper = info_ref[:, start + 2 : start + 3].astype(jnp.int32)
    target = upper * 256 + info_ref[:, start + 3 : start + 4].astype(jnp.int32)
    pick_row = (lax.broadcasted_iota(jnp.int32, (rows, states), 1) == ids).astype(BF16)
    column = lax.broadcasted_iota(jnp.int32, (rows, entries), 1)
    allowed, wanted = [], []
    for ref, which in ((own_mask_ref, core), (other_mask_ref, 1 - core)):
        table = (ref[...] == 1).astype(F32).astype(BF16)
        chosen = jnp.dot(pick_row, table, preferred_element_type=F32)
        is_target = column + (block + which) * entries == target
        wanted.append(is_target)
        allowed.append((chosen > 0.5) | is_target)
    tops = [
        jnp.max(jnp.where(a, x, NEG), axis=1, keepdims=True) for a, x in zip(allowed, logits)
    ]
    top = jnp.maximum(tops[0], tops[1])
    total = jnp.zeros((rows, 1), F32)
    picked = jnp.zeros((rows, 1), F32)
    for a, w, x in zip(allowed, wanted, logits):
        total = total + jnp.sum(jnp.where(a, jnp.exp(x - top), 0.0), axis=1, keepdims=True)
        picked = picked + jnp.sum(jnp.where(w, x, 0.0), axis=1, keepdims=True)
    own = rows // count
    lane = lax.broadcasted_iota(jnp.int32, (rows, LANES), 1)
    place = lane - (lax.broadcasted_iota(jnp.int32, (rows, LANES), 0) & (own - 1))
    stats = jnp.where(
        place == 0, top, jnp.where(place == GAP, total, jnp.where(place == 2 * GAP, picked, 0.0))
    )
    for k in range(count):
        out_ref[k] = jnp.sum(stats[k * own : (k + 1) * own], axis=0, keepdims=True)


def head(h, gain, own, other, own_mask, other_mask, info):
    count, half, width = h.shape
    whole = pl.BlockSpec(memory_space=VMEM)
    return pl.pallas_call(
        head_kernel,
        out_shape=jax.ShapeDtypeStruct((count, 1, LANES), F32),
        in_specs=[whole] * 8,
        compiler_params=grant(12),
        name="head",
    )(h, gain, own.T, *(o.T for o in other), own_mask, other_mask, info)


def combine_kernel(stats_ref, out_ref):
    tops = stats_ref[:, 0, :]
    totals = pltpu.roll(tops, LANES - GAP, 1)
    picked = pltpu.roll(tops, LANES - 2 * GAP, 1)
    top = jnp.max(tops, axis=0, keepdims=True)
    total = jnp.sum(totals * jnp.exp(tops - top), axis=0, keepdims=True)
    losses = jnp.log(total) + top - jnp.sum(picked, axis=0, keepdims=True)
    out_ref[...] = losses[:, 0 : out_ref.shape[1]]


def combine(own, stats):
    out = pl.pallas_call(
        combine_kernel,
        out_shape=jax.ShapeDtypeStruct((1, own), F32),
        compiler_params=grant(2),
        name="combine",
    )(stats)
    return out.reshape(own)


def wide_pack(count, ssm, gate, b, c, raw, bias, decay, skip, ids, targets):
    rows = ssm.shape[0]
    heads = raw.shape[1]

    def split(a):
        high = lax.reduce_precision(a, 8, 7)
        middle = lax.reduce_precision(a - high, 8, 7)
        return [high, middle, a - high - middle]

    parts = split(jax.nn.softplus(raw + bias[None, :]))
    parts += [a.astype(F32)[:, None] for a in (ids, targets // 256, targets % 256)]
    parts.append(jnp.zeros((rows, PARAMS - INFO - 3), F32))
    params = jnp.stack(split(-jnp.exp(decay)) + split(skip))
    parts.append(jnp.pad(params, ((0, rows - 6), (0, LANES - PARAMS - heads))))
    misc = jnp.concatenate(parts, axis=1).astype(BF16)
    row = jnp.concatenate([ssm, gate, b, c, misc], axis=1)
    return jnp.broadcast_to(row[None], (count,) + row.shape)


def wide_mixer(x, seq_rows, heads, gain, weight, residual):
    rows = x.shape[0]
    channels = gain.shape[1]
    state = (x.shape[1] - LANES - 2 * channels) // 2
    edge = 2 * channels
    core = lax.axis_index("vocab")
    misc = x[:, edge + 2 * state :].astype(F32)
    step = misc[:, 0:heads] + misc[:, heads : 2 * heads] + misc[:, 2 * heads : 3 * heads]
    params = misc[0:8, PARAMS : PARAMS + heads]
    decay = params[0] + params[1] + params[2]
    skip = params[3] + params[4] + params[5]
    log_cum = jnp.cumsum(step * decay[None, :], axis=0)
    corr = jnp.dot(
        x[:, edge + state : edge + 2 * state],
        x[:, edge : edge + state].T,
        preferred_element_type=F32,
    )
    values = x[:, 0:channels].astype(F32).reshape(rows, heads, -1).transpose(1, 0, 2)
    causal = jnp.arange(rows)[:, None] >= jnp.arange(rows)[None, :]

    def one(inputs):
        cum, size, v = inputs
        weights = jnp.exp(jnp.where(causal, cum[:, None] - cum[None, :], NEG))
        return jnp.dot(weights * corr * size[None, :], v, precision=HIGHEST)

    y = lax.map(one, (log_cum.T, step.T, values))
    mixed = (y + skip[:, None, None] * values).transpose(1, 0, 2).reshape(rows, channels)
    gated = (mixed * jax.nn.silu(x[:, channels:edge].astype(F32))).astype(BF16)
    wide = gated.astype(F32)
    squares = jnp.sum(wide * wide, axis=1, keepdims=True)
    unit = (wide * gain).astype(BF16)
    partial = jnp.dot(unit, weight, preferred_element_type=F32)
    width = weight.shape[1]
    start = (width + LANES - 1) // LANES * LANES
    info = jnp.concatenate([squares, misc[:, INFO : INFO + 3]], axis=1)
    sums = jnp.concatenate(
        [
            partial,
            jnp.zeros((rows, start - width), F32),
            info,
            jnp.zeros((rows, LANES - info.shape[1]), F32),
        ],
        axis=1,
    )

    def side(a, which):
        split = a.reshape(rows // seq_rows, 2, seq_rows // 2, -1)
        return lax.dynamic_index_in_dim(split, which, 1, False).reshape(rows // 2, -1)

    return side(sums, core), side(sums, 1 - core), side(residual.astype(F32), core)


def shards(
    ssm_input,
    gate_input,
    b_proj,
    readout_matrix,
    step_raw,
    step_bias,
    decay_log,
    head_skip_gain,
    norm_gain,
    out_weight,
    residual,
    final_gain,
    head_weight,
    mask_table,
    state_ids,
    targets,
):
    count = lax.axis_size("seq")
    rows, channels = ssm_input.shape
    features = 2 * channels
    small = count * rows <= LANES // 2
    swap = [(0, 1), (1, 0)]
    both = ("seq", "vocab")

    def exchange(a):
        if small:
            groups = circles(count)
            return lax.all_to_all(a, both, 0, 0, tiled=True, axis_index_groups=groups)
        return lax.all_to_all(a, "seq", 0, 0, tiled=True)

    packed = (pack if small else wide_pack)(
        count, ssm_input, gate_input, b_proj, readout_matrix, step_raw, step_bias, decay_log,
        head_skip_gain, state_ids, targets,
    )
    if small:
        depth = features // 2
        other_weight = tuple(
            lax.ppermute(head_weight[k * depth : (k + 1) * depth], "vocab", swap) for k in range(2)
        )
    else:
        other_weight = lax.ppermute(head_weight, "vocab", swap)
    other_mask = lax.ppermute(mask_table, "vocab", swap)
    gathered = lax.all_to_all(packed, "seq", 0, 0, tiled=True)
    final_gain = final_gain.reshape(count, features // count)
    norm_gain = norm_gain.reshape(1, channels)
    if small:
        gathered, other_weight, other_mask, final_gain = lax.optimization_barrier(
            (gathered, other_weight, other_mask, final_gain)
        )
    x = gathered.reshape(count * rows, packed.shape[2])
    mine, theirs, kept = (mixer if small else wide_mixer)(
        x, rows, step_bias.shape[0], norm_gain, out_weight, residual
    )
    arrived = lax.ppermute(theirs, "vocab", swap)
    if small:
        spread = hidden_rows(count, features, mine, arrived, kept)
    else:
        width = kept.shape[1]
        start = mine.shape[1] - LANES
        sums = mine + arrived
        scale = lax.rsqrt(sums[:, start : start + 1] / features + EPS)
        hidden = (kept + sums[:, 0:width] * scale).astype(BF16)
        spread = jnp.broadcast_to(hidden[None], (count,) + hidden.shape)
    full = exchange(spread)
    if small:
        stats = head(full, final_gain, head_weight, other_weight, mask_table, other_mask, mine)
    else:
        stats = wide_head(
            full, final_gain, head_weight, other_weight, mask_table, other_mask, mine
        )
    placed = exchange(stats)
    return combine(rows // 2, placed) if small else wide_combine(placed)


def wide_head(full, gain, own, other, own_mask, other_mask, info):
    count, rows, width = full.shape
    core = lax.axis_index("vocab")
    block = lax.axis_index("seq") * 2
    wide = full.transpose(1, 0, 2).reshape(rows, count * width).astype(F32)
    scale = lax.rsqrt(jnp.mean(wide * wide, axis=1, keepdims=True) + EPS)
    final = (wide * scale * gain.reshape(1, -1)).astype(BF16)
    start = info.shape[1] - LANES
    ids, upper, under = (info[:, start + k].astype(jnp.int32) for k in (1, 2, 3))
    target = upper * 256 + under
    entries = own.shape[1]
    logits, allowed, wanted = [], [], []
    for weight, table, which in ((own, own_mask, core), (other, other_mask, 1 - core)):
        logits.append(jnp.dot(final, weight, preferred_element_type=F32))
        column = (block + which) * entries + jnp.arange(entries, dtype=jnp.int32)
        wanted.append(column[None, :] == target[:, None])
        one_hot = (ids[:, None] == jnp.arange(table.shape[0])[None, :]).astype(BF16)
        chosen = jnp.dot(one_hot, (table == 1).astype(BF16), preferred_element_type=F32)
        allowed.append((chosen > 0.5) | wanted[-1])
    x, a, w = (jnp.concatenate(p, axis=1) for p in (logits, allowed, wanted))
    top = jnp.max(jnp.where(a, x, NEG), axis=1)
    total = jnp.sum(jnp.where(a, jnp.exp(x - top[:, None]), 0.0), axis=1)
    picked = jnp.sum(jnp.where(w, x, 0.0), axis=1)
    return jnp.stack([top, total, picked], axis=1).reshape(count, rows // count, 3)


def wide_combine(stats):
    top = jnp.max(stats[:, :, 0], axis=0)
    total = jnp.sum(stats[:, :, 1] * jnp.exp(stats[:, :, 0] - top[None, :]), axis=0)
    return jnp.log(total) + top - jnp.sum(stats[:, :, 2], axis=0)


def solution(mesh):
    placed = (
        P(("groups", "seq"), "vocab"),
        P(("groups", "seq"), "vocab"),
        P(("groups", "seq"), None),
        P(("groups", "seq"), None),
        P(("groups", "seq"), "vocab"),
        P("vocab"),
        P("vocab"),
        P("vocab"),
        P("vocab"),
        P("vocab", "seq"),
        P("groups", "seq"),
        P(),
        P(None, ("seq", "vocab")),
        P(None, ("seq", "vocab")),
        P(("groups", "seq")),
        P(("groups", "seq")),
    )
    return jax.shard_map(
        shards, mesh=mesh, in_specs=placed, out_specs=P(("groups", "seq", "vocab")), check_vma=False
    )
```

```python
import jax
import jax.numpy as jnp
from jax import lax
from jax.experimental import pallas as pl
from jax.experimental.pallas import tpu as pltpu
from jax.sharding import PartitionSpec as P

F32 = jnp.float32
BF16 = jnp.bfloat16
HIGHEST = lax.Precision.HIGHEST
EPS = 1e-05
LANES = 128
NEG = -1e30
INFO = 60
GAP = 32
PARAMS = 64
VMEM = pltpu.VMEM


def times_transposed(a, b):
    return lax.dot_general(a, b, (((1,), (1,)), ((), ())), preferred_element_type=F32)


def grant(mebibytes):
    return pltpu.CompilerParams(vmem_limit_bytes=mebibytes << 20)


def turn(seq):
    return seq % 2


def circles(count):
    return [[2 * s + (w + turn(s)) % 2 for s in range(count)] for w in range(2)]


def thirds(a):
    high = a.astype(BF16).astype(F32)
    middle = (a - high).astype(BF16).astype(F32)
    return high, middle, a - high - middle


def pack_kernel(
    ssm_ref, gate_ref, b_ref, c_ref, raw_ref, bias_ref, decay_ref, skip_ref, ids_ref, targets_ref,
    out_ref,
):
    count, rows, _ = out_ref.shape
    channels = ssm_ref.shape[1]
    state = b_ref.shape[1]
    heads = raw_ref.shape[1]
    edge = 2 * channels
    parts = list(thirds(jax.nn.softplus(raw_ref[...] + bias_ref[...])))
    row = lax.broadcasted_iota(jnp.int32, (rows, rows), 0)
    diagonal = row == lax.broadcasted_iota(jnp.int32, (rows, rows), 1)

    def upright(a):
        wide = jnp.broadcast_to(a.astype(F32), (rows, rows))
        return jnp.sum(jnp.where(diagonal, wide, 0.0), axis=1, keepdims=True)

    targets = upright(targets_ref[...])
    upper = jnp.floor(targets / 256.0)
    parts += [upright(ids_ref[...]), upper, targets - upper * 256.0]
    parts.append(jnp.zeros((rows, PARAMS - INFO - 3), F32))
    params = list(thirds(-jnp.exp(decay_ref[...]))) + list(thirds(skip_ref[...]))
    place = lax.broadcasted_iota(jnp.int32, (rows, heads), 0)
    table = jnp.zeros((rows, heads), F32)
    for k, part in enumerate(params):
        table = jnp.where(place == k, part, table)
    parts += [table, jnp.zeros((rows, LANES - PARAMS - heads), F32)]
    misc = jnp.concatenate(parts, axis=1).astype(BF16)
    for k in range(count):
        out_ref[k, :, 0:channels] = ssm_ref[...]
        out_ref[k, :, channels:edge] = gate_ref[...]
        out_ref[k, :, edge : edge + state] = b_ref[...]
        out_ref[k, :, edge + state : edge + 2 * state] = c_ref[...]
        out_ref[k, :, edge + 2 * state :] = misc


def pack(count, ssm, gate, b, c, raw, bias, decay, skip, ids, targets):
    rows, channels = ssm.shape
    heads = bias.shape[0]
    width = 2 * channels + 2 * b.shape[1] + LANES
    return pl.pallas_call(
        pack_kernel,
        out_shape=jax.ShapeDtypeStruct((count, rows, width), BF16),
        name="pack",
    )(
        ssm, gate, b, c, raw, bias.reshape(1, heads), decay.reshape(1, heads),
        skip.reshape(1, heads), ids.reshape(1, rows), targets.reshape(1, rows),
    )


def mixer_kernel(
    seq_rows, heads, x_ref, gain_ref, weight_ref, residual_ref,
    mine_ref, theirs_ref, kept_ref,
):
    mine = lax.axis_index("vocab") + turn(lax.axis_index("seq"))
    rows = x_ref.shape[0]
    channels = gain_ref.shape[1]
    state = (x_ref.shape[1] - LANES - 2 * channels) // 2
    edge = 2 * channels
    half = rows // 2
    size = channels // heads
    r64 = lax.broadcasted_iota(jnp.int32, (rows, rows), 0)
    c64 = lax.broadcasted_iota(jnp.int32, (rows, rows), 1)
    own = seq_rows // 2
    side = (r64 >= half).astype(jnp.int32)
    place = r64 - side * half
    seq = lax.shift_right_logical(place, own.bit_length() - 1)
    which = (mine + side + seq) & 1
    source = place + seq * own + which * own
    order = (c64 == source).astype(BF16)
    causal = c64 <= source
    moved = jnp.dot(order, x_ref[...], preferred_element_type=F32)

    misc = x_ref[:, edge + 2 * state :].astype(F32)
    step = misc[:, 0:heads] + misc[:, heads : 2 * heads] + misc[:, 2 * heads : 3 * heads]
    params = pltpu.roll(misc[0:8], LANES - PARAMS, 1)
    decay = params[0:1] + params[1:2] + params[2:3]
    gains = params[3:4] + params[4:5] + params[5:6]
    rates = jnp.concatenate(thirds(step * decay[:, 0:heads]), axis=1).astype(BF16)
    sums = jnp.concatenate([(c64 <= r64).astype(BF16), causal.astype(BF16)], axis=0)
    cums = jnp.dot(sums, rates, preferred_element_type=F32)
    cums = cums[:, 0:heads] + cums[:, heads : 2 * heads] + cums[:, 2 * heads :]
    middle = cums[half - 1 : half]
    ahead = jnp.exp(cums[rows:] - middle)
    back = jnp.exp(middle - cums[0:rows]) * step
    skips = jnp.broadcast_to(gains[:, 0:heads], (8, heads))
    factors = jnp.concatenate([ahead, back, skips], axis=0)
    factors = jnp.concatenate(thirds(factors), axis=1).astype(BF16)
    head_row = lax.broadcasted_iota(jnp.int32, (3 * heads, channels), 0)
    for _ in range(2):
        head_row = jnp.where(head_row >= heads, head_row - heads, head_row)
    from_head = lax.broadcasted_iota(jnp.int32, (3 * heads, channels), 1) - head_row * size
    spread = ((from_head >= 0) & (from_head < size)).astype(BF16)
    wide = jnp.dot(factors, spread, preferred_element_type=F32)

    c = moved[:, edge + state : edge + 2 * state].astype(BF16)
    corr = times_transposed(c, x_ref[:, edge : edge + state])
    corr = jnp.where(causal, corr, 0.0)
    high = corr.astype(BF16).astype(F32)
    corr = jnp.concatenate([high, corr - high, high], axis=1).astype(BF16)
    scaled = wide[rows : 2 * rows] * x_ref[:, 0:channels].astype(F32)
    high = scaled.astype(BF16)
    low = (scaled - high.astype(F32)).astype(BF16)
    y = jnp.dot(corr, jnp.concatenate([high, high, low], axis=0), preferred_element_type=F32)
    mixed = wide[0:rows] * y + wide[2 * rows : 2 * rows + 1] * moved[:, 0:channels]
    gate = moved[:, channels:edge]
    gated = (mixed * (gate / (1.0 + jnp.exp(-gate)))).astype(BF16).astype(F32)
    unit = gated * gain_ref[...]
    high = unit.astype(BF16)
    low = (unit - high.astype(F32)).astype(BF16)
    partial = times_transposed(jnp.concatenate([high, low], axis=0), weight_ref[...])
    partial = partial[0:rows] + partial[rows:]
    total = jnp.sum(gated * gated, axis=1, keepdims=True)
    kept_ref[...] = jnp.dot(order[0:half], residual_ref[...], preferred_element_type=F32)

    lane = lax.broadcasted_iota(jnp.int32, (rows, LANES), 1)
    info = pltpu.roll(moved[:, edge + 2 * state :], LANES + 1 - INFO, 1)
    info = jnp.where(lane == 0, total, info)
    width = partial.shape[1]
    start = mine_ref.shape[1] - LANES
    mine_ref[:, 0:width] = partial[0:half]
    mine_ref[:, start:] = info[0:half]
    theirs_ref[:, 0:width] = partial[half:]
    theirs_ref[:, start:] = info[half:]


def mixer(x, seq_rows, heads, gain, weight, residual):
    rows = x.shape[0]
    channels = gain.shape[1]
    width = weight.shape[1]
    total = (width + LANES - 1) // LANES * LANES + LANES
    half = rows // 2
    sums = jax.ShapeDtypeStruct((half, total), F32)
    whole = pl.BlockSpec(memory_space=VMEM)

    def kernel(*refs):
        mixer_kernel(seq_rows, heads, *refs)

    return pl.pallas_call(
        kernel,
        out_shape=(sums, sums, jax.ShapeDtypeStruct((half, width), F32)),
        in_specs=[whole] * 4,
        compiler_params=grant(8),
        name="mixer",
    )(x, gain, weight.T, residual)


def hidden_kernel(features, mine_ref, theirs_ref, kept_ref, out_ref):
    count, half, _ = out_ref.shape
    width = kept_ref.shape[1]
    start = mine_ref.shape[1] - LANES
    squares = mine_ref[:, start : start + 1] + theirs_ref[:, start : start + 1]
    scale = lax.rsqrt(squares / features + EPS)
    sums = mine_ref[:, 0:width] + theirs_ref[:, 0:width]
    hidden = (kept_ref[...] + sums * scale).astype(BF16).astype(F32)
    paired = jnp.concatenate([hidden[0:half], hidden[half:]], axis=1).astype(BF16)
    for k in range(count):
        out_ref[k] = paired


def hidden_rows(count, features, mine, theirs, kept):
    def kernel(*refs):
        hidden_kernel(features, *refs)

    return pl.pallas_call(
        kernel,
        out_shape=jax.ShapeDtypeStruct((count, kept.shape[0] // 2, 2 * kept.shape[1]), BF16),
        compiler_params=grant(4),
        name="hidden",
    )(mine, theirs, kept)


def head_kernel(
    h_ref, gain_ref, own_ref, upper_ref, lower_ref, own_mask_ref, other_mask_ref, info_ref, out_ref
):
    core = lax.axis_index("vocab")
    block = lax.axis_index("seq") * 2
    count, half, width = h_ref.shape
    rows, width = 2 * half, width // 2
    features = count * width
    squares = jnp.zeros((rows, width), F32)
    parts = []
    for k in range(count):
        pair = h_ref[k].astype(F32)
        part = jnp.concatenate([pair[:, 0:width], pair[:, width:]], axis=0)
        parts.append(part)
        squares = squares + part * part
    scale = lax.rsqrt(jnp.sum(squares, axis=1, keepdims=True) / features + EPS)
    entries = own_ref.shape[0]
    parts = [parts[k] * scale * gain_ref[k : k + 1, :] for k in range(count)]
    final = jnp.concatenate(parts, axis=1).astype(BF16)
    logits = [times_transposed(final, own_ref[...])]
    depth = features // 2
    logits.append(
        times_transposed(final[:, :depth], upper_ref[...])
        + times_transposed(final[:, depth:], lower_ref[...])
    )
    states = own_mask_ref.shape[0]
    start = info_ref.shape[1] - LANES
    ids = info_ref[:, start + 1 : start + 2].astype(jnp.int32)
    upper = info_ref[:, start + 2 : start + 3].astype(jnp.int32)
    target = upper * 256 + info_ref[:, start + 3 : start + 4].astype(jnp.int32)
    pick_row = (lax.broadcasted_iota(jnp.int32, (rows, states), 1) == ids).astype(BF16)
    column = lax.broadcasted_iota(jnp.int32, (rows, entries), 1)
    allowed, wanted = [], []
    for ref, which in ((own_mask_ref, core), (other_mask_ref, 1 - core)):
        table = (ref[...] == 1).astype(F32).astype(BF16)
        chosen = jnp.dot(pick_row, table, preferred_element_type=F32)
        is_target = column + (block + which) * entries == target
        wanted.append(is_target)
        allowed.append((chosen > 0.5) | is_target)
    tops = [
        jnp.max(jnp.where(a, x, NEG), axis=1, keepdims=True) for a, x in zip(allowed, logits)
    ]
    top = jnp.maximum(tops[0], tops[1])
    total = jnp.zeros((rows, 1), F32)
    picked = jnp.zeros((rows, 1), F32)
    for a, w, x in zip(allowed, wanted, logits):
        total = total + jnp.sum(jnp.where(a, jnp.exp(x - top), 0.0), axis=1, keepdims=True)
        picked = picked + jnp.sum(jnp.where(w, x, 0.0), axis=1, keepdims=True)
    own = rows // count
    lane = lax.broadcasted_iota(jnp.int32, (rows, LANES), 1)
    place = lane - (lax.broadcasted_iota(jnp.int32, (rows, LANES), 0) & (own - 1))
    stats = jnp.where(
        place == 0, top, jnp.where(place == GAP, total, jnp.where(place == 2 * GAP, picked, 0.0))
    )
    for k in range(count):
        out_ref[k] = jnp.sum(stats[k * own : (k + 1) * own], axis=0, keepdims=True)


def head(h, gain, own, other, own_mask, other_mask, info):
    count, half, width = h.shape
    whole = pl.BlockSpec(memory_space=VMEM)
    return pl.pallas_call(
        head_kernel,
        out_shape=jax.ShapeDtypeStruct((count, 1, LANES), F32),
        in_specs=[whole] * 8,
        compiler_params=grant(12),
        name="head",
    )(h, gain, own.T, *(o.T for o in other), own_mask, other_mask, info)


def combine_kernel(stats_ref, out_ref):
    tops = stats_ref[:, 0, :]
    totals = pltpu.roll(tops, LANES - GAP, 1)
    picked = pltpu.roll(tops, LANES - 2 * GAP, 1)
    top = jnp.max(tops, axis=0, keepdims=True)
    total = jnp.sum(totals * jnp.exp(tops - top), axis=0, keepdims=True)
    losses = jnp.log(total) + top - jnp.sum(picked, axis=0, keepdims=True)
    out_ref[...] = losses[:, 0 : out_ref.shape[1]]


def combine(own, stats):
    out = pl.pallas_call(
        combine_kernel,
        out_shape=jax.ShapeDtypeStruct((1, own), F32),
        compiler_params=grant(2),
        name="combine",
    )(stats)
    return out.reshape(own)


def wide_pack(count, ssm, gate, b, c, raw, bias, decay, skip, ids, targets):
    rows = ssm.shape[0]
    heads = raw.shape[1]

    def split(a):
        high = lax.reduce_precision(a, 8, 7)
        middle = lax.reduce_precision(a - high, 8, 7)
        return [high, middle, a - high - middle]

    parts = split(jax.nn.softplus(raw + bias[None, :]))
    parts += [a.astype(F32)[:, None] for a in (ids, targets // 256, targets % 256)]
    parts.append(jnp.zeros((rows, PARAMS - INFO - 3), F32))
    params = jnp.stack(split(-jnp.exp(decay)) + split(skip))
    parts.append(jnp.pad(params, ((0, rows - 6), (0, LANES - PARAMS - heads))))
    misc = jnp.concatenate(parts, axis=1).astype(BF16)
    row = jnp.concatenate([ssm, gate, b, c, misc], axis=1)
    return jnp.broadcast_to(row[None], (count,) + row.shape)


def wide_mixer(x, seq_rows, heads, gain, weight, residual):
    rows = x.shape[0]
    channels = gain.shape[1]
    state = (x.shape[1] - LANES - 2 * channels) // 2
    edge = 2 * channels
    core = lax.axis_index("vocab")
    misc = x[:, edge + 2 * state :].astype(F32)
    step = misc[:, 0:heads] + misc[:, heads : 2 * heads] + misc[:, 2 * heads : 3 * heads]
    params = misc[0:8, PARAMS : PARAMS + heads]
    decay = params[0] + params[1] + params[2]
    skip = params[3] + params[4] + params[5]
    log_cum = jnp.cumsum(step * decay[None, :], axis=0)
    corr = jnp.dot(
        x[:, edge + state : edge + 2 * state],
        x[:, edge : edge + state].T,
        preferred_element_type=F32,
    )
    values = x[:, 0:channels].astype(F32).reshape(rows, heads, -1).transpose(1, 0, 2)
    causal = jnp.arange(rows)[:, None] >= jnp.arange(rows)[None, :]

    def one(inputs):
        cum, size, v = inputs
        weights = jnp.exp(jnp.where(causal, cum[:, None] - cum[None, :], NEG))
        return jnp.dot(weights * corr * size[None, :], v, precision=HIGHEST)

    y = lax.map(one, (log_cum.T, step.T, values))
    mixed = (y + skip[:, None, None] * values).transpose(1, 0, 2).reshape(rows, channels)
    gated = (mixed * jax.nn.silu(x[:, channels:edge].astype(F32))).astype(BF16)
    wide = gated.astype(F32)
    squares = jnp.sum(wide * wide, axis=1, keepdims=True)
    unit = wide * gain
    high = lax.reduce_precision(unit, 8, 7)
    partial = jnp.dot(high.astype(BF16), weight, preferred_element_type=F32)
    low = (unit - high).astype(BF16)
    partial = partial + jnp.dot(low, weight, preferred_element_type=F32)
    width = weight.shape[1]
    start = (width + LANES - 1) // LANES * LANES
    info = jnp.concatenate([squares, misc[:, INFO : INFO + 3]], axis=1)
    sums = jnp.concatenate(
        [
            partial,
            jnp.zeros((rows, start - width), F32),
            info,
            jnp.zeros((rows, LANES - info.shape[1]), F32),
        ],
        axis=1,
    )

    def side(a, which):
        split = a.reshape(rows // seq_rows, 2, seq_rows // 2, -1)
        return lax.dynamic_index_in_dim(split, which, 1, False).reshape(rows // 2, -1)

    return side(sums, core), side(sums, 1 - core), side(residual.astype(F32), core)


def shards(
    ssm_input,
    gate_input,
    b_proj,
    readout_matrix,
    step_raw,
    step_bias,
    decay_log,
    head_skip_gain,
    norm_gain,
    out_weight,
    residual,
    final_gain,
    head_weight,
    mask_table,
    state_ids,
    targets,
):
    count = lax.axis_size("seq")
    rows, channels = ssm_input.shape
    features = 2 * channels
    small = count * rows <= LANES // 2
    swap = [(0, 1), (1, 0)]
    both = ("seq", "vocab")

    def exchange(a):
        if small:
            groups = circles(count)
            return lax.all_to_all(a, both, 0, 0, tiled=True, axis_index_groups=groups)
        return lax.all_to_all(a, "seq", 0, 0, tiled=True)

    packed = (pack if small else wide_pack)(
        count, ssm_input, gate_input, b_proj, readout_matrix, step_raw, step_bias, decay_log,
        head_skip_gain, state_ids, targets,
    )
    if small:
        depth = features // 2
        other_weight = tuple(
            lax.ppermute(head_weight[k * depth : (k + 1) * depth], "vocab", swap) for k in range(2)
        )
    else:
        other_weight = lax.ppermute(head_weight, "vocab", swap)
    other_mask = lax.ppermute(mask_table, "vocab", swap)
    gathered = lax.all_to_all(packed, "seq", 0, 0, tiled=True)
    final_gain = final_gain.reshape(count, features // count)
    norm_gain = norm_gain.reshape(1, channels)
    if small:
        gathered, other_weight, other_mask, final_gain = lax.optimization_barrier(
            (gathered, other_weight, other_mask, final_gain)
        )
    x = gathered.reshape(count * rows, packed.shape[2])
    mine, theirs, kept = (mixer if small else wide_mixer)(
        x, rows, step_bias.shape[0], norm_gain, out_weight, residual
    )
    arrived = lax.ppermute(theirs, "vocab", swap)
    if small:
        spread = hidden_rows(count, features, mine, arrived, kept)
    else:
        width = kept.shape[1]
        start = mine.shape[1] - LANES
        sums = mine + arrived
        scale = lax.rsqrt(sums[:, start : start + 1] / features + EPS)
        hidden = (kept + sums[:, 0:width] * scale).astype(BF16)
        spread = jnp.broadcast_to(hidden[None], (count,) + hidden.shape)
    full = exchange(spread)
    if small:
        stats = head(full, final_gain, head_weight, other_weight, mask_table, other_mask, mine)
    else:
        stats = wide_head(
            full, final_gain, head_weight, other_weight, mask_table, other_mask, mine
        )
    placed = exchange(stats)
    return combine(rows // 2, placed) if small else wide_combine(placed)


def wide_head(full, gain, own, other, own_mask, other_mask, info):
    count, rows, width = full.shape
    core = lax.axis_index("vocab")
    block = lax.axis_index("seq") * 2
    wide = full.transpose(1, 0, 2).reshape(rows, count * width).astype(F32)
    scale = lax.rsqrt(jnp.mean(wide * wide, axis=1, keepdims=True) + EPS)
    final = (wide * scale * gain.reshape(1, -1)).astype(BF16)
    start = info.shape[1] - LANES
    ids, upper, under = (info[:, start + k].astype(jnp.int32) for k in (1, 2, 3))
    target = upper * 256 + under
    entries = own.shape[1]
    logits, allowed, wanted = [], [], []
    for weight, table, which in ((own, own_mask, core), (other, other_mask, 1 - core)):
        logits.append(jnp.dot(final, weight, preferred_element_type=F32))
        column = (block + which) * entries + jnp.arange(entries, dtype=jnp.int32)
        wanted.append(column[None, :] == target[:, None])
        one_hot = (ids[:, None] == jnp.arange(table.shape[0])[None, :]).astype(BF16)
        chosen = jnp.dot(one_hot, (table == 1).astype(BF16), preferred_element_type=F32)
        allowed.append((chosen > 0.5) | wanted[-1])
    x, a, w = (jnp.concatenate(p, axis=1) for p in (logits, allowed, wanted))
    top = jnp.max(jnp.where(a, x, NEG), axis=1)
    total = jnp.sum(jnp.where(a, jnp.exp(x - top[:, None]), 0.0), axis=1)
    picked = jnp.sum(jnp.where(w, x, 0.0), axis=1)
    return jnp.stack([top, total, picked], axis=1).reshape(count, rows // count, 3)


def wide_combine(stats):
    top = jnp.max(stats[:, :, 0], axis=0)
    total = jnp.sum(stats[:, :, 1] * jnp.exp(stats[:, :, 0] - top[None, :]), axis=0)
    return jnp.log(total) + top - jnp.sum(stats[:, :, 2], axis=0)


def solution(mesh):
    placed = (
        P(("groups", "seq"), "vocab"),
        P(("groups", "seq"), "vocab"),
        P(("groups", "seq"), None),
        P(("groups", "seq"), None),
        P(("groups", "seq"), "vocab"),
        P("vocab"),
        P("vocab"),
        P("vocab"),
        P("vocab"),
        P("vocab", "seq"),
        P("groups", "seq"),
        P(),
        P(None, ("seq", "vocab")),
        P(None, ("seq", "vocab")),
        P(("groups", "seq")),
        P(("groups", "seq")),
    )
    return jax.shard_map(
        shards, mesh=mesh, in_specs=placed, out_specs=P(("groups", "seq", "vocab")), check_vma=False
    )
```

```python
import jax
import jax.numpy as jnp
from jax import lax
from jax.experimental import pallas as pl
from jax.experimental.pallas import tpu as pltpu
from jax.sharding import PartitionSpec as P

F32 = jnp.float32
BF16 = jnp.bfloat16
HIGHEST = lax.Precision.HIGHEST
EPS = 1e-05
LANES = 128
NEG = -1e30
INFO = 60
GAP = 32
PARAMS = 64
VMEM = pltpu.VMEM


def times_transposed(a, b):
    return lax.dot_general(a, b, (((1,), (1,)), ((), ())), preferred_element_type=F32)


def grant(mebibytes):
    return pltpu.CompilerParams(vmem_limit_bytes=mebibytes << 20)


def turn(seq):
    return seq // 4


def circles(count):
    return [[2 * s + (w + turn(s)) % 2 for s in range(count)] for w in range(2)]


def thirds(a):
    high = a.astype(BF16).astype(F32)
    middle = (a - high).astype(BF16).astype(F32)
    return high, middle, a - high - middle


def pack_kernel(
    ssm_ref, gate_ref, b_ref, c_ref, raw_ref, bias_ref, decay_ref, skip_ref, ids_ref, targets_ref,
    out_ref,
):
    count, rows, _ = out_ref.shape
    channels = ssm_ref.shape[1]
    state = b_ref.shape[1]
    heads = raw_ref.shape[1]
    edge = 2 * channels
    parts = list(thirds(jax.nn.softplus(raw_ref[...] + bias_ref[...])))
    row = lax.broadcasted_iota(jnp.int32, (rows, rows), 0)
    diagonal = row == lax.broadcasted_iota(jnp.int32, (rows, rows), 1)

    def upright(a):
        wide = jnp.broadcast_to(a.astype(F32), (rows, rows))
        return jnp.sum(jnp.where(diagonal, wide, 0.0), axis=1, keepdims=True)

    targets = upright(targets_ref[...])
    upper = jnp.floor(targets / 256.0)
    parts += [upright(ids_ref[...]), upper, targets - upper * 256.0]
    parts.append(jnp.zeros((rows, PARAMS - INFO - 3), F32))
    params = list(thirds(-jnp.exp(decay_ref[...]))) + list(thirds(skip_ref[...]))
    place = lax.broadcasted_iota(jnp.int32, (rows, heads), 0)
    table = jnp.zeros((rows, heads), F32)
    for k, part in enumerate(params):
        table = jnp.where(place == k, part, table)
    parts += [table, jnp.zeros((rows, LANES - PARAMS - heads), F32)]
    misc = jnp.concatenate(parts, axis=1).astype(BF16)
    for k in range(count):
        out_ref[k, :, 0:channels] = ssm_ref[...]
        out_ref[k, :, channels:edge] = gate_ref[...]
        out_ref[k, :, edge : edge + state] = b_ref[...]
        out_ref[k, :, edge + state : edge + 2 * state] = c_ref[...]
        out_ref[k, :, edge + 2 * state :] = misc


def pack(count, ssm, gate, b, c, raw, bias, decay, skip, ids, targets):
    rows, channels = ssm.shape
    heads = bias.shape[0]
    width = 2 * channels + 2 * b.shape[1] + LANES
    return pl.pallas_call(
        pack_kernel,
        out_shape=jax.ShapeDtypeStruct((count, rows, width), BF16),
        name="pack",
    )(
        ssm, gate, b, c, raw, bias.reshape(1, heads), decay.reshape(1, heads),
        skip.reshape(1, heads), ids.reshape(1, rows), targets.reshape(1, rows),
    )


def mixer_kernel(
    seq_rows, heads, x_ref, gain_ref, weight_ref, residual_ref,
    mine_ref, theirs_ref, kept_ref,
):
    mine = lax.axis_index("vocab") + turn(lax.axis_index("seq"))
    rows = x_ref.shape[0]
    channels = gain_ref.shape[1]
    state = (x_ref.shape[1] - LANES - 2 * channels) // 2
    edge = 2 * channels
    half = rows // 2
    size = channels // heads
    r64 = lax.broadcasted_iota(jnp.int32, (rows, rows), 0)
    c64 = lax.broadcasted_iota(jnp.int32, (rows, rows), 1)
    own = seq_rows // 2
    side = (r64 >= half).astype(jnp.int32)
    place = r64 - side * half
    seq = lax.shift_right_logical(place, own.bit_length() - 1)
    which = (mine + side + lax.shift_right_logical(seq, 2)) & 1
    source = place + seq * own + which * own
    order = (c64 == source).astype(BF16)
    causal = c64 <= source
    moved = jnp.dot(order, x_ref[...], preferred_element_type=F32)

    misc = x_ref[:, edge + 2 * state :].astype(F32)
    step = misc[:, 0:heads] + misc[:, heads : 2 * heads] + misc[:, 2 * heads : 3 * heads]
    params = pltpu.roll(misc[0:8], LANES - PARAMS, 1)
    decay = params[0:1] + params[1:2] + params[2:3]
    gains = params[3:4] + params[4:5] + params[5:6]
    rates = jnp.concatenate(thirds(step * decay[:, 0:heads]), axis=1).astype(BF16)
    sums = jnp.concatenate([(c64 <= r64).astype(BF16), causal.astype(BF16)], axis=0)
    cums = jnp.dot(sums, rates, preferred_element_type=F32)
    cums = cums[:, 0:heads] + cums[:, heads : 2 * heads] + cums[:, 2 * heads :]
    middle = cums[half - 1 : half]
    ahead = jnp.exp(cums[rows:] - middle)
    back = jnp.exp(middle - cums[0:rows]) * step
    skips = jnp.broadcast_to(gains[:, 0:heads], (8, heads))
    factors = jnp.concatenate([ahead, back, skips], axis=0)
    high = factors.astype(BF16).astype(F32)
    factors = jnp.concatenate([high, factors - high], axis=1).astype(BF16)
    head_row = lax.broadcasted_iota(jnp.int32, (2 * heads, channels), 0)
    head_row = jnp.where(head_row >= heads, head_row - heads, head_row)
    from_head = lax.broadcasted_iota(jnp.int32, (2 * heads, channels), 1) - head_row * size
    spread = ((from_head >= 0) & (from_head < size)).astype(BF16)
    wide = jnp.dot(factors, spread, preferred_element_type=F32)

    c = moved[:, edge + state : edge + 2 * state].astype(BF16)
    corr = times_transposed(c, x_ref[:, edge : edge + state])
    corr = jnp.where(causal, corr, 0.0)
    high = corr.astype(BF16).astype(F32)
    corr = jnp.concatenate([high, corr - high, high], axis=1).astype(BF16)
    scaled = wide[rows : 2 * rows] * x_ref[:, 0:channels].astype(F32)
    high = scaled.astype(BF16)
    low = (scaled - high.astype(F32)).astype(BF16)
    y = jnp.dot(corr, jnp.concatenate([high, high, low], axis=0), preferred_element_type=F32)
    mixed = wide[0:rows] * y + wide[2 * rows : 2 * rows + 1] * moved[:, 0:channels]
    gate = moved[:, channels:edge]
    gated = (mixed * (gate / (1.0 + jnp.exp(-gate)))).astype(BF16).astype(F32)
    unit = gated * gain_ref[...]
    high = unit.astype(BF16)
    low = (unit - high.astype(F32)).astype(BF16)
    partial = times_transposed(jnp.concatenate([high, low], axis=0), weight_ref[...])
    partial = partial[0:rows] + partial[rows:]
    total = jnp.sum(gated * gated, axis=1, keepdims=True)
    kept_ref[...] = jnp.dot(order[0:half], residual_ref[...], preferred_element_type=F32)

    lane = lax.broadcasted_iota(jnp.int32, (rows, LANES), 1)
    info = pltpu.roll(moved[:, edge + 2 * state :], LANES + 1 - INFO, 1)
    info = jnp.where(lane == 0, total, info)
    width = partial.shape[1]
    start = mine_ref.shape[1] - LANES
    mine_ref[:, 0:width] = partial[0:half]
    mine_ref[:, start:] = info[0:half]
    theirs_ref[:, 0:width] = partial[half:]
    theirs_ref[:, start:] = info[half:]


def mixer(x, seq_rows, heads, gain, weight, residual):
    rows = x.shape[0]
    channels = gain.shape[1]
    width = weight.shape[1]
    total = (width + LANES - 1) // LANES * LANES + LANES
    half = rows // 2
    sums = jax.ShapeDtypeStruct((half, total), F32)
    whole = pl.BlockSpec(memory_space=VMEM)

    def kernel(*refs):
        mixer_kernel(seq_rows, heads, *refs)

    return pl.pallas_call(
        kernel,
        out_shape=(sums, sums, jax.ShapeDtypeStruct((half, width), F32)),
        in_specs=[whole] * 4,
        compiler_params=grant(8),
        name="mixer",
    )(x, gain, weight.T, residual)


def hidden_kernel(features, mine_ref, theirs_ref, kept_ref, out_ref):
    count, half, _ = out_ref.shape
    width = kept_ref.shape[1]
    start = mine_ref.shape[1] - LANES
    squares = mine_ref[:, start : start + 1] + theirs_ref[:, start : start + 1]
    scale = lax.rsqrt(squares / features + EPS)
    sums = mine_ref[:, 0:width] + theirs_ref[:, 0:width]
    hidden = (kept_ref[...] + sums * scale).astype(BF16).astype(F32)
    paired = jnp.concatenate([hidden[0:half], hidden[half:]], axis=1).astype(BF16)
    for k in range(count):
        out_ref[k] = paired


def hidden_rows(count, features, mine, theirs, kept):
    def kernel(*refs):
        hidden_kernel(features, *refs)

    return pl.pallas_call(
        kernel,
        out_shape=jax.ShapeDtypeStruct((count, kept.shape[0] // 2, 2 * kept.shape[1]), BF16),
        compiler_params=grant(4),
        name="hidden",
    )(mine, theirs, kept)


def head_kernel(
    h_ref, gain_ref, own_ref, upper_ref, lower_ref, own_mask_ref, other_mask_ref, info_ref, out_ref
):
    core = lax.axis_index("vocab")
    block = lax.axis_index("seq") * 2
    count, half, width = h_ref.shape
    rows, width = 2 * half, width // 2
    features = count * width
    squares = jnp.zeros((rows, width), F32)
    parts = []
    for k in range(count):
        pair = h_ref[k].astype(F32)
        part = jnp.concatenate([pair[:, 0:width], pair[:, width:]], axis=0)
        parts.append(part)
        squares = squares + part * part
    scale = lax.rsqrt(jnp.sum(squares, axis=1, keepdims=True) / features + EPS)
    entries = own_ref.shape[0]
    parts = [parts[k] * scale * gain_ref[k : k + 1, :] for k in range(count)]
    final = jnp.concatenate(parts, axis=1).astype(BF16)
    logits = [times_transposed(final, own_ref[...])]
    depth = features // 2
    logits.append(
        times_transposed(final[:, :depth], upper_ref[...])
        + times_transposed(final[:, depth:], lower_ref[...])
    )
    states = own_mask_ref.shape[0]
    start = info_ref.shape[1] - LANES
    ids = info_ref[:, start + 1 : start + 2].astype(jnp.int32)
    upper = info_ref[:, start + 2 : start + 3].astype(jnp.int32)
    target = upper * 256 + info_ref[:, start + 3 : start + 4].astype(jnp.int32)
    pick_row = (lax.broadcasted_iota(jnp.int32, (rows, states), 1) == ids).astype(BF16)
    column = lax.broadcasted_iota(jnp.int32, (rows, entries), 1)
    allowed, wanted = [], []
    for ref, which in ((own_mask_ref, core), (other_mask_ref, 1 - core)):
        table = (ref[...] == 1).astype(F32).astype(BF16)
        chosen = jnp.dot(pick_row, table, preferred_element_type=F32)
        is_target = column + (block + which) * entries == target
        wanted.append(is_target)
        allowed.append((chosen > 0.5) | is_target)
    tops = [
        jnp.max(jnp.where(a, x, NEG), axis=1, keepdims=True) for a, x in zip(allowed, logits)
    ]
    top = jnp.maximum(tops[0], tops[1])
    total = jnp.zeros((rows, 1), F32)
    picked = jnp.zeros((rows, 1), F32)
    for a, w, x in zip(allowed, wanted, logits):
        total = total + jnp.sum(jnp.where(a, jnp.exp(x - top), 0.0), axis=1, keepdims=True)
        picked = picked + jnp.sum(jnp.where(w, x, 0.0), axis=1, keepdims=True)
    own = rows // count
    lane = lax.broadcasted_iota(jnp.int32, (rows, LANES), 1)
    place = lane - (lax.broadcasted_iota(jnp.int32, (rows, LANES), 0) & (own - 1))
    stats = jnp.where(
        place == 0, top, jnp.where(place == GAP, total, jnp.where(place == 2 * GAP, picked, 0.0))
    )
    for k in range(count):
        out_ref[k] = jnp.sum(stats[k * own : (k + 1) * own], axis=0, keepdims=True)


def head(h, gain, own, other, own_mask, other_mask, info):
    count, half, width = h.shape
    whole = pl.BlockSpec(memory_space=VMEM)
    return pl.pallas_call(
        head_kernel,
        out_shape=jax.ShapeDtypeStruct((count, 1, LANES), F32),
        in_specs=[whole] * 8,
        compiler_params=grant(12),
        name="head",
    )(h, gain, own.T, *(o.T for o in other), own_mask, other_mask, info)


def combine_kernel(stats_ref, out_ref):
    tops = stats_ref[:, 0, :]
    totals = pltpu.roll(tops, LANES - GAP, 1)
    picked = pltpu.roll(tops, LANES - 2 * GAP, 1)
    top = jnp.max(tops, axis=0, keepdims=True)
    total = jnp.sum(totals * jnp.exp(tops - top), axis=0, keepdims=True)
    losses = jnp.log(total) + top - jnp.sum(picked, axis=0, keepdims=True)
    out_ref[...] = losses[:, 0 : out_ref.shape[1]]


def combine(own, stats):
    out = pl.pallas_call(
        combine_kernel,
        out_shape=jax.ShapeDtypeStruct((1, own), F32),
        compiler_params=grant(2),
        name="combine",
    )(stats)
    return out.reshape(own)


def wide_pack(count, ssm, gate, b, c, raw, bias, decay, skip, ids, targets):
    rows = ssm.shape[0]
    heads = raw.shape[1]

    def split(a):
        high = lax.reduce_precision(a, 8, 7)
        middle = lax.reduce_precision(a - high, 8, 7)
        return [high, middle, a - high - middle]

    parts = split(jax.nn.softplus(raw + bias[None, :]))
    parts += [a.astype(F32)[:, None] for a in (ids, targets // 256, targets % 256)]
    parts.append(jnp.zeros((rows, PARAMS - INFO - 3), F32))
    params = jnp.stack(split(-jnp.exp(decay)) + split(skip))
    parts.append(jnp.pad(params, ((0, rows - 6), (0, LANES - PARAMS - heads))))
    misc = jnp.concatenate(parts, axis=1).astype(BF16)
    row = jnp.concatenate([ssm, gate, b, c, misc], axis=1)
    return jnp.broadcast_to(row[None], (count,) + row.shape)


def wide_mixer(x, seq_rows, heads, gain, weight, residual):
    rows = x.shape[0]
    channels = gain.shape[1]
    state = (x.shape[1] - LANES - 2 * channels) // 2
    edge = 2 * channels
    core = lax.axis_index("vocab")
    misc = x[:, edge + 2 * state :].astype(F32)
    step = misc[:, 0:heads] + misc[:, heads : 2 * heads] + misc[:, 2 * heads : 3 * heads]
    params = misc[0:8, PARAMS : PARAMS + heads]
    decay = params[0] + params[1] + params[2]
    skip = params[3] + params[4] + params[5]
    log_cum = jnp.cumsum(step * decay[None, :], axis=0)
    corr = jnp.dot(
        x[:, edge + state : edge + 2 * state],
        x[:, edge : edge + state].T,
        preferred_element_type=F32,
    )
    values = x[:, 0:channels].astype(F32).reshape(rows, heads, -1).transpose(1, 0, 2)
    causal = jnp.arange(rows)[:, None] >= jnp.arange(rows)[None, :]

    def one(inputs):
        cum, size, v = inputs
        weights = jnp.exp(jnp.where(causal, cum[:, None] - cum[None, :], NEG))
        return jnp.dot(weights * corr * size[None, :], v, precision=HIGHEST)

    y = lax.map(one, (log_cum.T, step.T, values))
    mixed = (y + skip[:, None, None] * values).transpose(1, 0, 2).reshape(rows, channels)
    gated = (mixed * jax.nn.silu(x[:, channels:edge].astype(F32))).astype(BF16)
    wide = gated.astype(F32)
    squares = jnp.sum(wide * wide, axis=1, keepdims=True)
    unit = wide * gain
    high = lax.reduce_precision(unit, 8, 7)
    partial = jnp.dot(high.astype(BF16), weight, preferred_element_type=F32)
    low = (unit - high).astype(BF16)
    partial = partial + jnp.dot(low, weight, preferred_element_type=F32)
    width = weight.shape[1]
    start = (width + LANES - 1) // LANES * LANES
    info = jnp.concatenate([squares, misc[:, INFO : INFO + 3]], axis=1)
    sums = jnp.concatenate(
        [
            partial,
            jnp.zeros((rows, start - width), F32),
            info,
            jnp.zeros((rows, LANES - info.shape[1]), F32),
        ],
        axis=1,
    )

    def side(a, which):
        split = a.reshape(rows // seq_rows, 2, seq_rows // 2, -1)
        return lax.dynamic_index_in_dim(split, which, 1, False).reshape(rows // 2, -1)

    return side(sums, core), side(sums, 1 - core), side(residual.astype(F32), core)


def shards(
    ssm_input,
    gate_input,
    b_proj,
    readout_matrix,
    step_raw,
    step_bias,
    decay_log,
    head_skip_gain,
    norm_gain,
    out_weight,
    residual,
    final_gain,
    head_weight,
    mask_table,
    state_ids,
    targets,
):
    count = lax.axis_size("seq")
    rows, channels = ssm_input.shape
    features = 2 * channels
    small = count * rows <= LANES // 2
    swap = [(0, 1), (1, 0)]
    both = ("seq", "vocab")

    def exchange(a):
        if small:
            groups = circles(count)
            return lax.all_to_all(a, both, 0, 0, tiled=True, axis_index_groups=groups)
        return lax.all_to_all(a, "seq", 0, 0, tiled=True)

    packed = (pack if small else wide_pack)(
        count, ssm_input, gate_input, b_proj, readout_matrix, step_raw, step_bias, decay_log,
        head_skip_gain, state_ids, targets,
    )
    if small:
        depth = features // 2
        other_weight = tuple(
            lax.ppermute(head_weight[k * depth : (k + 1) * depth], "vocab", swap) for k in range(2)
        )
    else:
        other_weight = lax.ppermute(head_weight, "vocab", swap)
    other_mask = lax.ppermute(mask_table, "vocab", swap)
    gathered = lax.all_to_all(packed, "seq", 0, 0, tiled=True)
    final_gain = final_gain.reshape(count, features // count)
    norm_gain = norm_gain.reshape(1, channels)
    if small:
        gathered, other_weight, other_mask, final_gain = lax.optimization_barrier(
            (gathered, other_weight, other_mask, final_gain)
        )
    x = gathered.reshape(count * rows, packed.shape[2])
    mine, theirs, kept = (mixer if small else wide_mixer)(
        x, rows, step_bias.shape[0], norm_gain, out_weight, residual
    )
    arrived = lax.ppermute(theirs, "vocab", swap)
    if small:
        spread = hidden_rows(count, features, mine, arrived, kept)
    else:
        width = kept.shape[1]
        start = mine.shape[1] - LANES
        sums = mine + arrived
        scale = lax.rsqrt(sums[:, start : start + 1] / features + EPS)
        hidden = (kept + sums[:, 0:width] * scale).astype(BF16)
        spread = jnp.broadcast_to(hidden[None], (count,) + hidden.shape)
    full = exchange(spread)
    if small:
        stats = head(full, final_gain, head_weight, other_weight, mask_table, other_mask, mine)
    else:
        stats = wide_head(
            full, final_gain, head_weight, other_weight, mask_table, other_mask, mine
        )
    placed = exchange(stats)
    return combine(rows // 2, placed) if small else wide_combine(placed)


def wide_head(full, gain, own, other, own_mask, other_mask, info):
    count, rows, width = full.shape
    core = lax.axis_index("vocab")
    block = lax.axis_index("seq") * 2
    wide = full.transpose(1, 0, 2).reshape(rows, count * width).astype(F32)
    scale = lax.rsqrt(jnp.mean(wide * wide, axis=1, keepdims=True) + EPS)
    final = (wide * scale * gain.reshape(1, -1)).astype(BF16)
    start = info.shape[1] - LANES
    ids, upper, under = (info[:, start + k].astype(jnp.int32) for k in (1, 2, 3))
    target = upper * 256 + under
    entries = own.shape[1]
    logits, allowed, wanted = [], [], []
    for weight, table, which in ((own, own_mask, core), (other, other_mask, 1 - core)):
        logits.append(jnp.dot(final, weight, preferred_element_type=F32))
        column = (block + which) * entries + jnp.arange(entries, dtype=jnp.int32)
        wanted.append(column[None, :] == target[:, None])
        one_hot = (ids[:, None] == jnp.arange(table.shape[0])[None, :]).astype(BF16)
        chosen = jnp.dot(one_hot, (table == 1).astype(BF16), preferred_element_type=F32)
        allowed.append((chosen > 0.5) | wanted[-1])
    x, a, w = (jnp.concatenate(p, axis=1) for p in (logits, allowed, wanted))
    top = jnp.max(jnp.where(a, x, NEG), axis=1)
    total = jnp.sum(jnp.where(a, jnp.exp(x - top[:, None]), 0.0), axis=1)
    picked = jnp.sum(jnp.where(w, x, 0.0), axis=1)
    return jnp.stack([top, total, picked], axis=1).reshape(count, rows // count, 3)


def wide_combine(stats):
    top = jnp.max(stats[:, :, 0], axis=0)
    total = jnp.sum(stats[:, :, 1] * jnp.exp(stats[:, :, 0] - top[None, :]), axis=0)
    return jnp.log(total) + top - jnp.sum(stats[:, :, 2], axis=0)


def solution(mesh):
    placed = (
        P(("groups", "seq"), "vocab"),
        P(("groups", "seq"), "vocab"),
        P(("groups", "seq"), None),
        P(("groups", "seq"), None),
        P(("groups", "seq"), "vocab"),
        P("vocab"),
        P("vocab"),
        P("vocab"),
        P("vocab"),
        P("vocab", "seq"),
        P("groups", "seq"),
        P(),
        P(None, ("seq", "vocab")),
        P(None, ("seq", "vocab")),
        P(("groups", "seq")),
        P(("groups", "seq")),
    )
    return jax.shard_map(
        shards, mesh=mesh, in_specs=placed, out_specs=P(("groups", "seq", "vocab")), check_vma=False
    )
```

```python
import jax
import jax.numpy as jnp
from jax import lax
from jax.experimental import pallas as pl
from jax.experimental.pallas import tpu as pltpu
from jax.sharding import PartitionSpec as P

F32 = jnp.float32
BF16 = jnp.bfloat16
HIGHEST = lax.Precision.HIGHEST
EPS = 1e-05
LANES = 128
NEG = -1e30
INFO = 60
GAP = 32
PARAMS = 64
VMEM = pltpu.VMEM


def times_transposed(a, b):
    return lax.dot_general(a, b, (((1,), (1,)), ((), ())), preferred_element_type=F32)


def grant(mebibytes):
    return pltpu.CompilerParams(vmem_limit_bytes=mebibytes << 20)


def turn(seq):
    return seq // 4


def circles(count):
    return [[2 * s + (w + turn(s)) % 2 for s in range(count)] for w in range(2)]


def thirds(a):
    high = a.astype(BF16).astype(F32)
    middle = (a - high).astype(BF16).astype(F32)
    return high, middle, a - high - middle


def pack_kernel(
    ssm_ref, gate_ref, b_ref, c_ref, raw_ref, bias_ref, decay_ref, skip_ref, ids_ref, targets_ref,
    out_ref,
):
    count, rows, _ = out_ref.shape
    channels = ssm_ref.shape[1]
    state = b_ref.shape[1]
    heads = raw_ref.shape[1]
    edge = 2 * channels
    parts = list(thirds(jax.nn.softplus(raw_ref[...] + bias_ref[...])))
    row = lax.broadcasted_iota(jnp.int32, (rows, rows), 0)
    diagonal = row == lax.broadcasted_iota(jnp.int32, (rows, rows), 1)

    def upright(a):
        wide = jnp.broadcast_to(a.astype(F32), (rows, rows))
        return jnp.sum(jnp.where(diagonal, wide, 0.0), axis=1, keepdims=True)

    targets = upright(targets_ref[...])
    upper = jnp.floor(targets / 256.0)
    parts += [upright(ids_ref[...]), upper, targets - upper * 256.0]
    parts.append(jnp.zeros((rows, PARAMS - INFO - 3), F32))
    params = list(thirds(-jnp.exp(decay_ref[...]))) + list(thirds(skip_ref[...]))
    place = lax.broadcasted_iota(jnp.int32, (rows, heads), 0)
    table = jnp.zeros((rows, heads), F32)
    for k, part in enumerate(params):
        table = jnp.where(place == k, part, table)
    parts += [table, jnp.zeros((rows, LANES - PARAMS - heads), F32)]
    misc = jnp.concatenate(parts, axis=1).astype(BF16)
    for k in range(count):
        out_ref[k, :, 0:channels] = ssm_ref[...]
        out_ref[k, :, channels:edge] = gate_ref[...]
        out_ref[k, :, edge : edge + state] = b_ref[...]
        out_ref[k, :, edge + state : edge + 2 * state] = c_ref[...]
        out_ref[k, :, edge + 2 * state :] = misc


def pack(count, ssm, gate, b, c, raw, bias, decay, skip, ids, targets):
    rows, channels = ssm.shape
    heads = bias.shape[0]
    width = 2 * channels + 2 * b.shape[1] + LANES
    return pl.pallas_call(
        pack_kernel,
        out_shape=jax.ShapeDtypeStruct((count, rows, width), BF16),
        name="pack",
    )(
        ssm, gate, b, c, raw, bias.reshape(1, heads), decay.reshape(1, heads),
        skip.reshape(1, heads), ids.reshape(1, rows), targets.reshape(1, rows),
    )


def mixer_kernel(
    seq_rows, heads, x_ref, gain_ref, weight_ref, residual_ref,
    mine_ref, theirs_ref, kept_ref,
):
    mine = lax.axis_index("vocab") + turn(lax.axis_index("seq"))
    rows = x_ref.shape[0]
    channels = gain_ref.shape[1]
    state = (x_ref.shape[1] - LANES - 2 * channels) // 2
    edge = 2 * channels
    half = rows // 2
    size = channels // heads
    r64 = lax.broadcasted_iota(jnp.int32, (rows, rows), 0)
    c64 = lax.broadcasted_iota(jnp.int32, (rows, rows), 1)
    own = seq_rows // 2
    side = (r64 >= half).astype(jnp.int32)
    place = r64 - side * half
    seq = lax.shift_right_logical(place, own.bit_length() - 1)
    which = (mine + side + lax.shift_right_logical(seq, 2)) & 1
    source = place + seq * own + which * own
    order = (c64 == source).astype(BF16)
    causal = c64 <= source
    moved = jnp.dot(order, x_ref[...], preferred_element_type=F32)

    misc = x_ref[:, edge + 2 * state :].astype(F32)
    step = misc[:, 0:heads] + misc[:, heads : 2 * heads] + misc[:, 2 * heads : 3 * heads]
    params = pltpu.roll(misc[0:8], LANES - PARAMS, 1)
    decay = params[0:1] + params[1:2] + params[2:3]
    gains = params[3:4] + params[4:5] + params[5:6]
    rates = jnp.concatenate(thirds(step * decay[:, 0:heads]), axis=1).astype(BF16)
    sums = jnp.concatenate([(c64 <= r64).astype(BF16), causal.astype(BF16)], axis=0)
    cums = jnp.dot(sums, rates, preferred_element_type=F32)
    cums = cums[:, 0:heads] + cums[:, heads : 2 * heads] + cums[:, 2 * heads :]
    middle = cums[half - 1 : half]
    ahead = jnp.exp(cums[rows:] - middle)
    back = jnp.exp(middle - cums[0:rows]) * step
    skips = jnp.broadcast_to(gains[:, 0:heads], (8, heads))
    factors = jnp.concatenate([ahead, back, skips], axis=0)
    factors = jnp.concatenate(thirds(factors), axis=1).astype(BF16)
    head_row = lax.broadcasted_iota(jnp.int32, (3 * heads, 1), 0)
    for _ in range(2):
        head_row = jnp.where(head_row >= heads, head_row - heads, head_row)
    head_lane = lax.shift_right_logical(
        lax.broadcasted_iota(jnp.int32, (1, channels), 1), size.bit_length() - 1
    )
    spread = (head_row == head_lane).astype(BF16)
    wide = jnp.dot(factors, spread, preferred_element_type=F32)

    c = moved[:, edge + state : edge + 2 * state].astype(BF16)
    corr = times_transposed(c, x_ref[:, edge : edge + state])
    corr = jnp.where(causal, corr, 0.0)
    high = corr.astype(BF16).astype(F32)
    corr = jnp.concatenate([high, corr - high, high], axis=1).astype(BF16)
    scaled = wide[rows : 2 * rows] * x_ref[:, 0:channels].astype(F32)
    high = scaled.astype(BF16)
    low = (scaled - high.astype(F32)).astype(BF16)
    y = jnp.dot(corr, jnp.concatenate([high, high, low], axis=0), preferred_element_type=F32)
    mixed = wide[0:rows] * y + wide[2 * rows : 2 * rows + 1] * moved[:, 0:channels]
    gate = moved[:, channels:edge]
    gated = (mixed * (gate / (1.0 + jnp.exp(-gate)))).astype(BF16).astype(F32)
    unit = gated * gain_ref[...]
    high = unit.astype(BF16)
    low = (unit - high.astype(F32)).astype(BF16)
    partial = times_transposed(jnp.concatenate([high, low], axis=0), weight_ref[...])
    partial = partial[0:rows] + partial[rows:]
    total = jnp.sum(gated * gated, axis=1, keepdims=True)
    kept_ref[...] = jnp.dot(order[0:half], residual_ref[...], preferred_element_type=F32)

    lane = lax.broadcasted_iota(jnp.int32, (rows, LANES), 1)
    info = pltpu.roll(moved[:, edge + 2 * state :], LANES + 1 - INFO, 1)
    info = jnp.where(lane == 0, total, info)
    width = partial.shape[1]
    start = mine_ref.shape[1] - LANES
    mine_ref[:, 0:width] = partial[0:half]
    mine_ref[:, start:] = info[0:half]
    theirs_ref[:, 0:width] = partial[half:]
    theirs_ref[:, start:] = info[half:]


def mixer(x, seq_rows, heads, gain, weight, residual):
    rows = x.shape[0]
    channels = gain.shape[1]
    width = weight.shape[1]
    total = (width + LANES - 1) // LANES * LANES + LANES
    half = rows // 2
    sums = jax.ShapeDtypeStruct((half, total), F32)
    whole = pl.BlockSpec(memory_space=VMEM)

    def kernel(*refs):
        mixer_kernel(seq_rows, heads, *refs)

    return pl.pallas_call(
        kernel,
        out_shape=(sums, sums, jax.ShapeDtypeStruct((half, width), F32)),
        in_specs=[whole] * 4,
        compiler_params=grant(8),
        name="mixer",
    )(x, gain, weight.T, residual)


def hidden_kernel(features, mine_ref, theirs_ref, kept_ref, out_ref):
    count, half, _ = out_ref.shape
    width = kept_ref.shape[1]
    start = mine_ref.shape[1] - LANES
    squares = mine_ref[:, start : start + 1] + theirs_ref[:, start : start + 1]
    scale = lax.rsqrt(squares / features + EPS)
    sums = mine_ref[:, 0:width] + theirs_ref[:, 0:width]
    hidden = (kept_ref[...] + sums * scale).astype(BF16).astype(F32)
    paired = jnp.concatenate([hidden[0:half], hidden[half:]], axis=1).astype(BF16)
    for k in range(count):
        out_ref[k] = paired


def hidden_rows(count, features, mine, theirs, kept):
    def kernel(*refs):
        hidden_kernel(features, *refs)

    return pl.pallas_call(
        kernel,
        out_shape=jax.ShapeDtypeStruct((count, kept.shape[0] // 2, 2 * kept.shape[1]), BF16),
        compiler_params=grant(4),
        name="hidden",
    )(mine, theirs, kept)


def head_kernel(
    h_ref, gain_ref, own_ref, upper_ref, lower_ref, own_mask_ref, other_mask_ref, info_ref, out_ref
):
    core = lax.axis_index("vocab")
    block = lax.axis_index("seq") * 2
    count, half, width = h_ref.shape
    rows, width = 2 * half, width // 2
    features = count * width
    squares = jnp.zeros((rows, width), F32)
    parts = []
    for k in range(count):
        pair = h_ref[k].astype(F32)
        part = jnp.concatenate([pair[:, 0:width], pair[:, width:]], axis=0)
        parts.append(part)
        squares = squares + part * part
    scale = lax.rsqrt(jnp.sum(squares, axis=1, keepdims=True) / features + EPS)
    entries = own_ref.shape[0]
    parts = [parts[k] * scale * gain_ref[k : k + 1, :] for k in range(count)]
    final = jnp.concatenate(parts, axis=1).astype(BF16)
    logits = [times_transposed(final, own_ref[...])]
    depth = features // 2
    logits.append(
        times_transposed(final[:, :depth], upper_ref[...])
        + times_transposed(final[:, depth:], lower_ref[...])
    )
    states = own_mask_ref.shape[0]
    start = info_ref.shape[1] - LANES
    ids = info_ref[:, start + 1 : start + 2].astype(jnp.int32)
    upper = info_ref[:, start + 2 : start + 3].astype(jnp.int32)
    target = upper * 256 + info_ref[:, start + 3 : start + 4].astype(jnp.int32)
    pick_row = (lax.broadcasted_iota(jnp.int32, (rows, states), 1) == ids).astype(BF16)
    column = lax.broadcasted_iota(jnp.int32, (rows, entries), 1)
    allowed, wanted = [], []
    for ref, which in ((own_mask_ref, core), (other_mask_ref, 1 - core)):
        chosen = jnp.dot(pick_row, ref[...], preferred_element_type=F32)
        is_target = column + (block + which) * entries == target
        wanted.append(is_target)
        allowed.append((chosen > 0.5) | is_target)
    tops = [
        jnp.max(jnp.where(a, x, NEG), axis=1, keepdims=True) for a, x in zip(allowed, logits)
    ]
    top = jnp.maximum(tops[0], tops[1])
    total = jnp.zeros((rows, 1), F32)
    picked = jnp.zeros((rows, 1), F32)
    for a, w, x in zip(allowed, wanted, logits):
        total = total + jnp.sum(jnp.where(a, jnp.exp(x - top), 0.0), axis=1, keepdims=True)
        picked = picked + jnp.sum(jnp.where(w, x, 0.0), axis=1, keepdims=True)
    own = rows // count
    lane = lax.broadcasted_iota(jnp.int32, (rows, LANES), 1)
    place = lane - (lax.broadcasted_iota(jnp.int32, (rows, LANES), 0) & (own - 1))
    stats = jnp.where(
        place == 0, top, jnp.where(place == GAP, total, jnp.where(place == 2 * GAP, picked, 0.0))
    )
    for k in range(count):
        out_ref[k] = jnp.sum(stats[k * own : (k + 1) * own], axis=0, keepdims=True)


def head(h, gain, own, other, own_mask, other_mask, info):
    count, half, width = h.shape
    whole = pl.BlockSpec(memory_space=VMEM)
    return pl.pallas_call(
        head_kernel,
        out_shape=jax.ShapeDtypeStruct((count, 1, LANES), F32),
        in_specs=[whole] * 8,
        compiler_params=grant(12),
        name="head",
    )(h, gain, own.T, *(o.T for o in other), own_mask, other_mask, info)


def combine_kernel(stats_ref, out_ref):
    tops = stats_ref[:, 0, :]
    totals = pltpu.roll(tops, LANES - GAP, 1)
    picked = pltpu.roll(tops, LANES - 2 * GAP, 1)
    top = jnp.max(tops, axis=0, keepdims=True)
    total = jnp.sum(totals * jnp.exp(tops - top), axis=0, keepdims=True)
    losses = jnp.log(total) + top - jnp.sum(picked, axis=0, keepdims=True)
    out_ref[...] = losses[:, 0 : out_ref.shape[1]]


def combine(own, stats):
    out = pl.pallas_call(
        combine_kernel,
        out_shape=jax.ShapeDtypeStruct((1, own), F32),
        compiler_params=grant(2),
        name="combine",
    )(stats)
    return out.reshape(own)


def wide_pack(count, ssm, gate, b, c, raw, bias, decay, skip, ids, targets):
    rows = ssm.shape[0]
    heads = raw.shape[1]

    def split(a):
        high = lax.reduce_precision(a, 8, 7)
        middle = lax.reduce_precision(a - high, 8, 7)
        return [high, middle, a - high - middle]

    parts = split(jax.nn.softplus(raw + bias[None, :]))
    parts += [a.astype(F32)[:, None] for a in (ids, targets // 256, targets % 256)]
    parts.append(jnp.zeros((rows, PARAMS - INFO - 3), F32))
    params = jnp.stack(split(-jnp.exp(decay)) + split(skip))
    parts.append(jnp.pad(params, ((0, rows - 6), (0, LANES - PARAMS - heads))))
    misc = jnp.concatenate(parts, axis=1).astype(BF16)
    row = jnp.concatenate([ssm, gate, b, c, misc], axis=1)
    return jnp.broadcast_to(row[None], (count,) + row.shape)


def wide_mixer(x, seq_rows, heads, gain, weight, residual):
    rows = x.shape[0]
    channels = gain.shape[1]
    state = (x.shape[1] - LANES - 2 * channels) // 2
    edge = 2 * channels
    core = lax.axis_index("vocab")
    misc = x[:, edge + 2 * state :].astype(F32)
    step = misc[:, 0:heads] + misc[:, heads : 2 * heads] + misc[:, 2 * heads : 3 * heads]
    params = misc[0:8, PARAMS : PARAMS + heads]
    decay = params[0] + params[1] + params[2]
    skip = params[3] + params[4] + params[5]
    log_cum = jnp.cumsum(step * decay[None, :], axis=0)
    corr = jnp.dot(
        x[:, edge + state : edge + 2 * state],
        x[:, edge : edge + state].T,
        preferred_element_type=F32,
    )
    values = x[:, 0:channels].astype(F32).reshape(rows, heads, -1).transpose(1, 0, 2)
    causal = jnp.arange(rows)[:, None] >= jnp.arange(rows)[None, :]

    def one(inputs):
        cum, size, v = inputs
        weights = jnp.exp(jnp.where(causal, cum[:, None] - cum[None, :], NEG))
        return jnp.dot(weights * corr * size[None, :], v, precision=HIGHEST)

    y = lax.map(one, (log_cum.T, step.T, values))
    mixed = (y + skip[:, None, None] * values).transpose(1, 0, 2).reshape(rows, channels)
    gated = (mixed * jax.nn.silu(x[:, channels:edge].astype(F32))).astype(BF16)
    wide = gated.astype(F32)
    squares = jnp.sum(wide * wide, axis=1, keepdims=True)
    unit = wide * gain
    high = lax.reduce_precision(unit, 8, 7)
    partial = jnp.dot(high.astype(BF16), weight, preferred_element_type=F32)
    low = (unit - high).astype(BF16)
    partial = partial + jnp.dot(low, weight, preferred_element_type=F32)
    width = weight.shape[1]
    start = (width + LANES - 1) // LANES * LANES
    info = jnp.concatenate([squares, misc[:, INFO : INFO + 3]], axis=1)
    sums = jnp.concatenate(
        [
            partial,
            jnp.zeros((rows, start - width), F32),
            info,
            jnp.zeros((rows, LANES - info.shape[1]), F32),
        ],
        axis=1,
    )

    def side(a, which):
        split = a.reshape(rows // seq_rows, 2, seq_rows // 2, -1)
        return lax.dynamic_index_in_dim(split, which, 1, False).reshape(rows // 2, -1)

    return side(sums, core), side(sums, 1 - core), side(residual.astype(F32), core)


def shards(
    ssm_input,
    gate_input,
    b_proj,
    readout_matrix,
    step_raw,
    step_bias,
    decay_log,
    head_skip_gain,
    norm_gain,
    out_weight,
    residual,
    final_gain,
    head_weight,
    mask_table,
    state_ids,
    targets,
):
    count = lax.axis_size("seq")
    rows, channels = ssm_input.shape
    features = 2 * channels
    small = count * rows <= LANES // 2
    swap = [(0, 1), (1, 0)]
    both = ("seq", "vocab")

    def exchange(a):
        if small:
            groups = circles(count)
            return lax.all_to_all(a, both, 0, 0, tiled=True, axis_index_groups=groups)
        return lax.all_to_all(a, "seq", 0, 0, tiled=True)

    packed = (pack if small else wide_pack)(
        count, ssm_input, gate_input, b_proj, readout_matrix, step_raw, step_bias, decay_log,
        head_skip_gain, state_ids, targets,
    )
    if small:
        depth = features // 2
        other_weight = tuple(
            lax.ppermute(head_weight[k * depth : (k + 1) * depth], "vocab", swap) for k in range(2)
        )
    else:
        other_weight = lax.ppermute(head_weight, "vocab", swap)
    mask_table = (mask_table == 1).astype(BF16)
    other_mask = lax.ppermute(mask_table, "vocab", swap)
    gathered = lax.all_to_all(packed, "seq", 0, 0, tiled=True)
    final_gain = final_gain.reshape(count, features // count)
    norm_gain = norm_gain.reshape(1, channels)
    if small:
        gathered, other_weight, mask_table, other_mask, final_gain = lax.optimization_barrier(
            (gathered, other_weight, mask_table, other_mask, final_gain)
        )
    x = gathered.reshape(count * rows, packed.shape[2])
    mine, theirs, kept = (mixer if small else wide_mixer)(
        x, rows, step_bias.shape[0], norm_gain, out_weight, residual
    )
    arrived = lax.ppermute(theirs, "vocab", swap)
    if small:
        spread = hidden_rows(count, features, mine, arrived, kept)
    else:
        width = kept.shape[1]
        start = mine.shape[1] - LANES
        sums = mine + arrived
        scale = lax.rsqrt(sums[:, start : start + 1] / features + EPS)
        hidden = (kept + sums[:, 0:width] * scale).astype(BF16)
        spread = jnp.broadcast_to(hidden[None], (count,) + hidden.shape)
    full = exchange(spread)
    if small:
        stats = head(full, final_gain, head_weight, other_weight, mask_table, other_mask, mine)
    else:
        stats = wide_head(
            full, final_gain, head_weight, other_weight, mask_table, other_mask, mine
        )
    placed = exchange(stats)
    return combine(rows // 2, placed) if small else wide_combine(placed)


def wide_head(full, gain, own, other, own_mask, other_mask, info):
    count, rows, width = full.shape
    core = lax.axis_index("vocab")
    block = lax.axis_index("seq") * 2
    wide = full.transpose(1, 0, 2).reshape(rows, count * width).astype(F32)
    scale = lax.rsqrt(jnp.mean(wide * wide, axis=1, keepdims=True) + EPS)
    final = (wide * scale * gain.reshape(1, -1)).astype(BF16)
    start = info.shape[1] - LANES
    ids, upper, under = (info[:, start + k].astype(jnp.int32) for k in (1, 2, 3))
    target = upper * 256 + under
    entries = own.shape[1]
    logits, allowed, wanted = [], [], []
    for weight, table, which in ((own, own_mask, core), (other, other_mask, 1 - core)):
        logits.append(jnp.dot(final, weight, preferred_element_type=F32))
        column = (block + which) * entries + jnp.arange(entries, dtype=jnp.int32)
        wanted.append(column[None, :] == target[:, None])
        one_hot = (ids[:, None] == jnp.arange(table.shape[0])[None, :]).astype(BF16)
        chosen = jnp.dot(one_hot, (table == 1).astype(BF16), preferred_element_type=F32)
        allowed.append((chosen > 0.5) | wanted[-1])
    x, a, w = (jnp.concatenate(p, axis=1) for p in (logits, allowed, wanted))
    top = jnp.max(jnp.where(a, x, NEG), axis=1)
    total = jnp.sum(jnp.where(a, jnp.exp(x - top[:, None]), 0.0), axis=1)
    picked = jnp.sum(jnp.where(w, x, 0.0), axis=1)
    return jnp.stack([top, total, picked], axis=1).reshape(count, rows // count, 3)


def wide_combine(stats):
    top = jnp.max(stats[:, :, 0], axis=0)
    total = jnp.sum(stats[:, :, 1] * jnp.exp(stats[:, :, 0] - top[None, :]), axis=0)
    return jnp.log(total) + top - jnp.sum(stats[:, :, 2], axis=0)


def solution(mesh):
    placed = (
        P(("groups", "seq"), "vocab"),
        P(("groups", "seq"), "vocab"),
        P(("groups", "seq"), None),
        P(("groups", "seq"), None),
        P(("groups", "seq"), "vocab"),
        P("vocab"),
        P("vocab"),
        P("vocab"),
        P("vocab"),
        P("vocab", "seq"),
        P("groups", "seq"),
        P(),
        P(None, ("seq", "vocab")),
        P(None, ("seq", "vocab")),
        P(("groups", "seq")),
        P(("groups", "seq")),
    )
    return jax.shard_map(
        shards, mesh=mesh, in_specs=placed, out_specs=P(("groups", "seq", "vocab")), check_vma=False
    )
```

```python
import jax
import jax.numpy as jnp
from jax import lax
from jax.experimental import pallas as pl
from jax.experimental.pallas import tpu as pltpu
from jax.sharding import PartitionSpec as P

F32 = jnp.float32
BF16 = jnp.bfloat16
HIGHEST = lax.Precision.HIGHEST
EPS = 1e-05
LANES = 128
NEG = -1e30
INFO = 60
GAP = 32
PARAMS = 64
VMEM = pltpu.VMEM


def times_transposed(a, b):
    return lax.dot_general(a, b, (((1,), (1,)), ((), ())), preferred_element_type=F32)


def grant(mebibytes):
    return pltpu.CompilerParams(vmem_limit_bytes=mebibytes << 20)


def turn(seq):
    return seq // 4


def circles(count):
    return [[2 * s + (w + turn(s)) % 2 for s in range(count)] for w in range(2)]


def thirds(a):
    high = a.astype(BF16).astype(F32)
    middle = (a - high).astype(BF16).astype(F32)
    return high, middle, a - high - middle


def pack_kernel(
    ssm_ref, gate_ref, b_ref, c_ref, raw_ref, bias_ref, decay_ref, skip_ref, ids_ref, targets_ref,
    out_ref,
):
    count, rows, _ = out_ref.shape
    channels = ssm_ref.shape[1]
    state = b_ref.shape[1]
    heads = raw_ref.shape[1]
    edge = 2 * channels
    parts = list(thirds(jax.nn.softplus(raw_ref[...] + bias_ref[...])))
    row = lax.broadcasted_iota(jnp.int32, (rows, rows), 0)
    diagonal = row == lax.broadcasted_iota(jnp.int32, (rows, rows), 1)

    def upright(a):
        wide = jnp.broadcast_to(a.astype(F32), (rows, rows))
        return jnp.sum(jnp.where(diagonal, wide, 0.0), axis=1, keepdims=True)

    targets = upright(targets_ref[...])
    upper = jnp.floor(targets / 256.0)
    parts += [upright(ids_ref[...]), upper, targets - upper * 256.0]
    parts.append(jnp.zeros((rows, PARAMS - INFO - 3), F32))
    params = list(thirds(-jnp.exp(decay_ref[...]))) + list(thirds(skip_ref[...]))
    place = lax.broadcasted_iota(jnp.int32, (rows, heads), 0)
    table = jnp.zeros((rows, heads), F32)
    for k, part in enumerate(params):
        table = jnp.where(place == k, part, table)
    parts += [table, jnp.zeros((rows, LANES - PARAMS - heads), F32)]
    misc = jnp.concatenate(parts, axis=1).astype(BF16)
    for k in range(count):
        out_ref[k, :, 0:channels] = ssm_ref[...]
        out_ref[k, :, channels:edge] = gate_ref[...]
        out_ref[k, :, edge : edge + state] = b_ref[...]
        out_ref[k, :, edge + state : edge + 2 * state] = c_ref[...]
        out_ref[k, :, edge + 2 * state :] = misc


def pack(count, ssm, gate, b, c, raw, bias, decay, skip, ids, targets):
    rows, channels = ssm.shape
    heads = bias.shape[0]
    width = 2 * channels + 2 * b.shape[1] + LANES
    return pl.pallas_call(
        pack_kernel,
        out_shape=jax.ShapeDtypeStruct((count, rows, width), BF16),
        name="pack",
    )(
        ssm, gate, b, c, raw, bias.reshape(1, heads), decay.reshape(1, heads),
        skip.reshape(1, heads), ids.reshape(1, rows), targets.reshape(1, rows),
    )


def row_order(rows, seq_rows, half, mine):
    r64 = lax.broadcasted_iota(jnp.int32, (rows, rows), 0)
    c64 = lax.broadcasted_iota(jnp.int32, (rows, rows), 1)
    own = seq_rows // 2
    side = (r64 >= half).astype(jnp.int32)
    place = r64 - side * half
    seq = lax.shift_right_logical(place, own.bit_length() - 1)
    which = (mine + side + lax.shift_right_logical(seq, 2)) & 1
    source = place + seq * own + which * own
    return r64, c64, source


def keep_kernel(seq_rows, residual_ref, kept_ref):
    mine = lax.axis_index("vocab") + turn(lax.axis_index("seq"))
    rows, half = residual_ref.shape[0], kept_ref.shape[0]
    _, c64, source = row_order(rows, seq_rows, half, mine)
    order = (c64 == source).astype(BF16)
    kept_ref[...] = jnp.dot(order[0:half], residual_ref[...], preferred_element_type=F32)


def keep(seq_rows, residual):
    rows, width = residual.shape

    def kernel(*refs):
        keep_kernel(seq_rows, *refs)

    return pl.pallas_call(
        kernel,
        out_shape=jax.ShapeDtypeStruct((rows // 2, width), F32),
        compiler_params=grant(2),
        name="keep",
    )(residual)


def mixer_kernel(
    seq_rows, heads, x_ref, gain_ref, weight_ref, mine_ref, theirs_ref,
):
    mine = lax.axis_index("vocab") + turn(lax.axis_index("seq"))
    rows = x_ref.shape[0]
    channels = gain_ref.shape[1]
    state = (x_ref.shape[1] - LANES - 2 * channels) // 2
    edge = 2 * channels
    half = rows // 2
    size = channels // heads
    r64, c64, source = row_order(rows, seq_rows, half, mine)
    order = (c64 == source).astype(BF16)
    causal = c64 <= source
    moved = jnp.dot(order, x_ref[...], preferred_element_type=F32)

    misc = x_ref[:, edge + 2 * state :].astype(F32)
    step = misc[:, 0:heads] + misc[:, heads : 2 * heads] + misc[:, 2 * heads : 3 * heads]
    params = pltpu.roll(misc[0:8], LANES - PARAMS, 1)
    decay = params[0:1] + params[1:2] + params[2:3]
    gains = params[3:4] + params[4:5] + params[5:6]
    rates = jnp.concatenate(thirds(step * decay[:, 0:heads]), axis=1).astype(BF16)
    sums = jnp.concatenate([(c64 <= r64).astype(BF16), causal.astype(BF16)], axis=0)
    cums = jnp.dot(sums, rates, preferred_element_type=F32)
    cums = cums[:, 0:heads] + cums[:, heads : 2 * heads] + cums[:, 2 * heads :]
    middle = cums[half - 1 : half]
    ahead = jnp.exp(cums[rows:] - middle)
    back = jnp.exp(middle - cums[0:rows]) * step
    skips = jnp.broadcast_to(gains[:, 0:heads], (8, heads))
    factors = jnp.concatenate([ahead, back, skips], axis=0)
    factors = jnp.concatenate(thirds(factors), axis=1).astype(BF16)
    head_row = lax.broadcasted_iota(jnp.int32, (3 * heads, 1), 0)
    for _ in range(2):
        head_row = jnp.where(head_row >= heads, head_row - heads, head_row)
    head_lane = lax.shift_right_logical(
        lax.broadcasted_iota(jnp.int32, (1, channels), 1), size.bit_length() - 1
    )
    spread = (head_row == head_lane).astype(BF16)
    wide = jnp.dot(factors, spread, preferred_element_type=F32)

    c = moved[:, edge + state : edge + 2 * state].astype(BF16)
    corr = times_transposed(c, x_ref[:, edge : edge + state])
    corr = jnp.where(causal, corr, 0.0)
    high = corr.astype(BF16).astype(F32)
    corr = jnp.concatenate([high, corr - high, high], axis=1).astype(BF16)
    scaled = wide[rows : 2 * rows] * x_ref[:, 0:channels].astype(F32)
    high = scaled.astype(BF16)
    low = (scaled - high.astype(F32)).astype(BF16)
    y = jnp.dot(corr, jnp.concatenate([high, high, low], axis=0), preferred_element_type=F32)
    mixed = wide[0:rows] * y + wide[2 * rows : 2 * rows + 1] * moved[:, 0:channels]
    gate = moved[:, channels:edge]
    gated = (mixed * (gate / (1.0 + jnp.exp(-gate)))).astype(BF16).astype(F32)
    unit = gated * gain_ref[...]
    high = unit.astype(BF16)
    low = (unit - high.astype(F32)).astype(BF16)
    partial = times_transposed(jnp.concatenate([high, low], axis=0), weight_ref[...])
    partial = partial[0:rows] + partial[rows:]
    total = jnp.sum(gated * gated, axis=1, keepdims=True)
    lane = lax.broadcasted_iota(jnp.int32, (rows, LANES), 1)
    info = pltpu.roll(moved[:, edge + 2 * state :], LANES + 1 - INFO, 1)
    info = jnp.where(lane == 0, total, info)
    width = partial.shape[1]
    start = mine_ref.shape[1] - LANES
    mine_ref[:, 0:width] = partial[0:half]
    mine_ref[:, start:] = info[0:half]
    theirs_ref[:, 0:width] = partial[half:]
    theirs_ref[:, start:] = info[half:]


def mixer(x, seq_rows, heads, gain, weight):
    rows = x.shape[0]
    channels = gain.shape[1]
    width = weight.shape[1]
    total = (width + LANES - 1) // LANES * LANES + LANES
    half = rows // 2
    sums = jax.ShapeDtypeStruct((half, total), F32)
    whole = pl.BlockSpec(memory_space=VMEM)

    def kernel(*refs):
        mixer_kernel(seq_rows, heads, *refs)

    return pl.pallas_call(
        kernel,
        out_shape=(sums, sums),
        in_specs=[whole] * 3,
        compiler_params=grant(8),
        name="mixer",
    )(x, gain, weight.T)


def hidden_kernel(features, mine_ref, theirs_ref, kept_ref, out_ref):
    count, half, _ = out_ref.shape
    width = kept_ref.shape[1]
    start = mine_ref.shape[1] - LANES
    squares = mine_ref[:, start : start + 1] + theirs_ref[:, start : start + 1]
    scale = lax.rsqrt(squares / features + EPS)
    sums = mine_ref[:, 0:width] + theirs_ref[:, 0:width]
    hidden = (kept_ref[...] + sums * scale).astype(BF16).astype(F32)
    paired = jnp.concatenate([hidden[0:half], hidden[half:]], axis=1).astype(BF16)
    for k in range(count):
        out_ref[k] = paired


def hidden_rows(count, features, mine, theirs, kept):
    def kernel(*refs):
        hidden_kernel(features, *refs)

    return pl.pallas_call(
        kernel,
        out_shape=jax.ShapeDtypeStruct((count, kept.shape[0] // 2, 2 * kept.shape[1]), BF16),
        compiler_params=grant(4),
        name="hidden",
    )(mine, theirs, kept)


def head_kernel(
    h_ref, gain_ref, own_ref, upper_ref, lower_ref, own_mask_ref, other_mask_ref, info_ref, out_ref
):
    core = lax.axis_index("vocab")
    block = lax.axis_index("seq") * 2
    count, half, width = h_ref.shape
    rows, width = 2 * half, width // 2
    features = count * width
    squares = jnp.zeros((rows, width), F32)
    parts = []
    for k in range(count):
        pair = h_ref[k].astype(F32)
        part = jnp.concatenate([pair[:, 0:width], pair[:, width:]], axis=0)
        parts.append(part)
        squares = squares + part * part
    scale = lax.rsqrt(jnp.sum(squares, axis=1, keepdims=True) / features + EPS)
    entries = own_ref.shape[0]
    parts = [parts[k] * scale * gain_ref[k : k + 1, :] for k in range(count)]
    final = jnp.concatenate(parts, axis=1).astype(BF16)
    logits = [times_transposed(final, own_ref[...])]
    depth = features // 2
    logits.append(
        times_transposed(final[:, :depth], upper_ref[...])
        + times_transposed(final[:, depth:], lower_ref[...])
    )
    states = own_mask_ref.shape[0]
    start = info_ref.shape[1] - LANES
    ids = info_ref[:, start + 1 : start + 2].astype(jnp.int32)
    upper = info_ref[:, start + 2 : start + 3].astype(jnp.int32)
    target = upper * 256 + info_ref[:, start + 3 : start + 4].astype(jnp.int32)
    pick_row = (lax.broadcasted_iota(jnp.int32, (rows, states), 1) == ids).astype(BF16)
    column = lax.broadcasted_iota(jnp.int32, (rows, entries), 1)
    allowed, wanted = [], []
    for ref, which in ((own_mask_ref, core), (other_mask_ref, 1 - core)):
        chosen = jnp.dot(pick_row, ref[...], preferred_element_type=F32)
        is_target = column + (block + which) * entries == target
        wanted.append(is_target)
        allowed.append((chosen > 0.5) | is_target)
    tops = [
        jnp.max(jnp.where(a, x, NEG), axis=1, keepdims=True) for a, x in zip(allowed, logits)
    ]
    top = jnp.maximum(tops[0], tops[1])
    total = jnp.zeros((rows, 1), F32)
    picked = jnp.zeros((rows, 1), F32)
    for a, w, x in zip(allowed, wanted, logits):
        total = total + jnp.sum(jnp.where(a, jnp.exp(x - top), 0.0), axis=1, keepdims=True)
        picked = picked + jnp.sum(jnp.where(w, x, 0.0), axis=1, keepdims=True)
    own = rows // count
    lane = lax.broadcasted_iota(jnp.int32, (rows, LANES), 1)
    place = lane - (lax.broadcasted_iota(jnp.int32, (rows, LANES), 0) & (own - 1))
    stats = jnp.where(
        place == 0, top, jnp.where(place == GAP, total, jnp.where(place == 2 * GAP, picked, 0.0))
    )
    for k in range(count):
        out_ref[k] = jnp.sum(stats[k * own : (k + 1) * own], axis=0, keepdims=True)


def head(h, gain, own, other, own_mask, other_mask, info):
    count, half, width = h.shape
    whole = pl.BlockSpec(memory_space=VMEM)
    return pl.pallas_call(
        head_kernel,
        out_shape=jax.ShapeDtypeStruct((count, 1, LANES), F32),
        in_specs=[whole] * 8,
        compiler_params=grant(12),
        name="head",
    )(h, gain, own.T, *(o.T for o in other), own_mask, other_mask, info)


def combine_kernel(stats_ref, out_ref):
    tops = stats_ref[:, 0, :]
    totals = pltpu.roll(tops, LANES - GAP, 1)
    picked = pltpu.roll(tops, LANES - 2 * GAP, 1)
    top = jnp.max(tops, axis=0, keepdims=True)
    total = jnp.sum(totals * jnp.exp(tops - top), axis=0, keepdims=True)
    losses = jnp.log(total) + top - jnp.sum(picked, axis=0, keepdims=True)
    out_ref[...] = losses[:, 0 : out_ref.shape[1]]


def combine(own, stats):
    out = pl.pallas_call(
        combine_kernel,
        out_shape=jax.ShapeDtypeStruct((1, own), F32),
        compiler_params=grant(2),
        name="combine",
    )(stats)
    return out.reshape(own)


def wide_pack(count, ssm, gate, b, c, raw, bias, decay, skip, ids, targets):
    rows = ssm.shape[0]
    heads = raw.shape[1]

    def split(a):
        high = lax.reduce_precision(a, 8, 7)
        middle = lax.reduce_precision(a - high, 8, 7)
        return [high, middle, a - high - middle]

    parts = split(jax.nn.softplus(raw + bias[None, :]))
    parts += [a.astype(F32)[:, None] for a in (ids, targets // 256, targets % 256)]
    parts.append(jnp.zeros((rows, PARAMS - INFO - 3), F32))
    params = jnp.stack(split(-jnp.exp(decay)) + split(skip))
    parts.append(jnp.pad(params, ((0, rows - 6), (0, LANES - PARAMS - heads))))
    misc = jnp.concatenate(parts, axis=1).astype(BF16)
    row = jnp.concatenate([ssm, gate, b, c, misc], axis=1)
    return jnp.broadcast_to(row[None], (count,) + row.shape)


def wide_mixer(x, seq_rows, heads, gain, weight, residual):
    rows = x.shape[0]
    channels = gain.shape[1]
    state = (x.shape[1] - LANES - 2 * channels) // 2
    edge = 2 * channels
    core = lax.axis_index("vocab")
    misc = x[:, edge + 2 * state :].astype(F32)
    step = misc[:, 0:heads] + misc[:, heads : 2 * heads] + misc[:, 2 * heads : 3 * heads]
    params = misc[0:8, PARAMS : PARAMS + heads]
    decay = params[0] + params[1] + params[2]
    skip = params[3] + params[4] + params[5]
    log_cum = jnp.cumsum(step * decay[None, :], axis=0)
    corr = jnp.dot(
        x[:, edge + state : edge + 2 * state],
        x[:, edge : edge + state].T,
        preferred_element_type=F32,
    )
    values = x[:, 0:channels].astype(F32).reshape(rows, heads, -1).transpose(1, 0, 2)
    causal = jnp.arange(rows)[:, None] >= jnp.arange(rows)[None, :]

    def one(inputs):
        cum, size, v = inputs
        weights = jnp.exp(jnp.where(causal, cum[:, None] - cum[None, :], NEG))
        return jnp.dot(weights * corr * size[None, :], v, precision=HIGHEST)

    y = lax.map(one, (log_cum.T, step.T, values))
    mixed = (y + skip[:, None, None] * values).transpose(1, 0, 2).reshape(rows, channels)
    gated = (mixed * jax.nn.silu(x[:, channels:edge].astype(F32))).astype(BF16)
    wide = gated.astype(F32)
    squares = jnp.sum(wide * wide, axis=1, keepdims=True)
    unit = wide * gain
    high = lax.reduce_precision(unit, 8, 7)
    partial = jnp.dot(high.astype(BF16), weight, preferred_element_type=F32)
    low = (unit - high).astype(BF16)
    partial = partial + jnp.dot(low, weight, preferred_element_type=F32)
    width = weight.shape[1]
    start = (width + LANES - 1) // LANES * LANES
    info = jnp.concatenate([squares, misc[:, INFO : INFO + 3]], axis=1)
    sums = jnp.concatenate(
        [
            partial,
            jnp.zeros((rows, start - width), F32),
            info,
            jnp.zeros((rows, LANES - info.shape[1]), F32),
        ],
        axis=1,
    )

    def side(a, which):
        split = a.reshape(rows // seq_rows, 2, seq_rows // 2, -1)
        return lax.dynamic_index_in_dim(split, which, 1, False).reshape(rows // 2, -1)

    return side(sums, core), side(sums, 1 - core), side(residual.astype(F32), core)


def shards(
    ssm_input,
    gate_input,
    b_proj,
    readout_matrix,
    step_raw,
    step_bias,
    decay_log,
    head_skip_gain,
    norm_gain,
    out_weight,
    residual,
    final_gain,
    head_weight,
    mask_table,
    state_ids,
    targets,
):
    count = lax.axis_size("seq")
    rows, channels = ssm_input.shape
    features = 2 * channels
    small = count * rows <= LANES // 2
    swap = [(0, 1), (1, 0)]
    both = ("seq", "vocab")

    def exchange(a):
        if small:
            groups = circles(count)
            return lax.all_to_all(a, both, 0, 0, tiled=True, axis_index_groups=groups)
        return lax.all_to_all(a, "seq", 0, 0, tiled=True)

    packed = (pack if small else wide_pack)(
        count, ssm_input, gate_input, b_proj, readout_matrix, step_raw, step_bias, decay_log,
        head_skip_gain, state_ids, targets,
    )
    if small:
        depth = features // 2
        other_weight = tuple(
            lax.ppermute(head_weight[k * depth : (k + 1) * depth], "vocab", swap) for k in range(2)
        )
    else:
        other_weight = lax.ppermute(head_weight, "vocab", swap)
    mask_table = (mask_table == 1).astype(BF16)
    other_mask = lax.ppermute(mask_table, "vocab", swap)
    gathered = lax.all_to_all(packed, "seq", 0, 0, tiled=True)
    final_gain = final_gain.reshape(count, features // count)
    norm_gain = norm_gain.reshape(1, channels)
    if small:
        kept = keep(rows, residual)
        gathered, other_weight, mask_table, other_mask, final_gain, kept = lax.optimization_barrier(
            (gathered, other_weight, mask_table, other_mask, final_gain, kept)
        )
    x = gathered.reshape(count * rows, packed.shape[2])
    heads = step_bias.shape[0]
    if small:
        mine, theirs = mixer(x, rows, heads, norm_gain, out_weight)
    else:
        mine, theirs, kept = wide_mixer(x, rows, heads, norm_gain, out_weight, residual)
    arrived = lax.ppermute(theirs, "vocab", swap)
    if small:
        spread = hidden_rows(count, features, mine, arrived, kept)
    else:
        width = kept.shape[1]
        start = mine.shape[1] - LANES
        sums = mine + arrived
        scale = lax.rsqrt(sums[:, start : start + 1] / features + EPS)
        hidden = (kept + sums[:, 0:width] * scale).astype(BF16)
        spread = jnp.broadcast_to(hidden[None], (count,) + hidden.shape)
    full = exchange(spread)
    if small:
        stats = head(full, final_gain, head_weight, other_weight, mask_table, other_mask, mine)
    else:
        stats = wide_head(
            full, final_gain, head_weight, other_weight, mask_table, other_mask, mine
        )
    placed = exchange(stats)
    return combine(rows // 2, placed) if small else wide_combine(placed)


def wide_head(full, gain, own, other, own_mask, other_mask, info):
    count, rows, width = full.shape
    core = lax.axis_index("vocab")
    block = lax.axis_index("seq") * 2
    wide = full.transpose(1, 0, 2).reshape(rows, count * width).astype(F32)
    scale = lax.rsqrt(jnp.mean(wide * wide, axis=1, keepdims=True) + EPS)
    final = (wide * scale * gain.reshape(1, -1)).astype(BF16)
    start = info.shape[1] - LANES
    ids, upper, under = (info[:, start + k].astype(jnp.int32) for k in (1, 2, 3))
    target = upper * 256 + under
    entries = own.shape[1]
    logits, allowed, wanted = [], [], []
    for weight, table, which in ((own, own_mask, core), (other, other_mask, 1 - core)):
        logits.append(jnp.dot(final, weight, preferred_element_type=F32))
        column = (block + which) * entries + jnp.arange(entries, dtype=jnp.int32)
        wanted.append(column[None, :] == target[:, None])
        one_hot = (ids[:, None] == jnp.arange(table.shape[0])[None, :]).astype(BF16)
        chosen = jnp.dot(one_hot, (table == 1).astype(BF16), preferred_element_type=F32)
        allowed.append((chosen > 0.5) | wanted[-1])
    x, a, w = (jnp.concatenate(p, axis=1) for p in (logits, allowed, wanted))
    top = jnp.max(jnp.where(a, x, NEG), axis=1)
    total = jnp.sum(jnp.where(a, jnp.exp(x - top[:, None]), 0.0), axis=1)
    picked = jnp.sum(jnp.where(w, x, 0.0), axis=1)
    return jnp.stack([top, total, picked], axis=1).reshape(count, rows // count, 3)


def wide_combine(stats):
    top = jnp.max(stats[:, :, 0], axis=0)
    total = jnp.sum(stats[:, :, 1] * jnp.exp(stats[:, :, 0] - top[None, :]), axis=0)
    return jnp.log(total) + top - jnp.sum(stats[:, :, 2], axis=0)


def solution(mesh):
    placed = (
        P(("groups", "seq"), "vocab"),
        P(("groups", "seq"), "vocab"),
        P(("groups", "seq"), None),
        P(("groups", "seq"), None),
        P(("groups", "seq"), "vocab"),
        P("vocab"),
        P("vocab"),
        P("vocab"),
        P("vocab"),
        P("vocab", "seq"),
        P("groups", "seq"),
        P(),
        P(None, ("seq", "vocab")),
        P(None, ("seq", "vocab")),
        P(("groups", "seq")),
        P(("groups", "seq")),
    )
    return jax.shard_map(
        shards, mesh=mesh, in_specs=placed, out_specs=P(("groups", "seq", "vocab")), check_vma=False
    )
```

```python
import jax
import jax.numpy as jnp
from jax import lax
from jax.experimental import pallas as pl
from jax.experimental.pallas import tpu as pltpu
from jax.sharding import PartitionSpec as P

F32 = jnp.float32
BF16 = jnp.bfloat16
HIGHEST = lax.Precision.HIGHEST
EPS = 1e-05
LANES = 128
NEG = -1e30
INFO = 60
GAP = 32
PARAMS = 64
VMEM = pltpu.VMEM


def times_transposed(a, b):
    return lax.dot_general(a, b, (((1,), (1,)), ((), ())), preferred_element_type=F32)


def grant(mebibytes):
    return pltpu.CompilerParams(vmem_limit_bytes=mebibytes << 20)


def turn(seq):
    return seq % 2


def circles(count):
    return [[2 * s + (w + turn(s)) % 2 for s in range(count)] for w in range(2)]


def thirds(a):
    high = a.astype(BF16).astype(F32)
    middle = (a - high).astype(BF16).astype(F32)
    return high, middle, a - high - middle


def pack_kernel(
    ssm_ref, gate_ref, b_ref, c_ref, raw_ref, bias_ref, decay_ref, skip_ref, ids_ref, targets_ref,
    out_ref,
):
    count, rows, _ = out_ref.shape
    channels = ssm_ref.shape[1]
    state = b_ref.shape[1]
    heads = raw_ref.shape[1]
    edge = 2 * channels
    parts = list(thirds(jax.nn.softplus(raw_ref[...] + bias_ref[...])))
    row = lax.broadcasted_iota(jnp.int32, (rows, rows), 0)
    diagonal = row == lax.broadcasted_iota(jnp.int32, (rows, rows), 1)

    def upright(a):
        wide = jnp.broadcast_to(a.astype(F32), (rows, rows))
        return jnp.sum(jnp.where(diagonal, wide, 0.0), axis=1, keepdims=True)

    targets = upright(targets_ref[...])
    upper = jnp.floor(targets / 256.0)
    parts += [upright(ids_ref[...]), upper, targets - upper * 256.0]
    parts.append(jnp.zeros((rows, PARAMS - INFO - 3), F32))
    params = list(thirds(-jnp.exp(decay_ref[...]))) + list(thirds(skip_ref[...]))
    place = lax.broadcasted_iota(jnp.int32, (rows, heads), 0)
    table = jnp.zeros((rows, heads), F32)
    for k, part in enumerate(params):
        table = jnp.where(place == k, part, table)
    parts += [table, jnp.zeros((rows, LANES - PARAMS - heads), F32)]
    misc = jnp.concatenate(parts, axis=1).astype(BF16)
    for k in range(count):
        out_ref[k, :, 0:channels] = ssm_ref[...]
        out_ref[k, :, channels:edge] = gate_ref[...]
        out_ref[k, :, edge : edge + state] = b_ref[...]
        out_ref[k, :, edge + state : edge + 2 * state] = c_ref[...]
        out_ref[k, :, edge + 2 * state :] = misc


def pack(count, ssm, gate, b, c, raw, bias, decay, skip, ids, targets):
    rows, channels = ssm.shape
    heads = bias.shape[0]
    width = 2 * channels + 2 * b.shape[1] + LANES
    return pl.pallas_call(
        pack_kernel,
        out_shape=jax.ShapeDtypeStruct((count, rows, width), BF16),
        name="pack",
    )(
        ssm, gate, b, c, raw, bias.reshape(1, heads), decay.reshape(1, heads),
        skip.reshape(1, heads), ids.reshape(1, rows), targets.reshape(1, rows),
    )


def row_order(rows, seq_rows, half, mine):
    r64 = lax.broadcasted_iota(jnp.int32, (rows, rows), 0)
    c64 = lax.broadcasted_iota(jnp.int32, (rows, rows), 1)
    own = seq_rows // 2
    side = (r64 >= half).astype(jnp.int32)
    place = r64 - side * half
    seq = lax.shift_right_logical(place, own.bit_length() - 1)
    which = (mine + side + seq) & 1
    source = place + seq * own + which * own
    return r64, c64, source


def keep_kernel(seq_rows, residual_ref, kept_ref):
    mine = lax.axis_index("vocab") + turn(lax.axis_index("seq"))
    rows, half = residual_ref.shape[0], kept_ref.shape[0]
    _, c64, source = row_order(rows, seq_rows, half, mine)
    order = (c64 == source).astype(BF16)
    kept_ref[...] = jnp.dot(order[0:half], residual_ref[...], preferred_element_type=F32)


def keep(seq_rows, residual):
    rows, width = residual.shape

    def kernel(*refs):
        keep_kernel(seq_rows, *refs)

    return pl.pallas_call(
        kernel,
        out_shape=jax.ShapeDtypeStruct((rows // 2, width), F32),
        compiler_params=grant(2),
        name="keep",
    )(residual)


def mixer_kernel(
    seq_rows, heads, x_ref, gain_ref, weight_ref, mine_ref, theirs_ref,
):
    mine = lax.axis_index("vocab") + turn(lax.axis_index("seq"))
    rows = x_ref.shape[0]
    channels = gain_ref.shape[1]
    state = (x_ref.shape[1] - LANES - 2 * channels) // 2
    edge = 2 * channels
    half = rows // 2
    size = channels // heads
    r64, c64, source = row_order(rows, seq_rows, half, mine)
    order = (c64 == source).astype(BF16)
    causal = c64 <= source
    moved = jnp.dot(order, x_ref[...], preferred_element_type=F32)

    misc = x_ref[:, edge + 2 * state :].astype(F32)
    step = misc[:, 0:heads] + misc[:, heads : 2 * heads] + misc[:, 2 * heads : 3 * heads]
    params = pltpu.roll(misc[0:8], LANES - PARAMS, 1)
    decay = params[0:1] + params[1:2] + params[2:3]
    gains = params[3:4] + params[4:5] + params[5:6]
    rates = jnp.concatenate(thirds(step * decay[:, 0:heads]), axis=1).astype(BF16)
    sums = jnp.concatenate([(c64 <= r64).astype(BF16), causal.astype(BF16)], axis=0)
    cums = jnp.dot(sums, rates, preferred_element_type=F32)
    cums = cums[:, 0:heads] + cums[:, heads : 2 * heads] + cums[:, 2 * heads :]
    middle = cums[half - 1 : half]
    ahead = jnp.exp(cums[rows:] - middle)
    back = jnp.exp(middle - cums[0:rows]) * step
    skips = jnp.broadcast_to(gains[:, 0:heads], (8, heads))
    factors = jnp.concatenate([ahead, back, skips], axis=0)
    factors = jnp.concatenate(thirds(factors), axis=1).astype(BF16)
    head_row = lax.broadcasted_iota(jnp.int32, (3 * heads, 1), 0)
    for _ in range(2):
        head_row = jnp.where(head_row >= heads, head_row - heads, head_row)
    head_lane = lax.shift_right_logical(
        lax.broadcasted_iota(jnp.int32, (1, channels), 1), size.bit_length() - 1
    )
    spread = (head_row == head_lane).astype(BF16)
    wide = jnp.dot(factors, spread, preferred_element_type=F32)

    c = moved[:, edge + state : edge + 2 * state].astype(BF16)
    corr = times_transposed(c, x_ref[:, edge : edge + state])
    corr = jnp.where(causal, corr, 0.0)
    high = corr.astype(BF16).astype(F32)
    corr = jnp.concatenate([high, corr - high, high], axis=1).astype(BF16)
    scaled = wide[rows : 2 * rows] * x_ref[:, 0:channels].astype(F32)
    high = scaled.astype(BF16)
    low = (scaled - high.astype(F32)).astype(BF16)
    y = jnp.dot(corr, jnp.concatenate([high, high, low], axis=0), preferred_element_type=F32)
    mixed = wide[0:rows] * y + wide[2 * rows : 2 * rows + 1] * moved[:, 0:channels]
    gate = moved[:, channels:edge]
    gated = (mixed * (gate / (1.0 + jnp.exp(-gate)))).astype(BF16).astype(F32)
    unit = gated * gain_ref[...]
    high = unit.astype(BF16)
    low = (unit - high.astype(F32)).astype(BF16)
    partial = times_transposed(jnp.concatenate([high, low], axis=0), weight_ref[...])
    partial = partial[0:rows] + partial[rows:]
    total = jnp.sum(gated * gated, axis=1, keepdims=True)
    lane = lax.broadcasted_iota(jnp.int32, (rows, LANES), 1)
    info = pltpu.roll(moved[:, edge + 2 * state :], LANES + 1 - INFO, 1)
    info = jnp.where(lane == 0, total, info)
    width = partial.shape[1]
    start = mine_ref.shape[1] - LANES
    mine_ref[:, 0:width] = partial[0:half]
    mine_ref[:, start:] = info[0:half]
    theirs_ref[:, 0:width] = partial[half:]
    theirs_ref[:, start:] = info[half:]


def mixer(x, seq_rows, heads, gain, weight):
    rows = x.shape[0]
    channels = gain.shape[1]
    width = weight.shape[1]
    total = (width + LANES - 1) // LANES * LANES + LANES
    half = rows // 2
    sums = jax.ShapeDtypeStruct((half, total), F32)
    whole = pl.BlockSpec(memory_space=VMEM)

    def kernel(*refs):
        mixer_kernel(seq_rows, heads, *refs)

    return pl.pallas_call(
        kernel,
        out_shape=(sums, sums),
        in_specs=[whole] * 3,
        compiler_params=grant(8),
        name="mixer",
    )(x, gain, weight.T)


def hidden_kernel(features, mine_ref, theirs_ref, kept_ref, out_ref):
    count, half, _ = out_ref.shape
    width = kept_ref.shape[1]
    start = mine_ref.shape[1] - LANES
    squares = mine_ref[:, start : start + 1] + theirs_ref[:, start : start + 1]
    scale = lax.rsqrt(squares / features + EPS)
    sums = mine_ref[:, 0:width] + theirs_ref[:, 0:width]
    hidden = (kept_ref[...] + sums * scale).astype(BF16).astype(F32)
    paired = jnp.concatenate([hidden[0:half], hidden[half:]], axis=1).astype(BF16)
    for k in range(count):
        out_ref[k] = paired


def hidden_rows(count, features, mine, theirs, kept):
    def kernel(*refs):
        hidden_kernel(features, *refs)

    return pl.pallas_call(
        kernel,
        out_shape=jax.ShapeDtypeStruct((count, kept.shape[0] // 2, 2 * kept.shape[1]), BF16),
        compiler_params=grant(4),
        name="hidden",
    )(mine, theirs, kept)


def head_kernel(
    h_ref, gain_ref, own_ref, upper_ref, lower_ref, own_mask_ref, other_mask_ref, info_ref, out_ref
):
    core = lax.axis_index("vocab")
    block = lax.axis_index("seq") * 2
    count, half, width = h_ref.shape
    rows, width = 2 * half, width // 2
    features = count * width
    squares = jnp.zeros((rows, width), F32)
    parts = []
    for k in range(count):
        pair = h_ref[k].astype(F32)
        part = jnp.concatenate([pair[:, 0:width], pair[:, width:]], axis=0)
        parts.append(part)
        squares = squares + part * part
    scale = lax.rsqrt(jnp.sum(squares, axis=1, keepdims=True) / features + EPS)
    entries = own_ref.shape[0]
    parts = [parts[k] * scale * gain_ref[k : k + 1, :] for k in range(count)]
    final = jnp.concatenate(parts, axis=1).astype(BF16)
    logits = [times_transposed(final, own_ref[...])]
    depth = features // 2
    logits.append(
        times_transposed(final[:, :depth], upper_ref[...])
        + times_transposed(final[:, depth:], lower_ref[...])
    )
    states = own_mask_ref.shape[0]
    start = info_ref.shape[1] - LANES
    ids = info_ref[:, start + 1 : start + 2].astype(jnp.int32)
    upper = info_ref[:, start + 2 : start + 3].astype(jnp.int32)
    target = upper * 256 + info_ref[:, start + 3 : start + 4].astype(jnp.int32)
    pick_row = (lax.broadcasted_iota(jnp.int32, (rows, states), 1) == ids).astype(BF16)
    column = lax.broadcasted_iota(jnp.int32, (rows, entries), 1)
    allowed, wanted = [], []
    for ref, which in ((own_mask_ref, core), (other_mask_ref, 1 - core)):
        chosen = jnp.dot(pick_row, ref[...], preferred_element_type=F32)
        is_target = column + (block + which) * entries == target
        wanted.append(is_target)
        allowed.append((chosen > 0.5) | is_target)
    tops = [
        jnp.max(jnp.where(a, x, NEG), axis=1, keepdims=True) for a, x in zip(allowed, logits)
    ]
    top = jnp.maximum(tops[0], tops[1])
    total = jnp.zeros((rows, 1), F32)
    picked = jnp.zeros((rows, 1), F32)
    for a, w, x in zip(allowed, wanted, logits):
        total = total + jnp.sum(jnp.where(a, jnp.exp(x - top), 0.0), axis=1, keepdims=True)
        picked = picked + jnp.sum(jnp.where(w, x, 0.0), axis=1, keepdims=True)
    own = rows // count
    lane = lax.broadcasted_iota(jnp.int32, (rows, LANES), 1)
    place = lane - (lax.broadcasted_iota(jnp.int32, (rows, LANES), 0) & (own - 1))
    stats = jnp.where(
        place == 0, top, jnp.where(place == GAP, total, jnp.where(place == 2 * GAP, picked, 0.0))
    )
    for k in range(count):
        out_ref[k] = jnp.sum(stats[k * own : (k + 1) * own], axis=0, keepdims=True)


def head(h, gain, own, other, own_mask, other_mask, info):
    count, half, width = h.shape
    whole = pl.BlockSpec(memory_space=VMEM)
    return pl.pallas_call(
        head_kernel,
        out_shape=jax.ShapeDtypeStruct((count, 1, LANES), F32),
        in_specs=[whole] * 8,
        compiler_params=grant(12),
        name="head",
    )(h, gain, own.T, *(o.T for o in other), own_mask, other_mask, info)


def combine_kernel(stats_ref, out_ref):
    tops = stats_ref[:, 0, :]
    totals = pltpu.roll(tops, LANES - GAP, 1)
    picked = pltpu.roll(tops, LANES - 2 * GAP, 1)
    top = jnp.max(tops, axis=0, keepdims=True)
    total = jnp.sum(totals * jnp.exp(tops - top), axis=0, keepdims=True)
    losses = jnp.log(total) + top - jnp.sum(picked, axis=0, keepdims=True)
    out_ref[...] = losses[:, 0 : out_ref.shape[1]]


def combine(own, stats):
    out = pl.pallas_call(
        combine_kernel,
        out_shape=jax.ShapeDtypeStruct((1, own), F32),
        compiler_params=grant(2),
        name="combine",
    )(stats)
    return out.reshape(own)


def wide_pack(count, ssm, gate, b, c, raw, bias, decay, skip, ids, targets):
    rows = ssm.shape[0]
    heads = raw.shape[1]

    def split(a):
        high = lax.reduce_precision(a, 8, 7)
        middle = lax.reduce_precision(a - high, 8, 7)
        return [high, middle, a - high - middle]

    parts = split(jax.nn.softplus(raw + bias[None, :]))
    parts += [a.astype(F32)[:, None] for a in (ids, targets // 256, targets % 256)]
    parts.append(jnp.zeros((rows, PARAMS - INFO - 3), F32))
    params = jnp.stack(split(-jnp.exp(decay)) + split(skip))
    parts.append(jnp.pad(params, ((0, rows - 6), (0, LANES - PARAMS - heads))))
    misc = jnp.concatenate(parts, axis=1).astype(BF16)
    row = jnp.concatenate([ssm, gate, b, c, misc], axis=1)
    return jnp.broadcast_to(row[None], (count,) + row.shape)


def wide_mixer(x, seq_rows, heads, gain, weight, residual):
    rows = x.shape[0]
    channels = gain.shape[1]
    state = (x.shape[1] - LANES - 2 * channels) // 2
    edge = 2 * channels
    core = lax.axis_index("vocab")
    misc = x[:, edge + 2 * state :].astype(F32)
    step = misc[:, 0:heads] + misc[:, heads : 2 * heads] + misc[:, 2 * heads : 3 * heads]
    params = misc[0:8, PARAMS : PARAMS + heads]
    decay = params[0] + params[1] + params[2]
    skip = params[3] + params[4] + params[5]
    log_cum = jnp.cumsum(step * decay[None, :], axis=0)
    corr = jnp.dot(
        x[:, edge + state : edge + 2 * state],
        x[:, edge : edge + state].T,
        preferred_element_type=F32,
    )
    values = x[:, 0:channels].astype(F32).reshape(rows, heads, -1).transpose(1, 0, 2)
    causal = jnp.arange(rows)[:, None] >= jnp.arange(rows)[None, :]

    def one(inputs):
        cum, size, v = inputs
        weights = jnp.exp(jnp.where(causal, cum[:, None] - cum[None, :], NEG))
        return jnp.dot(weights * corr * size[None, :], v, precision=HIGHEST)

    y = lax.map(one, (log_cum.T, step.T, values))
    mixed = (y + skip[:, None, None] * values).transpose(1, 0, 2).reshape(rows, channels)
    gated = (mixed * jax.nn.silu(x[:, channels:edge].astype(F32))).astype(BF16)
    wide = gated.astype(F32)
    squares = jnp.sum(wide * wide, axis=1, keepdims=True)
    unit = wide * gain
    high = lax.reduce_precision(unit, 8, 7)
    partial = jnp.dot(high.astype(BF16), weight, preferred_element_type=F32)
    low = (unit - high).astype(BF16)
    partial = partial + jnp.dot(low, weight, preferred_element_type=F32)
    width = weight.shape[1]
    start = (width + LANES - 1) // LANES * LANES
    info = jnp.concatenate([squares, misc[:, INFO : INFO + 3]], axis=1)
    sums = jnp.concatenate(
        [
            partial,
            jnp.zeros((rows, start - width), F32),
            info,
            jnp.zeros((rows, LANES - info.shape[1]), F32),
        ],
        axis=1,
    )

    def side(a, which):
        split = a.reshape(rows // seq_rows, 2, seq_rows // 2, -1)
        return lax.dynamic_index_in_dim(split, which, 1, False).reshape(rows // 2, -1)

    return side(sums, core), side(sums, 1 - core), side(residual.astype(F32), core)


def shards(
    ssm_input,
    gate_input,
    b_proj,
    readout_matrix,
    step_raw,
    step_bias,
    decay_log,
    head_skip_gain,
    norm_gain,
    out_weight,
    residual,
    final_gain,
    head_weight,
    mask_table,
    state_ids,
    targets,
):
    count = lax.axis_size("seq")
    rows, channels = ssm_input.shape
    features = 2 * channels
    small = count * rows <= LANES // 2
    swap = [(0, 1), (1, 0)]
    both = ("seq", "vocab")

    def exchange(a):
        if small:
            groups = circles(count)
            return lax.all_to_all(a, both, 0, 0, tiled=True, axis_index_groups=groups)
        return lax.all_to_all(a, "seq", 0, 0, tiled=True)

    packed = (pack if small else wide_pack)(
        count, ssm_input, gate_input, b_proj, readout_matrix, step_raw, step_bias, decay_log,
        head_skip_gain, state_ids, targets,
    )
    if small:
        depth = features // 2
        other_weight = tuple(
            lax.ppermute(head_weight[k * depth : (k + 1) * depth], "vocab", swap) for k in range(2)
        )
    else:
        other_weight = lax.ppermute(head_weight, "vocab", swap)
    mask_table = (mask_table == 1).astype(BF16)
    other_mask = lax.ppermute(mask_table, "vocab", swap)
    gathered = lax.all_to_all(packed, "seq", 0, 0, tiled=True)
    final_gain = final_gain.reshape(count, features // count)
    norm_gain = norm_gain.reshape(1, channels)
    if small:
        kept = keep(rows, residual)
        gathered, other_weight, mask_table, other_mask, final_gain, kept = lax.optimization_barrier(
            (gathered, other_weight, mask_table, other_mask, final_gain, kept)
        )
    x = gathered.reshape(count * rows, packed.shape[2])
    heads = step_bias.shape[0]
    if small:
        mine, theirs = mixer(x, rows, heads, norm_gain, out_weight)
    else:
        mine, theirs, kept = wide_mixer(x, rows, heads, norm_gain, out_weight, residual)
    arrived = lax.ppermute(theirs, "vocab", swap)
    if small:
        spread = hidden_rows(count, features, mine, arrived, kept)
    else:
        width = kept.shape[1]
        start = mine.shape[1] - LANES
        sums = mine + arrived
        scale = lax.rsqrt(sums[:, start : start + 1] / features + EPS)
        hidden = (kept + sums[:, 0:width] * scale).astype(BF16)
        spread = jnp.broadcast_to(hidden[None], (count,) + hidden.shape)
    full = exchange(spread)
    if small:
        stats = head(full, final_gain, head_weight, other_weight, mask_table, other_mask, mine)
    else:
        stats = wide_head(
            full, final_gain, head_weight, other_weight, mask_table, other_mask, mine
        )
    placed = exchange(stats)
    return combine(rows // 2, placed) if small else wide_combine(placed)


def wide_head(full, gain, own, other, own_mask, other_mask, info):
    count, rows, width = full.shape
    core = lax.axis_index("vocab")
    block = lax.axis_index("seq") * 2
    wide = full.transpose(1, 0, 2).reshape(rows, count * width).astype(F32)
    scale = lax.rsqrt(jnp.mean(wide * wide, axis=1, keepdims=True) + EPS)
    final = (wide * scale * gain.reshape(1, -1)).astype(BF16)
    start = info.shape[1] - LANES
    ids, upper, under = (info[:, start + k].astype(jnp.int32) for k in (1, 2, 3))
    target = upper * 256 + under
    entries = own.shape[1]
    logits, allowed, wanted = [], [], []
    for weight, table, which in ((own, own_mask, core), (other, other_mask, 1 - core)):
        logits.append(jnp.dot(final, weight, preferred_element_type=F32))
        column = (block + which) * entries + jnp.arange(entries, dtype=jnp.int32)
        wanted.append(column[None, :] == target[:, None])
        one_hot = (ids[:, None] == jnp.arange(table.shape[0])[None, :]).astype(BF16)
        chosen = jnp.dot(one_hot, (table == 1).astype(BF16), preferred_element_type=F32)
        allowed.append((chosen > 0.5) | wanted[-1])
    x, a, w = (jnp.concatenate(p, axis=1) for p in (logits, allowed, wanted))
    top = jnp.max(jnp.where(a, x, NEG), axis=1)
    total = jnp.sum(jnp.where(a, jnp.exp(x - top[:, None]), 0.0), axis=1)
    picked = jnp.sum(jnp.where(w, x, 0.0), axis=1)
    return jnp.stack([top, total, picked], axis=1).reshape(count, rows // count, 3)


def wide_combine(stats):
    top = jnp.max(stats[:, :, 0], axis=0)
    total = jnp.sum(stats[:, :, 1] * jnp.exp(stats[:, :, 0] - top[None, :]), axis=0)
    return jnp.log(total) + top - jnp.sum(stats[:, :, 2], axis=0)


def solution(mesh):
    placed = (
        P(("groups", "seq"), "vocab"),
        P(("groups", "seq"), "vocab"),
        P(("groups", "seq"), None),
        P(("groups", "seq"), None),
        P(("groups", "seq"), "vocab"),
        P("vocab"),
        P("vocab"),
        P("vocab"),
        P("vocab"),
        P("vocab", "seq"),
        P("groups", "seq"),
        P(),
        P(None, ("seq", "vocab")),
        P(None, ("seq", "vocab")),
        P(("groups", "seq")),
        P(("groups", "seq")),
    )
    return jax.shard_map(
        shards, mesh=mesh, in_specs=placed, out_specs=P(("groups", "seq", "vocab")), check_vma=False
    )
```
